32 devices in a mesh: head: 2 (over x), blk: 16 (over z, y, core).
Axes of the slice: x: 2, y: 2, z: 4, core: 2. Of those that a mesh axis runs over, the one named last changes fastest.
Arguments:
- hidden_states: bfloat16 [16384, 768], P(('head', 'blk')), may hold values from -6 to 6
- owner_rows: int32 [16384], P(('head', 'blk')), may hold values from 0 to 16383, as said below
- lengths: int32 [4], replicated, may hold values from 1005 to 8534, as said below
- attention_weight: bfloat16 [768, 2304], P(('head', 'blk')), may hold values from -0.21875 to 0.21875
- output_weight: bfloat16 [768, 768], P(('head', 'blk')), may hold values from -1.25 to 1.25
- upward_weight: bfloat16 [768, 3072], P(('head', 'blk')), may hold values from -0.21875 to 0.21875
- downward_weight: bfloat16 [3072, 768], P(('head', 'blk')), may hold values from -0.109375 to 0.109375
- query_bias: bfloat16 [768], P(('head', 'blk')), may hold values from -3 to 3
- value_bias: bfloat16 [768], P(('head', 'blk')), may hold values from -3 to 3
- output_bias: bfloat16 [768], P(('head', 'blk')), may hold values from -3 to 3
- upward_bias: bfloat16 [3072], P(('head', 'blk')), may hold values from -3 to 3
- downward_bias: bfloat16 [768], P(('head', 'blk')), may hold values from -3 to 3
- first_gain: bfloat16 [768], P(('head', 'blk')), may hold values from 0.5 to 1.5
- first_shift: bfloat16 [768], P(('head', 'blk')), may hold values from -3 to 3
- second_gain: bfloat16 [768], P(('head', 'blk')), may hold values from 0.5 to 1.5
- second_shift: bfloat16 [768], P(('head', 'blk')), may hold values from -3 to 3
- output_cotangent: bfloat16 [16384, 768], P(('head', 'blk')), may hold values from -6 to 6
Outputs:
- layer_output: bfloat16 [16384, 768], P(('head', 'blk'))
- grad_hidden: float32 [16384, 768], P(('head', 'blk'))
- grad_attention_weight: float32 [768, 2304], P(('head', 'blk'))
- grad_output_weight: float32 [768, 768], P(('head', 'blk'))
- grad_upward_weight: float32 [768, 3072], P(('head', 'blk'))
- grad_downward_weight: float32 [3072, 768], P(('head', 'blk'))
- grad_query_bias: float32 [768], P(('head', 'blk'))
- grad_value_bias: float32 [768], P(('head', 'blk'))
- grad_output_bias: float32 [768], P(('head', 'blk'))
- grad_upward_bias: float32 [3072], P(('head', 'blk'))
- grad_downward_bias: float32 [768], P(('head', 'blk'))
- grad_first_gain: float32 [768], P(('head', 'blk'))
- grad_first_shift: float32 [768], P(('head', 'blk'))
- grad_second_gain: float32 [768], P(('head', 'blk'))
- grad_second_shift: float32 [768], P(('head', 'blk'))
The draws below stay inside these ranges and needn't reach their ends.
Inputs may be any that keep to these rules, and one draw needn't show every extreme that they name: Each packed row appears once. For every i, owner_rows[i] // 512 = (i // 512 % 16) * 2 + i // 512 // 16. `lengths`: the segments of all sequences, laid out as in the reference program, fill exactly 16384 rows.
All inputs are finite; a program needn't handle non-finite values.
Results may differ from the reference program's by a relative error of at most 0.013.
The reference program's roundings to bfloat16 on the way count: a program that leaves them out, or rounds other values in their place, can miss the bound.
Values may be sent and summed in bfloat16 or wider, within the bound.
No kernel may reach another device: no remote copies, remote signals or barrier semaphores. Data moves between devices by JAX's collectives and lax.ppermute only.
A program may use at most 192 MiB of HBM per device.

```python
import jax
import jax.numpy as jnp
import numpy as np
from jax import lax

D = 768
DH = 64
FF = 3072
SEG_TOK = 502
MEMR = 10
MIN_FULL = 2
MAX_FULL = 16
QBLOCK = 512
ROWS_DEV = 512
HEAD_GROUPS = 2
BLK_GROUPS = 16
SEG_ROWS = 522
ROWS = 16384
NSEQ = 4


def draw_lengths(key, part):
    key_tail, key_share, key_order = jax.random.split(key, 3)
    last_tokens = jax.random.randint(key_tail, (NSEQ,), 1, SEG_TOK + 1, dtype=jnp.int32)
    last_tokens = last_tokens.at[2].set(SEG_TOK).at[3].set(1)
    rows_left = ROWS - jnp.sum(last_tokens[2:], dtype=jnp.int32) - 2 * MEMR * NSEQ
    residue = rows_left % SEG_ROWS
    paired = jnp.where(residue < 2, residue + SEG_ROWS, residue)
    first_last = (paired + 1) // 2
    last_tokens = last_tokens.at[0].set(first_last).at[1].set(paired - first_last)
    full_total = (rows_left - paired) // SEG_ROWS
    spare_fulls = full_total - MAX_FULL - MIN_FULL * (NSEQ - 1)
    room_each = MAX_FULL - MIN_FULL
    shuffled = jax.random.permutation(key_share, (NSEQ - 2) * room_each)
    chosen = (shuffled < spare_fulls).astype(jnp.int32).reshape(NSEQ - 2, room_each)
    extra_fulls = jnp.sum(chosen, axis=1, dtype=jnp.int32)
    others = np.concatenate([np.arange(2), np.arange(4, NSEQ)]).astype(np.int32)
    full_counts = jnp.full((NSEQ,), MIN_FULL, jnp.int32).at[others].add(extra_fulls).at[2].set(MAX_FULL)
    lengths = full_counts * SEG_TOK + last_tokens
    return lengths[jax.random.permutation(key_order, NSEQ)].astype(jnp.int32)


def draw_owner_rows(key, part):
    block_total = HEAD_GROUPS * BLK_GROUPS
    scores = jax.random.randint(key, (block_total, ROWS_DEV), 0, 1 << 18, dtype=jnp.int32) * ROWS_DEV + jnp.arange(ROWS_DEV, dtype=jnp.int32)[None, :]
    within = jnp.argsort(scores, axis=1, stable=True).astype(jnp.int32)
    device = jnp.arange(block_total, dtype=jnp.int32)
    packed = device % BLK_GROUPS * HEAD_GROUPS + device // BLK_GROUPS
    return (packed[:, None] * ROWS_DEV + within).reshape(block_total * ROWS_DEV)


def raised(array, stream_key, source, target, shards_of, factor):
    def block_of(position):
        return (jnp.arange(array.shape[position]) // (array.shape[position] // shards_of)).reshape((-1,) + (1,) * (array.ndim - 1 - position))

    one_side = jax.random.permutation(stream_key, shards_of)[block_of(target)]
    second = (block_of(target) + shards_of // 2) % shards_of
    return jnp.where((block_of(source) == one_side) | (block_of(source) == second), factor * array, array)


def levels(stream_key, shape, cuts, least, largest):
    factor_of = 1.0
    for position, parts in cuts:
        heights = jax.random.uniform(jax.random.fold_in(jax.random.fold_in(stream_key, 6), position), (parts,), jnp.float32, least / len(cuts), largest / len(cuts))
        factor_of = factor_of * jnp.repeat(jnp.exp(heights), shape[position] // parts).reshape((-1,) + (1,) * (len(shape) - 1 - position))
    return factor_of


def gaussian(own_key, shape, scale, most, cuts=(), kind=jnp.bfloat16):
    array = jax.random.normal(own_key, shape, jnp.float32) * scale
    if len(cuts) > 0:
        array = levels(own_key, shape, cuts, -0.22, 0.18) * array
    return jnp.clip(array, min=-most, max=most).astype(kind)


def gaussian_with(stream_key, extent, scale, most, cuts, heavy, held_as=jnp.bfloat16):
    drawn = scale * jax.random.normal(stream_key, extent, jnp.float32)
    if cuts:
        drawn = drawn * levels(stream_key, extent, cuts, -0.22, 0.18)
    return jnp.clip(raised(drawn, jax.random.fold_in(stream_key, 3), *heavy), -most, most).astype(held_as)


def setup_inputs(seed: int = 0) -> dict:
    streams_of = jax.random.split(jax.random.key(seed), 18)
    hidden_states = gaussian_with(streams_of[0], (ROWS, D), 1.0, 6.0, ((0, 32),), (0, 1, 32, 2.75))
    owner_rows = draw_owner_rows(jax.random.fold_in(streams_of[17], 71), 0)
    lengths = draw_lengths(jax.random.fold_in(streams_of[17], 71), 0)
    attention_weight = gaussian(streams_of[3], (D, 3 * D), D ** -0.5, 0.21875, ((0, 32),))
    output_weight = gaussian(streams_of[4], (D, D), (D // 32) ** -0.5, 1.25, ((0, 32),))
    upward_weight = gaussian(streams_of[5], (D, FF), D ** -0.5, 0.21875, ((0, 32),))
    downward_weight = gaussian(streams_of[6], (FF, D), FF ** -0.5, 0.109375, ((0, 32),))
    query_bias = gaussian(streams_of[7], (D,), 0.5, 3.0, ((0, 32),))
    value_bias = gaussian(streams_of[8], (D,), 0.5, 3.0, ((0, 32),))
    output_bias = gaussian(streams_of[9], (D,), 0.5, 3.0, ((0, 32),))
    upward_bias = gaussian(streams_of[10], (FF,), 0.5, 3.0, ((0, 32),))
    downward_bias = gaussian(streams_of[11], (D,), 0.5, 3.0, ((0, 32),))
    first_gain = jnp.clip(1.0 + 0.1 * jax.random.normal(streams_of[12], (D,), jnp.float32), 0.5, 1.5).astype(jnp.bfloat16)
    first_shift = gaussian(streams_of[13], (D,), 0.5, 3.0, ((0, 32),))
    second_gain = jnp.clip(1.0 + 0.1 * jax.random.normal(streams_of[14], (D,), jnp.float32), 0.5, 1.5).astype(jnp.bfloat16)
    second_shift = gaussian(streams_of[15], (D,), 0.5, 3.0, ((0, 32),))
    output_cotangent = gaussian(streams_of[16], (ROWS, D), 1.0, 6.0, ((0, 32),))
    return dict(hidden_states=hidden_states, owner_rows=owner_rows, lengths=lengths, attention_weight=attention_weight, output_weight=output_weight, upward_weight=upward_weight, downward_weight=downward_weight, query_bias=query_bias, value_bias=value_bias, output_bias=output_bias, upward_bias=upward_bias, downward_bias=downward_bias, first_gain=first_gain, first_shift=first_shift, second_gain=second_gain, second_shift=second_shift, output_cotangent=output_cotangent)


norm_eps = 1e-12
masked_score = -1e+30
score_scale = 0.125

@jax.custom_vjp
def low(v):
    return lax.optimization_barrier(v.astype(jnp.bfloat16)).astype(jnp.float32)

@jax.custom_vjp
def low_back(v):
    return v

def low_keep(v):
    return (low(v), None)

def low_pass(kept, grad):
    return (grad,)

def back_keep(v):
    return (v, None)

def back_low(kept, grad):
    return (low(grad),)
low.defvjp(low_keep, low_pass)
low_back.defvjp(back_keep, back_low)

def segment_ids(positions, lengths):
    segment_count = (lengths + SEG_TOK - 1) // SEG_TOK
    sequence_rows = lengths + 2 * MEMR * segment_count
    row_ends = jnp.cumsum(sequence_rows, dtype=jnp.int32)
    row_starts = row_ends - sequence_rows
    inside = ((positions[:, None] >= row_starts[None, :]) & (positions[:, None] < row_ends[None, :])).astype(jnp.int32)
    sequence_index = lax.optimization_barrier(jnp.sum(inside * jnp.arange(lengths.shape[0], dtype=jnp.int32)[None, :], axis=1, dtype=jnp.int32))
    sequence_first = lax.optimization_barrier(jnp.sum(inside * row_starts[None, :], axis=1, dtype=jnp.int32))
    found_rows = lax.optimization_barrier(jnp.sum(inside, axis=1, dtype=jnp.int32))
    within = (positions - sequence_first) // (SEG_TOK + 2 * MEMR)
    return jnp.where(found_rows > 0, sequence_index * (MAX_FULL + 2) + within, -1).astype(jnp.int32)

def normalize_rows(summed):
    row_mean = lax.optimization_barrier(jnp.mean(summed, axis=-1, keepdims=True))
    centered = summed - row_mean
    variance = lax.optimization_barrier(jnp.mean(centered * centered, axis=-1, keepdims=True))
    return centered * lax.rsqrt(variance + norm_eps)

def product(left, right):
    return jnp.dot(left, right, precision=lax.Precision.HIGHEST, preferred_element_type=jnp.float32)

def attention(queries, keys, values, segments_all):
    row_count = queries.shape[0]
    margin = SEG_TOK + 2 * MEMR - 1
    key_span = QBLOCK + 2 * margin
    head_count = queries.shape[1] // DH
    padded_keys = jnp.pad(keys, ((margin, margin), (0, 0)))
    padded_values = jnp.pad(values, ((margin, margin), (0, 0)))
    padded_segments = jnp.pad(segments_all, (margin, margin), constant_values=-1)

    def attend_block(block_index):
        block_start = block_index * QBLOCK
        query_part = lax.dynamic_slice_in_dim(queries, block_start, QBLOCK, 0).reshape(QBLOCK, head_count, DH)
        key_part = lax.dynamic_slice_in_dim(padded_keys, block_start, key_span, 0).reshape(key_span, head_count, DH)
        value_part = lax.dynamic_slice_in_dim(padded_values, block_start, key_span, 0).reshape(key_span, head_count, DH)
        allowed = lax.dynamic_slice_in_dim(segments_all, block_start, QBLOCK, 0)[:, None] == lax.dynamic_slice_in_dim(padded_segments, block_start, key_span, 0)[None, :]
        scores = jnp.einsum('qhd,khd->hqk', query_part, key_part, precision=lax.Precision.HIGHEST, preferred_element_type=jnp.float32) * score_scale
        scores = low_back(scores)
        scores = jnp.where(allowed[None], scores, masked_score)
        row_max = lax.optimization_barrier(jnp.max(scores, axis=2, keepdims=True))
        exp_scores = jnp.exp(scores - row_max)
        probabilities = exp_scores / lax.optimization_barrier(jnp.sum(exp_scores, axis=2, keepdims=True))
        attn_mix = jnp.einsum('hqk,khd->qhd', low(probabilities), value_part, precision=lax.Precision.HIGHEST, preferred_element_type=jnp.float32)
        return attn_mix.reshape(QBLOCK, head_count * DH)
    block_ids = jnp.arange(row_count // QBLOCK, dtype=jnp.int32)
    return lax.map(jax.checkpoint(attend_block), block_ids).reshape(row_count, head_count * DH)

def layer(states, segments_all, attention_weight, output_weight, upward_weight, downward_weight, query_bias, value_bias, output_bias, upward_bias, downward_bias, first_gain, first_shift, second_gain, second_shift):
    row_count, model_width = states.shape
    piece_count = row_count // QBLOCK
    bias_joint = jnp.concatenate([query_bias, jnp.zeros_like(query_bias), value_bias])

    def project(state_rows):
        return low_back(low(product(state_rows, attention_weight) + bias_joint))
    joint = lax.map(jax.checkpoint(project), states.reshape(piece_count, QBLOCK, model_width)).reshape(row_count, 3 * model_width)
    queries = joint[:, :model_width]
    keys = joint[:, model_width:2 * model_width]
    values = joint[:, 2 * model_width:]
    attn_mix = attention(queries, keys, values, segments_all)

    def finish(row_pair):
        mix_rows, state_rows = row_pair
        attended = low_back(low(mix_rows))
        branch = low_back(product(attended, output_weight) + output_bias)
        first_norm = normalize_rows(state_rows + branch) * first_gain + first_shift
        lifted = low_back(product(low(first_norm), upward_weight) + upward_bias)
        activated = low(jax.nn.gelu(lifted, approximate=False))
        branch_two = low_back(product(activated, downward_weight) + downward_bias)
        return normalize_rows(first_norm + branch_two) * second_gain + second_shift
    result = lax.map(jax.checkpoint(finish), (attn_mix.reshape(piece_count, QBLOCK, model_width), states.reshape(piece_count, QBLOCK, model_width)))
    return result.reshape(row_count, model_width)

def reference(hidden_states, owner_rows, lengths, attention_weight, output_weight, upward_weight, downward_weight, query_bias, value_bias, output_bias, upward_bias, downward_bias, first_gain, first_shift, second_gain, second_shift, output_cotangent):
    row_count = hidden_states.shape[0]
    states = jnp.zeros(hidden_states.shape, jnp.float32).at[owner_rows].set(hidden_states.astype(jnp.float32))
    cotangent = jnp.zeros(hidden_states.shape, jnp.float32).at[owner_rows].set(output_cotangent.astype(jnp.float32))
    segments_all = segment_ids(jnp.arange(row_count, dtype=jnp.int32), lengths)
    parameters = tuple((element.astype(jnp.float32) for element in (attention_weight, output_weight, upward_weight, downward_weight, query_bias, value_bias, output_bias, upward_bias, downward_bias, first_gain, first_shift, second_gain, second_shift)))

    def forward(state_rows, *weights_all):
        return layer(state_rows, segments_all, *weights_all)
    result, pullback = jax.vjp(forward, states, *parameters)
    gradients = pullback(cotangent)
    layer_output = result.astype(jnp.bfloat16)[owner_rows]
    grad_hidden = gradients[0][owner_rows]
    return (layer_output, grad_hidden, gradients[1], gradients[2], gradients[3], gradients[4], gradients[5], gradients[6], gradients[7], gradients[8], gradients[9], gradients[10], gradients[11], gradients[12], gradients[13])
```

```python
import functools

import jax
import jax.numpy as jnp
import numpy as np
from jax import lax
from jax.experimental import pallas as pl
from jax.experimental.pallas import tpu as pltpu
from jax.sharding import PartitionSpec as P

DH = 64
SEG_TOK = 502
MEMR = 10
SEG_ROWS = SEG_TOK + 2 * MEMR
AXES = ("head", "blk")
TILE = 128
PAIR = 2 * DH
WINDOW = 544

norm_eps = 1e-12
masked_score = -1e30
score_scale = 0.125
root_half = 0.7071067811865476
inverse_root_two_pi = 0.3989422804014327
f32 = jnp.float32
bf16 = jnp.bfloat16


def swap(block, bit, count):
    return lax.ppermute(block, AXES, [(i, i ^ bit) for i in range(count)])


def gathered(shard, order, count, me):
    held, have = shard, []
    for bit in order:
        axis = sum(b > bit for b in have)
        have.append(bit)
        other = jnp.expand_dims(swap(held, bit, count), axis)
        own = jnp.expand_dims(held, axis)
        held = jnp.where(
            (me & bit) == 0,
            jnp.concatenate([own, other], axis=axis),
            jnp.concatenate([other, own], axis=axis),
        )
    return held.reshape((count * shard.shape[0],) + shard.shape[1:])


def reduced(blocks, order, count, me):
    have = sorted(order, reverse=True)
    held = blocks.reshape((2,) * len(have) + blocks.shape[1:])
    for step, bit in enumerate(order):
        axis = have.index(bit)
        have.remove(bit)
        mine = ((me & bit) != 0).astype(jnp.int32)
        keep = lax.dynamic_index_in_dim(held, mine, axis, keepdims=False)
        send = lax.dynamic_index_in_dim(held, 1 - mine, axis, keepdims=False)
        total = keep.astype(f32) + swap(send, bit, count).astype(f32)
        held = total if not have else total.astype(blocks.dtype)
    return held


def segment_at(lengths_ref, sequences, position):
    start = jnp.int32(0)
    low = jnp.int32(0)
    high = jnp.int32(0)
    for i in range(sequences):
        tokens = lengths_ref[i]
        end = start + tokens + 2 * MEMR * lax.div(tokens + (SEG_TOK - 1), jnp.int32(SEG_TOK))
        inside = (position >= start) & (position < end)
        first = start + lax.div(position - start, jnp.int32(SEG_ROWS)) * SEG_ROWS
        low = jnp.where(inside, first, low)
        high = jnp.where(inside, jnp.minimum(first + SEG_ROWS, end), high)
        start = end
    return low, high


def over_segments(lengths_ref, sequences, first_row, rows, side, body):
    def step(position):
        low, high = segment_at(lengths_ref, sequences, position)
        high = jnp.maximum(high, position + 1)
        low_at = low - first_row + side
        high_at = high - first_row + side
        window = jnp.minimum(lax.div(low_at, jnp.int32(16)) * 16, rows + 2 * side - WINDOW)
        window = pl.multiple_of(jnp.maximum(window, 0), 16)
        tile_from = lax.div(jnp.maximum(low - first_row, 0), jnp.int32(TILE))
        tile_to = lax.div(jnp.minimum(high - first_row, rows) + TILE - 1, jnp.int32(TILE))
        body(low_at, high_at, window, tile_from, tile_to)
        return high

    lax.while_loop(lambda position: position < first_row + rows, step, first_row)


def two_heads(block):
    lane = lax.broadcasted_iota(jnp.int32, block.shape, 1)
    zero = jnp.zeros_like(block)
    return jnp.concatenate(
        [jnp.where(lane < DH, block, zero), jnp.where(lane < DH, zero, block)], axis=0
    )


def own_blocks(product):
    return jnp.concatenate([product[:DH, :TILE], product[DH:, TILE:]], axis=0).T


def key_bias(low_at, high_at, window):
    row = lax.broadcasted_iota(jnp.int32, (WINDOW, 2 * TILE), 0) + window
    return jnp.where((row >= low_at) & (row < high_at), 0.0, masked_score)


def rows_inside(tile, low_at, high_at, side, shape, dim):
    at = lax.broadcasted_iota(jnp.int32, shape, dim)
    if dim == 1:
        at = at & (TILE - 1)
    at = at + (tile * TILE + side)
    return (at >= low_at) & (at < high_at)


NT = (((1,), (1,)), ((), ()))
NN = (((1,), (0,)), ((), ()))


def mul(left, right, dims=NN):
    return lax.dot_general(left, right, dims, preferred_element_type=f32)


def forward_kernel(
    sequences, side, lengths_ref, first_ref, q_ref, k_ref, v_ref, o_ref, stat_ref, bias_ref, vt_ref
):
    rows = q_ref.shape[0]
    stat_ref[...] = jnp.zeros_like(stat_ref)
    o_ref[...] = jnp.zeros_like(o_ref)

    def segment(low_at, high_at, window, tile_from, tile_to):
        bias_ref[...] = key_bias(low_at, high_at, window)
        vt_ref[...] = v_ref[pl.ds(window, WINDOW), :].T

        def one(tile, carry):
            at = pl.ds(pl.multiple_of(tile * TILE, TILE), TILE)
            wide = pl.ds(pl.multiple_of(tile * 2 * TILE, 2 * TILE), 2 * TILE)
            queries = two_heads(q_ref[at, :])
            scores = mul(k_ref[pl.ds(window, WINDOW), :], queries, NT) + bias_ref[...]
            top = jnp.max(scores, axis=0, keepdims=True)
            raised = jnp.exp(scores - top)
            inverse = 1.0 / jnp.sum(raised, axis=0, keepdims=True)
            weights = (raised * inverse).astype(bf16)
            mixed = own_blocks(mul(vt_ref[...], weights)).astype(bf16)
            here = rows_inside(tile, low_at, high_at, side, (TILE, PAIR), 0)
            o_ref[at, :] = jnp.where(here, mixed, o_ref[at, :])
            there = rows_inside(tile, low_at, high_at, side, (1, 2 * TILE), 1)
            stat_ref[0, 0:1, wide] = jnp.where(there, top, stat_ref[0, 0:1, wide])
            stat_ref[0, 1:2, wide] = jnp.where(there, inverse, stat_ref[0, 1:2, wide])
            return carry

        lax.fori_loop(tile_from, tile_to, one, 0)

    over_segments(lengths_ref, sequences, first_ref[0], rows, side, segment)


def backward_kernel(
    sequences,
    side,
    lengths_ref,
    first_ref,
    q_ref,
    k_ref,
    v_ref,
    g_ref,
    stat_ref,
    dq_ref,
    dk_ref,
    dv_ref,
    bias_ref,
    kt_ref,
    dq_acc,
    dk_acc,
    dv_acc,
):
    rows = q_ref.shape[0]
    dq_acc[...] = jnp.zeros_like(dq_acc)
    dk_acc[...] = jnp.zeros_like(dk_acc)
    dv_acc[...] = jnp.zeros_like(dv_acc)

    def segment(low_at, high_at, window, tile_from, tile_to):
        bias_ref[...] = key_bias(low_at, high_at, window)
        keys_at = pl.ds(window, WINDOW)
        kt_ref[...] = k_ref[keys_at, :].T

        def one(tile, carry):
            at = pl.ds(pl.multiple_of(tile * TILE, TILE), TILE)
            wide = pl.ds(pl.multiple_of(tile * 2 * TILE, 2 * TILE), 2 * TILE)
            queries = two_heads(q_ref[at, :])
            grads = two_heads(g_ref[at, :])
            there = rows_inside(tile, low_at, high_at, side, (1, 2 * TILE), 1)
            top = jnp.where(there, stat_ref[0, 0:1, wide], -masked_score)
            inverse = jnp.where(there, stat_ref[0, 1:2, wide], 0.0)
            scores = mul(k_ref[keys_at, :], queries, NT) + bias_ref[...]
            probs = jnp.exp(scores - top) * inverse
            grad_probs = mul(v_ref[keys_at, :], grads, NT)
            shared = jnp.sum(probs * grad_probs, axis=0, keepdims=True)
            grad_scores = (probs * (grad_probs - shared)).astype(bf16)
            dv_acc[keys_at, :] += mul(probs.astype(bf16), grads)
            dk_acc[keys_at, :] += mul(grad_scores, queries)
            dq_acc[at, :] += own_blocks(mul(kt_ref[...], grad_scores))
            return carry

        lax.fori_loop(tile_from, tile_to, one, 0)

    over_segments(lengths_ref, sequences, first_ref[0], rows, side, segment)
    dq_ref[...] = (dq_acc[...] * score_scale).astype(bf16)
    dk_ref[...] = dk_acc[...].astype(bf16)
    dv_ref[...] = dv_acc[...].astype(bf16)


def attention_forward(lengths, first, queries, keys, values, side):
    rows, width = queries.shape
    pairs = width // PAIR
    column = lambda n: pl.BlockSpec((n, PAIR), lambda h, *_: (0, h))
    return pl.pallas_call(
        functools.partial(forward_kernel, lengths.shape[0], side),
        name="attention_forward",
        out_shape=(
            jax.ShapeDtypeStruct((rows, width), bf16),
            jax.ShapeDtypeStruct((pairs, 8, 2 * rows), f32),
        ),
        grid_spec=pltpu.PrefetchScalarGridSpec(
            num_scalar_prefetch=2,
            grid=(pairs,),
            in_specs=[column(rows), column(keys.shape[0]), column(keys.shape[0])],
            out_specs=[column(rows), pl.BlockSpec((1, 8, 2 * rows), lambda h, *_: (h, 0, 0))],
            scratch_shapes=[
                pltpu.VMEM((WINDOW, 2 * TILE), f32),
                pltpu.VMEM((PAIR, WINDOW), bf16),
            ],
        ),
        compiler_params=pltpu.CompilerParams(vmem_limit_bytes=48 * 2**20),
    )(lengths, first, queries, keys, values)


def attention_backward(lengths, first, queries, keys, values, grads, stats, side):
    rows, width = queries.shape
    wide = keys.shape[0]
    pairs = width // PAIR
    column = lambda n: pl.BlockSpec((n, PAIR), lambda h, *_: (0, h))
    return pl.pallas_call(
        functools.partial(backward_kernel, lengths.shape[0], side),
        name="attention_backward",
        out_shape=(
            jax.ShapeDtypeStruct((rows, width), bf16),
            jax.ShapeDtypeStruct((wide, width), bf16),
            jax.ShapeDtypeStruct((wide, width), bf16),
        ),
        grid_spec=pltpu.PrefetchScalarGridSpec(
            num_scalar_prefetch=2,
            grid=(pairs,),
            in_specs=[
                column(rows),
                column(wide),
                column(wide),
                column(rows),
                pl.BlockSpec((1, 8, 2 * rows), lambda h, *_: (h, 0, 0)),
            ],
            out_specs=[column(rows), column(wide), column(wide)],
            scratch_shapes=[
                pltpu.VMEM((WINDOW, 2 * TILE), f32),
                pltpu.VMEM((PAIR, WINDOW), bf16),
                pltpu.VMEM((rows, PAIR), f32),
                pltpu.VMEM((wide, PAIR), f32),
                pltpu.VMEM((wide, PAIR), f32),
            ],
        ),
        compiler_params=pltpu.CompilerParams(vmem_limit_bytes=48 * 2**20),
    )(lengths, first, queries, keys, values, grads, stats)


def normalize(summed):
    row_mean = jnp.mean(summed, axis=-1, keepdims=True)
    centered = summed - row_mean
    variance = jnp.mean(centered * centered, axis=-1, keepdims=True)
    inverse_std = lax.rsqrt(variance + norm_eps)
    return (centered * inverse_std, inverse_std)


def normalize_back(grad_normed, normed, inverse_std):
    grad_mean = jnp.mean(grad_normed, axis=-1, keepdims=True)
    cross_mean = jnp.mean(grad_normed * normed, axis=-1, keepdims=True)
    return inverse_std * (grad_normed - grad_mean - normed * cross_mean)


def local(
    hidden_states,
    owner_rows,
    lengths,
    attention_weight,
    output_weight,
    upward_weight,
    downward_weight,
    query_bias,
    value_bias,
    output_bias,
    upward_bias,
    downward_bias,
    first_gain,
    first_shift,
    second_gain,
    second_shift,
    output_cotangent,
):
    rows, width = hidden_states.shape
    heads_axis, blocks_axis = lax.axis_size("head"), lax.axis_size("blk")
    count = heads_axis * blocks_axis
    me = lax.axis_index(AXES)
    place = lax.axis_index("blk") * heads_axis + lax.axis_index("head")
    first = (place * rows).astype(jnp.int32).reshape(1)
    bits = [1 << b for b in range((count - 1).bit_length())]
    far = [b for b in bits if b not in (1, 2, blocks_axis)]
    order_a = tuple(far + [2, blocks_axis, 1])
    order_b = tuple(far + [blocks_axis, 2, 1])
    back_a = order_a[::-1]
    back_b = order_b[::-1]

    def shift(block, by):
        index_of = lambda q: q % heads_axis * blocks_axis + q // heads_axis
        pairs = [
            (index_of(q), index_of(q + by)) for q in range(count) if 0 <= q + by < count
        ]
        return lax.ppermute(block, AXES, pairs)

    slot_index = owner_rows % rows
    pick = (slot_index[None, :] == jnp.arange(rows, dtype=jnp.int32)[:, None]).astype(bf16)
    states = jnp.dot(pick, hidden_states, preferred_element_type=f32).astype(bf16)
    grad_result = jnp.dot(pick, output_cotangent, preferred_element_type=f32)

    thin = -(-max(SEG_ROWS - 1 - rows, 0) // 16) * 16
    near = min(rows, -(-(SEG_ROWS - 1) // 16) * 16)
    side = near + thin
    parts = [
        shift(states[rows - near :], 1),
        states,
        shift(states[:near], -1),
    ]
    if thin:
        parts = [shift(states[rows - thin :], 2), *parts, shift(states[:thin], -2)]
    reach = jnp.concatenate(parts, axis=0)

    half = 3 * width // 2
    weight_a = gathered(attention_weight[:, :half], order_a, count, me)
    weight_b = gathered(attention_weight[:, half:], order_b, count, me)
    triple_weight = jnp.concatenate([weight_a, weight_b], axis=1)
    small = (
        query_bias,
        value_bias,
        output_bias,
        downward_bias,
        first_gain,
        first_shift,
        second_gain,
        second_shift,
        upward_bias,
    )
    small_widths = [s.shape[0] for s in small]
    small_ends = np.cumsum(small_widths)
    packed = jnp.concatenate(small)
    packed = jnp.pad(packed, (0, -packed.shape[0] % 128))
    packed_all = gathered(packed[None], order_a, count, me).astype(f32)
    (
        bias_query,
        bias_value,
        bias_output,
        bias_downward,
        gain_one,
        shift_one,
        gain_two,
        shift_two,
        bias_upward,
    ) = [
        packed_all[:, end - n : end].reshape(count * n)
        for end, n in zip(small_ends, small_widths)
    ]
    mixer_weight = gathered(output_weight, order_a, count, me)
    upward_full = gathered(upward_weight, order_a, count, me)
    downward_full = gathered(downward_weight, order_b, count, me)

    queries = (
        (jnp.dot(states, triple_weight[:, :width], preferred_element_type=f32) + bias_query)
        .astype(bf16) * jnp.asarray(score_scale, bf16)
    )
    keys = jnp.dot(reach, triple_weight[:, width : 2 * width], preferred_element_type=f32).astype(bf16)
    values = (
        jnp.dot(reach, triple_weight[:, 2 * width :], preferred_element_type=f32) + bias_value
    ).astype(bf16)
    attended, stats = attention_forward(lengths, first, queries, keys, values, side)

    branch = jnp.dot(attended, mixer_weight, preferred_element_type=f32) + bias_output
    normed_one, scale_one = normalize(states.astype(f32) + branch)
    first_norm = normed_one * gain_one + shift_one
    inner_rows = first_norm.astype(bf16)
    lifted = jnp.dot(inner_rows, upward_full, preferred_element_type=f32) + bias_upward
    activated = jax.nn.gelu(lifted, approximate=False).astype(bf16)
    branch_two = jnp.dot(activated, downward_full, preferred_element_type=f32) + bias_downward
    normed_two, scale_two = normalize(first_norm + branch_two)
    result = normed_two * gain_two + shift_two
    layer_output = jnp.take(result.astype(bf16), slot_index, axis=0)

    grad_second_gain = jnp.sum(grad_result * normed_two, axis=0)
    grad_second_shift = jnp.sum(grad_result, axis=0)
    grad_mid = normalize_back(grad_result * gain_two, normed_two, scale_two)
    grad_down_rows = grad_mid.astype(bf16)
    grad_downward_bias = jnp.sum(grad_down_rows.astype(f32), axis=0)
    grad_downward_weight = jnp.einsum(
        "rf,rd->fd", activated, grad_down_rows, preferred_element_type=f32
    ).astype(bf16)
    grad_activated = jnp.einsum(
        "rd,fd->rf", grad_down_rows, downward_full, preferred_element_type=f32
    )
    gelu_slope = 0.5 * (1.0 + lax.erf(lifted * root_half)) + lifted * inverse_root_two_pi * jnp.exp(
        -0.5 * lifted * lifted
    )
    grad_lifted = (grad_activated * gelu_slope).astype(bf16)
    grad_upward_bias = jnp.sum(grad_lifted.astype(f32), axis=0)
    grad_upward_weight = jnp.einsum(
        "rd,rf->df", inner_rows, grad_lifted, preferred_element_type=f32
    ).astype(bf16)
    grad_first = (
        jnp.einsum("rf,df->rd", grad_lifted, upward_full, preferred_element_type=f32) + grad_mid
    )
    grad_first_gain = jnp.sum(grad_first * normed_one, axis=0)
    grad_first_shift = jnp.sum(grad_first, axis=0)
    grad_residual = normalize_back(grad_first * gain_one, normed_one, scale_one)
    grad_branch = grad_residual.astype(bf16)
    grad_output_bias = jnp.sum(grad_branch.astype(f32), axis=0)
    grad_output_weight = jnp.einsum(
        "rd,re->de", attended, grad_branch, preferred_element_type=f32
    ).astype(bf16)
    grad_attended = jnp.einsum(
        "re,de->rd", grad_branch, mixer_weight, preferred_element_type=f32
    ).astype(bf16)
    by_device = lambda grad: grad.reshape((count, grad.shape[0] // count) + grad.shape[1:])
    out_downward = reduced(by_device(grad_downward_weight), back_b, count, me)
    out_upward = reduced(by_device(grad_upward_weight), back_a, count, me)
    out_mixer = reduced(by_device(grad_output_weight), back_b, count, me)

    grad_query, grad_key, grad_value = attention_backward(
        lengths, first, queries, keys, values, grad_attended, stats, side
    )
    grad_triple = jnp.concatenate(
        [
            jnp.einsum("rd,rc->dc", states, grad_query, preferred_element_type=f32),
            jnp.einsum("rd,rc->dc", reach, grad_key, preferred_element_type=f32),
            jnp.einsum("rd,rc->dc", reach, grad_value, preferred_element_type=f32),
        ],
        axis=1,
    ).astype(bf16)
    grad_query_bias = jnp.sum(grad_query.astype(f32), axis=0)
    grad_value_bias = jnp.sum(grad_value.astype(f32), axis=0)
    grad_reach = jnp.einsum(
        "rc,dc->rd", grad_key, triple_weight[:, width : 2 * width], preferred_element_type=f32
    ) + jnp.einsum(
        "rc,dc->rd", grad_value, triple_weight[:, 2 * width :], preferred_element_type=f32
    )
    from_right = shift(grad_reach[thin : side].astype(bf16), -1).astype(f32)
    from_left = shift(grad_reach[side + rows : side + rows + near].astype(bf16), 1).astype(f32)
    grad_input = (
        grad_reach[side : side + rows]
        + jnp.einsum("rc,dc->rd", grad_query, triple_weight[:, :width], preferred_element_type=f32)
        + grad_residual
    )
    grad_input = (
        grad_input
        + jnp.pad(from_right, ((rows - near, 0), (0, 0)))
        + jnp.pad(from_left, ((0, rows - near), (0, 0)))
    )
    if thin:
        far_right = shift(grad_reach[:thin].astype(bf16), -2).astype(f32)
        far_left = shift(grad_reach[side + rows + near :].astype(bf16), 2).astype(f32)
        grad_input = (
            grad_input
            + jnp.pad(far_right, ((rows - thin, 0), (0, 0)))
            + jnp.pad(far_left, ((0, rows - thin), (0, 0)))
        )
    grad_hidden = jnp.take(grad_input, slot_index, axis=0)

    out_a = reduced(by_device(grad_triple[:, :half]), back_a, count, me)
    out_b = reduced(by_device(grad_triple[:, half:]), back_b, count, me)
    out_triple = jnp.concatenate([out_a, out_b], axis=1)
    grads_small = (
        grad_query_bias,
        grad_value_bias,
        grad_output_bias,
        grad_downward_bias,
        grad_first_gain,
        grad_first_shift,
        grad_second_gain,
        grad_second_shift,
        grad_upward_bias,
    )
    packed_grads = jnp.concatenate([by_device(g) for g in grads_small], axis=1)
    packed_grads = jnp.pad(packed_grads, ((0, 0), (0, -packed_grads.shape[1] % 128)))
    summed = reduced(packed_grads, back_a, count, me)
    (
        out_query,
        out_value,
        out_output,
        out_down_bias,
        out_gain_one,
        out_shift_one,
        out_gain_two,
        out_shift_two,
        out_up_bias,
    ) = [summed[end - n : end] for end, n in zip(small_ends, small_widths)]
    return (
        layer_output,
        grad_hidden,
        out_triple,
        out_mixer,
        out_upward,
        out_downward,
        out_query,
        out_value,
        out_output,
        out_up_bias,
        out_down_bias,
        out_gain_one,
        out_shift_one,
        out_gain_two,
        out_shift_two,
    )


def solution(mesh):
    matrix, vector = P(AXES, None), P(AXES)
    return jax.shard_map(
        local,
        mesh=mesh,
        in_specs=(matrix, vector, P(), *[matrix] * 4, *[vector] * 9, matrix),
        out_specs=(*[matrix] * 6, *[vector] * 9),
        check_vma=False,
    )
```

```python
import functools

import jax
import jax.numpy as jnp
import numpy as np
from jax import lax
from jax.experimental import pallas as pl
from jax.experimental.pallas import tpu as pltpu
from jax.sharding import PartitionSpec as P

DH = 64
SEG_TOK = 502
MEMR = 10
SEG_ROWS = SEG_TOK + 2 * MEMR
AXES = ("head", "blk")
TILE = 128
PAIR = 2 * DH
WINDOW = 544

norm_eps = 1e-12
masked_score = -1e30
score_scale = 0.125
root_half = 0.7071067811865476
inverse_root_two_pi = 0.3989422804014327
f32 = jnp.float32
bf16 = jnp.bfloat16


def swap(block, bit, count):
    return lax.ppermute(block, AXES, [(i, i ^ bit) for i in range(count)])


def after(value, *others):
    return lax.optimization_barrier((value, *others))[0]


def merge(held, have, other, bit, me):
    axis = sum(b > bit for b in have)
    other, own = jnp.expand_dims(other, axis), jnp.expand_dims(held, axis)
    return jnp.where(
        (me & bit) == 0,
        jnp.concatenate([own, other], axis=axis),
        jnp.concatenate([other, own], axis=axis),
    )


def flat(held, rows, count):
    return held.reshape((count * rows,) + held.shape[-1:])


def reduced(blocks, order, count, me):
    have = sorted(order, reverse=True)
    held = blocks.reshape((2,) * len(have) + blocks.shape[1:])
    for step, bit in enumerate(order):
        axis = have.index(bit)
        have.remove(bit)
        mine = ((me & bit) != 0).astype(jnp.int32)
        keep = lax.dynamic_index_in_dim(held, mine, axis, keepdims=False)
        send = lax.dynamic_index_in_dim(held, 1 - mine, axis, keepdims=False)
        total = keep.astype(f32) + swap(send, bit, count).astype(f32)
        held = total if not have else total.astype(blocks.dtype)
    return held


def relative(bits):
    return [sum(bit for at, bit in enumerate(bits) if j >> at & 1) for j in range(1 << len(bits))]


def halved(keep, send, order, count):
    total = keep.astype(f32)
    for bit in order:
        total = total + swap(send, bit, count).astype(f32)
        half = total.shape[0] // 2
        send, total = total[half:].astype(bf16), total[: max(half, 1)]
        send = yield send
    yield total[0]


def segment_at(lengths_ref, sequences, position):
    start = jnp.int32(0)
    low = jnp.int32(0)
    high = jnp.int32(0)
    for i in range(sequences):
        tokens = lengths_ref[i]
        end = start + tokens + 2 * MEMR * lax.div(tokens + (SEG_TOK - 1), jnp.int32(SEG_TOK))
        inside = (position >= start) & (position < end)
        first = start + lax.div(position - start, jnp.int32(SEG_ROWS)) * SEG_ROWS
        low = jnp.where(inside, first, low)
        high = jnp.where(inside, jnp.minimum(first + SEG_ROWS, end), high)
        start = end
    return low, high


def over_segments(lengths_ref, sequences, first_row, rows, side, body):
    def step(position):
        low, high = segment_at(lengths_ref, sequences, position)
        high = jnp.maximum(high, position + 1)
        low_at = low - first_row + side
        high_at = high - first_row + side
        window = jnp.minimum(lax.div(low_at, jnp.int32(16)) * 16, rows + 2 * side - WINDOW)
        window = pl.multiple_of(jnp.maximum(window, 0), 16)
        tile_from = lax.div(jnp.maximum(low - first_row, 0), jnp.int32(TILE))
        tile_to = lax.div(jnp.minimum(high - first_row, rows) + TILE - 1, jnp.int32(TILE))
        body(low_at, high_at, window, tile_from, tile_to)
        return high

    lax.while_loop(lambda position: position < first_row + rows, step, first_row)


def two_heads(block):
    lane = lax.broadcasted_iota(jnp.int32, block.shape, 1)
    zero = jnp.zeros_like(block)
    return jnp.concatenate(
        [jnp.where(lane < DH, block, zero), jnp.where(lane < DH, zero, block)], axis=0
    )


def own_blocks(product):
    return jnp.concatenate([product[:DH, :TILE], product[DH:, TILE:]], axis=0).T


def key_bias(low_at, high_at, window):
    row = lax.broadcasted_iota(jnp.int32, (WINDOW, 2 * TILE), 0) + window
    return jnp.where((row >= low_at) & (row < high_at), 0.0, masked_score)


def rows_inside(tile, low_at, high_at, side, shape, dim):
    at = lax.broadcasted_iota(jnp.int32, shape, dim)
    if dim == 1:
        at = at & (TILE - 1)
    at = at + (tile * TILE + side)
    return (at >= low_at) & (at < high_at)


NT = (((1,), (1,)), ((), ()))
NN = (((1,), (0,)), ((), ()))


def mul(left, right, dims=NN):
    return lax.dot_general(left, right, dims, preferred_element_type=f32)


def forward_kernel(
    sequences, side, lengths_ref, first_ref, q_ref, k_ref, v_ref, o_ref, stat_ref, bias_ref, vt_ref
):
    rows = q_ref.shape[0]
    stat_ref[...] = jnp.zeros_like(stat_ref)
    o_ref[...] = jnp.zeros_like(o_ref)

    def segment(low_at, high_at, window, tile_from, tile_to):
        bias_ref[...] = key_bias(low_at, high_at, window)
        vt_ref[...] = v_ref[pl.ds(window, WINDOW), :].T

        def one(tile, carry):
            at = pl.ds(pl.multiple_of(tile * TILE, TILE), TILE)
            wide = pl.ds(pl.multiple_of(tile * 2 * TILE, 2 * TILE), 2 * TILE)
            queries = two_heads(q_ref[at, :])
            scores = mul(k_ref[pl.ds(window, WINDOW), :], queries, NT) + bias_ref[...]
            top = jnp.max(scores, axis=0, keepdims=True)
            raised = jnp.exp(scores - top)
            inverse = 1.0 / jnp.sum(raised, axis=0, keepdims=True)
            weights = (raised * inverse).astype(bf16)
            mixed = own_blocks(mul(vt_ref[...], weights)).astype(bf16)
            here = rows_inside(tile, low_at, high_at, side, (TILE, PAIR), 0)
            o_ref[at, :] = jnp.where(here, mixed, o_ref[at, :])
            there = rows_inside(tile, low_at, high_at, side, (1, 2 * TILE), 1)
            stat_ref[0, 0:1, wide] = jnp.where(there, top, stat_ref[0, 0:1, wide])
            stat_ref[0, 1:2, wide] = jnp.where(there, inverse, stat_ref[0, 1:2, wide])
            return carry

        lax.fori_loop(tile_from, tile_to, one, 0)

    over_segments(lengths_ref, sequences, first_ref[0], rows, side, segment)


def backward_kernel(
    sequences,
    side,
    lengths_ref,
    first_ref,
    q_ref,
    k_ref,
    v_ref,
    g_ref,
    stat_ref,
    dq_ref,
    dk_ref,
    dv_ref,
    bias_ref,
    kt_ref,
    dq_acc,
    dk_acc,
    dv_acc,
):
    rows = q_ref.shape[0]
    dq_acc[...] = jnp.zeros_like(dq_acc)
    dk_acc[...] = jnp.zeros_like(dk_acc)
    dv_acc[...] = jnp.zeros_like(dv_acc)

    def segment(low_at, high_at, window, tile_from, tile_to):
        bias_ref[...] = key_bias(low_at, high_at, window)
        keys_at = pl.ds(window, WINDOW)
        kt_ref[...] = k_ref[keys_at, :].T

        def one(tile, carry):
            at = pl.ds(pl.multiple_of(tile * TILE, TILE), TILE)
            wide = pl.ds(pl.multiple_of(tile * 2 * TILE, 2 * TILE), 2 * TILE)
            queries = two_heads(q_ref[at, :])
            grads = two_heads(g_ref[at, :])
            there = rows_inside(tile, low_at, high_at, side, (1, 2 * TILE), 1)
            top = jnp.where(there, stat_ref[0, 0:1, wide], -masked_score)
            inverse = jnp.where(there, stat_ref[0, 1:2, wide], 0.0)
            scores = mul(k_ref[keys_at, :], queries, NT) + bias_ref[...]
            probs = jnp.exp(scores - top) * inverse
            grad_probs = mul(v_ref[keys_at, :], grads, NT)
            shared = jnp.sum(probs * grad_probs, axis=0, keepdims=True)
            grad_scores = (probs * (grad_probs - shared)).astype(bf16)
            dv_acc[keys_at, :] += mul(probs.astype(bf16), grads)
            dk_acc[keys_at, :] += mul(grad_scores, queries)
            dq_acc[at, :] += own_blocks(mul(kt_ref[...], grad_scores))
            return carry

        lax.fori_loop(tile_from, tile_to, one, 0)

    over_segments(lengths_ref, sequences, first_ref[0], rows, side, segment)
    dq_ref[...] = (dq_acc[...] * score_scale).astype(bf16)
    dk_ref[...] = dk_acc[...].astype(bf16)
    dv_ref[...] = dv_acc[...].astype(bf16)


def attention_forward(lengths, first, queries, keys, values, side):
    rows, width = queries.shape
    pairs = width // PAIR
    column = lambda n: pl.BlockSpec((n, PAIR), lambda h, *_: (0, h))
    return pl.pallas_call(
        functools.partial(forward_kernel, lengths.shape[0], side),
        name="attention_forward",
        out_shape=(
            jax.ShapeDtypeStruct((rows, width), bf16),
            jax.ShapeDtypeStruct((pairs, 8, 2 * rows), f32),
        ),
        grid_spec=pltpu.PrefetchScalarGridSpec(
            num_scalar_prefetch=2,
            grid=(pairs,),
            in_specs=[column(rows), column(keys.shape[0]), column(keys.shape[0])],
            out_specs=[column(rows), pl.BlockSpec((1, 8, 2 * rows), lambda h, *_: (h, 0, 0))],
            scratch_shapes=[
                pltpu.VMEM((WINDOW, 2 * TILE), f32),
                pltpu.VMEM((PAIR, WINDOW), bf16),
            ],
        ),
        compiler_params=pltpu.CompilerParams(vmem_limit_bytes=48 * 2**20),
    )(lengths, first, queries, keys, values)


def attention_backward(lengths, first, queries, keys, values, grads, stats, side):
    rows, width = queries.shape
    wide = keys.shape[0]
    pairs = width // PAIR
    column = lambda n: pl.BlockSpec((n, PAIR), lambda h, *_: (0, h))
    return pl.pallas_call(
        functools.partial(backward_kernel, lengths.shape[0], side),
        name="attention_backward",
        out_shape=(
            jax.ShapeDtypeStruct((rows, width), bf16),
            jax.ShapeDtypeStruct((wide, width), bf16),
            jax.ShapeDtypeStruct((wide, width), bf16),
        ),
        grid_spec=pltpu.PrefetchScalarGridSpec(
            num_scalar_prefetch=2,
            grid=(pairs,),
            in_specs=[
                column(rows),
                column(wide),
                column(wide),
                column(rows),
                pl.BlockSpec((1, 8, 2 * rows), lambda h, *_: (h, 0, 0)),
            ],
            out_specs=[column(rows), column(wide), column(wide)],
            scratch_shapes=[
                pltpu.VMEM((WINDOW, 2 * TILE), f32),
                pltpu.VMEM((PAIR, WINDOW), bf16),
                pltpu.VMEM((rows, PAIR), f32),
                pltpu.VMEM((wide, PAIR), f32),
                pltpu.VMEM((wide, PAIR), f32),
            ],
        ),
        compiler_params=pltpu.CompilerParams(vmem_limit_bytes=48 * 2**20),
    )(lengths, first, queries, keys, values, grads, stats)


TN = (((0,), (0,)), ((), ()))


def row_mean(value):
    return jnp.mean(value, axis=-1, keepdims=True)


def column_sum(value):
    return jnp.sum(value, axis=0, keepdims=True)


def normalize(summed):
    centered = summed - row_mean(summed)
    inverse_std = lax.rsqrt(row_mean(centered * centered) + norm_eps)
    return centered * inverse_std, inverse_std


def normalize_back(grad, normed, inverse_std):
    return inverse_std * (grad - row_mean(grad) - normed * row_mean(grad * normed))


def feed_kernel(plan, *refs):
    held, in_dest, out_slot, shard, deep, thin_first = plan
    me_ref, att_ref, states_ref, cot_ref, vec_ref, upb_ref = refs[:6]
    mixed_in, down_in = refs[6 : 6 + held], refs[6 + held : 6 + 2 * held]
    at = 6 + 2 * held
    result_ref, res_ref, gatt_ref, small_ref = refs[at : at + 4]
    mixed_out, down_out = refs[at + 4 : at + 4 + held], refs[at + 4 + held : at + 4 + 2 * held]
    at += 4 + 2 * held
    (wslot, wmix, wdown, act, slope, gmix, gdown, acc, in_sem, out_sem) = refs[at:]
    me = me_ref[0]
    width = states_ref.shape[1]
    hidden = wdown.shape[0]
    slots = len(in_dest[0][0])

    def copies_in():
        for a in range(held):
            for j in range(slots):
                dest = in_dest[0][a][j] ^ me
                yield pltpu.make_async_copy(
                    mixed_in[a].at[j], wslot.at[dest], in_sem.at[0, a * slots + j]
                )

    def copies_down():
        for a in range(held):
            for j in range(slots):
                dest = pl.multiple_of((in_dest[1][a][j] ^ me) * deep, 16)
                yield pltpu.make_async_copy(
                    down_in[a].at[j], wdown.at[pl.ds(dest, deep), :], in_sem.at[1, a * slots + j]
                )

    for copy in copies_in():
        copy.start()
    for copy in copies_down():
        copy.start()
    for copy in copies_in():
        copy.wait()
    total = held * slots
    step = min(total, 8)
    for d in range(0, total, step):
        block = wslot[d : d + step].astype(f32).reshape(step * shard, wslot.shape[2])
        wmix[d * shard : (d + step) * shard, :] = block.astype(bf16)

    bias_out, bias_down, gain_one, shift_one, gain_two, shift_two = (
        vec_ref[i : i + 1, :] for i in range(6)
    )
    branch = mul(att_ref[...], wmix[:, :width]) + bias_out
    normed_one, scale_one = normalize(states_ref[...].astype(f32) + branch)
    first_norm = normed_one * gain_one + shift_one
    inner = first_norm.astype(bf16)
    for copy in copies_down():
        copy.wait()
    chunks = range(0, hidden, width)
    for c in chunks:
        lifted = mul(inner, wmix[:, width + c : 2 * width + c]) + upb_ref[:, c : c + width]
        phi_sum = 0.5 * (1.0 + lax.erf(lifted * root_half))
        active = (lifted * phi_sum).astype(bf16)
        act[:, c : c + width] = active
        slope[:, c : c + width] = phi_sum + lifted * (
            inverse_root_two_pi * jnp.exp(-0.5 * lifted * lifted)
        )
        part = mul(active, wdown[c : c + width, :])
        acc[...] = part if c == 0 else acc[...] + part
    normed_two, scale_two = normalize(first_norm + (acc[...] + bias_down))
    result_ref[...] = (normed_two * gain_two + shift_two).astype(bf16)

    cot = cot_ref[...].astype(f32)
    small_ref[4:5, :] = column_sum(cot * normed_two)
    small_ref[5:6, :] = column_sum(cot)
    grad_mid = normalize_back(cot * gain_two, normed_two, scale_two)
    grad_down = grad_mid.astype(bf16)
    small_ref[1:2, :] = column_sum(grad_down.astype(f32))

    def put(target, order, value, first, per):
        for i in range(value.shape[0] // per):
            rows = value[i * per : (i + 1) * per]
            yield out_slot(order, (first + i) ^ me if total > 1 else 0), rows

    def copies_out(order, source, targets, sem):
        for a in range(held):
            yield pltpu.make_async_copy(
                source.at[pl.ds(a * slots, slots)], targets[a], out_sem.at[sem, a]
            )

    inner_t = inner.T
    for c in chunks:
        active = act[:, c : c + width]
        grad_active = mul(grad_down, wdown[c : c + width, :], NT)
        grad_lift = (grad_active * slope[:, c : c + width]).astype(bf16)
        small_ref[8 + c // width : 9 + c // width, :] = column_sum(grad_lift.astype(f32))
        grad_w = mul(active, grad_down, TN).astype(bf16)
        for slot, rows in put(gdown, 1, grad_w, c // deep, min(deep, width)):
            if total > 1:
                gdown[slot] = rows
            else:
                gdown[slot, c : c + width, :] = rows
        grad_w = mul(inner_t, grad_lift)
        for slot, rows in put(gmix, 0, grad_w, 0, shard):
            gmix[slot, :, width + c : 2 * width + c] = rows.astype(bf16)
        part = mul(grad_lift, wmix[:, width + c : 2 * width + c], NT)
        acc[...] = part if c == 0 else acc[...] + part
    for copy in copies_out(1, gdown, down_out, 1):
        copy.start()
    grad_first = acc[...] + grad_mid
    small_ref[2:3, :] = column_sum(grad_first * normed_one)
    small_ref[3:4, :] = column_sum(grad_first)
    grad_residual = normalize_back(grad_first * gain_one, normed_one, scale_one)
    res_ref[...] = grad_residual
    grad_branch = grad_residual.astype(bf16)
    small_ref[0:1, :] = column_sum(grad_branch.astype(f32))
    grad_w = mul(att_ref[...], grad_branch, TN)
    for slot, rows in put(gmix, 0, grad_w, 0, shard):
        gmix[slot, :, :width] = rows.astype(bf16)
    for copy in copies_out(0, gmix, mixed_out, 0):
        copy.start()
    gatt_ref[...] = mul(grad_branch, wmix[:, :width], NT).astype(bf16)
    small_ref[6:8, :] = jnp.zeros((2, width), f32)
    small_ref[12:, :] = jnp.zeros((small_ref.shape[0] - 12, width), f32)
    for copy in (*copies_out(1, gdown, down_out, 1), *copies_out(0, gmix, mixed_out, 0)):
        copy.wait()


def exchange_slot(bits):
    def slot(diff):
        found = jnp.int32(0)
        for at, bit in enumerate(reversed(bits)):
            found = found + (((diff & bit) != 0).astype(jnp.int32) << at)
        return found

    return slot


def feed_forward(me, attended, states, cotangent, vectors, up_bias, mixed, down, orders, backs):
    rows, width = states.shape
    held, (slots, shard, columns) = len(mixed), mixed[0].shape
    deep = down[0].shape[1]
    hidden = held * slots * deep
    if held > 1:
        dest = [
            [relative(order[:-1]), [r + order[-1] for r in relative(order[:-1])]]
            for order in orders
        ]
    else:
        dest = [[[0]], [[0]]]
    slot_of = [exchange_slot(back) for back in backs]
    plan = (held, dest, lambda order, diff: slot_of[order](diff) if held > 1 else 0, shard, deep, 0)
    whole = pl.BlockSpec(memory_space=pltpu.VMEM)
    anywhere = pl.BlockSpec(memory_space=pl.ANY)
    shape = jax.ShapeDtypeStruct
    total = held * slots
    return pl.pallas_call(
        functools.partial(feed_kernel, plan),
        name="feed_forward",
        out_shape=(
            shape((rows, width), bf16),
            shape((rows, width), f32),
            shape((rows, width), bf16),
            shape((16, width), f32),
            *[shape((slots, shard, columns), bf16)] * held,
            *[shape((slots, deep, width), bf16)] * held,
        ),
        in_specs=[pl.BlockSpec(memory_space=pltpu.SMEM), *[whole] * 5, *[anywhere] * (2 * held)],
        out_specs=[*[whole] * 4, *[anywhere] * (2 * held)],
        scratch_shapes=[
            pltpu.VMEM((total, shard, columns), bf16),
            pltpu.VMEM((total * shard, columns), bf16),
            pltpu.VMEM((hidden, width), bf16),
            pltpu.VMEM((rows, hidden), bf16),
            pltpu.VMEM((rows, hidden), f32),
            pltpu.VMEM((total, shard, columns), bf16),
            pltpu.VMEM((total, deep, width), bf16),
            pltpu.VMEM((rows, width), f32),
            pltpu.SemaphoreType.DMA((2, total)),
            pltpu.SemaphoreType.DMA((2, held)),
        ],
        compiler_params=pltpu.CompilerParams(vmem_limit_bytes=60 * 2**20),
    )(me, attended, states, cotangent, vectors, up_bias, *mixed, *down)


def local(
    hidden_states,
    owner_rows,
    lengths,
    attention_weight,
    output_weight,
    upward_weight,
    downward_weight,
    query_bias,
    value_bias,
    output_bias,
    upward_bias,
    downward_bias,
    first_gain,
    first_shift,
    second_gain,
    second_shift,
    output_cotangent,
):
    rows, width = hidden_states.shape
    heads_axis, blocks_axis = lax.axis_size("head"), lax.axis_size("blk")
    count = heads_axis * blocks_axis
    me = lax.axis_index(AXES)
    head, blk = lax.axis_index("head"), lax.axis_index("blk")
    first = ((blk * heads_axis + head) * rows).astype(jnp.int32).reshape(1)
    bits = [1 << b for b in range((count - 1).bit_length())]
    far = [b for b in bits if b not in (1, 2, blocks_axis)][::-1]
    order_a = tuple(far + [blocks_axis, 2, 1])
    order_b = tuple(far + [2, blocks_axis, 1])
    back_a, back_b = order_a[::-1], order_b[::-1]
    shard = attention_weight.shape[0]
    slotted = shard % 8 == 0
    half = width // 2

    def along(block, by_first, by_second):
        pairs = [
            (h * blocks_axis + b, h * blocks_axis + b + by)
            for h, by in ((0, by_first), (1, by_second))
            for b in range(blocks_axis)
            if 0 <= b + by < blocks_axis
        ]
        return lax.ppermute(block, AXES, pairs)

    slot_index = owner_rows % rows
    pick = (slot_index[None, :] == jnp.arange(rows, dtype=jnp.int32)[:, None]).astype(bf16)
    states = jnp.dot(pick, hidden_states, preferred_element_type=f32).astype(bf16)
    cotangent = jnp.dot(pick, output_cotangent, preferred_element_type=f32).astype(bf16)

    thin = -(-(SEG_ROWS - 1 - rows) // 16) * 16
    side = rows + thin
    partner = swap(states, blocks_axis, count)
    is_first = head == 0
    sent = jnp.where(
        is_first,
        jnp.concatenate([states[rows - thin :], partner], axis=0),
        jnp.concatenate([partner, states[:thin]], axis=0),
    )
    outer = along(sent, 1, -1)
    edge = along(jnp.where(is_first, states[:thin], states[rows - thin :]), -1, 1)
    reach = jnp.where(
        is_first,
        jnp.concatenate([outer, states, partner, edge], axis=0),
        jnp.concatenate([edge, partner, states, outer], axis=0),
    )

    small = (
        query_bias,
        value_bias,
        output_bias,
        downward_bias,
        first_gain,
        first_shift,
        second_gain,
        second_shift,
        upward_bias,
    )
    small_widths = [v.shape[0] for v in small]
    small_ends = np.cumsum(small_widths)
    packed = jnp.concatenate([v.reshape(shard, -1) for v in small], axis=1)
    packed = jnp.pad(packed, ((0, 0), (0, -packed.shape[1] % 128)))
    lead = [
        jnp.concatenate([attention_weight[:, n * width + o :][:, :half] for n in range(3)], axis=1)
        for o in (0, half)
    ]
    lead[0] = jnp.concatenate([lead[0], packed], axis=1)
    lead_orders = (order_a, order_b)
    follow = [jnp.concatenate([output_weight, upward_weight], axis=1), downward_weight]
    follow_orders = (order_a, order_b)
    if slotted:
        follow = [block[None] for block in follow]
    follow_parts = [[block] for block in follow]
    for step in range(len(bits)):
        lead_recv = [swap(b, o[step], count) for b, o in zip(lead, lead_orders)]
        if slotted and step == len(bits) - 1:
            lead = [
                merge(b, o[:step], r, o[step], me)
                for b, o, r in zip(lead, lead_orders, lead_recv)
            ]
            break
        follow = [after(b, *lead_recv) for b in follow]
        follow_recv = [swap(b, o[step], count) for b, o in zip(follow, follow_orders)]
        lead = [
            merge(b, o[:step], r, o[step], me) for b, o, r in zip(lead, lead_orders, lead_recv)
        ]
        if not slotted:
            follow = [
                merge(b, o[:step], r, o[step], me)
                for b, o, r in zip(follow, follow_orders, follow_recv)
            ]
            follow_parts = [
                [flat(b, rest.shape[0], 2 << step)[None]]
                for b, rest in zip(follow, (output_weight, downward_weight))
            ]
        elif step < len(bits) - 1:
            follow = [jnp.concatenate(pair, axis=0) for pair in zip(follow, follow_recv)]
    weight_a, weight_b = (flat(b, shard, count) for b in lead[:2])
    packed_all = weight_a[:, 3 * half :].astype(f32)
    (
        bias_query,
        bias_value,
        bias_output,
        bias_downward,
        gain_one,
        shift_one,
        gain_two,
        shift_two,
        bias_upward,
    ) = [
        packed_all[:, (end - n) // shard : end // shard].reshape(count * n)
        for end, n in zip(small_ends, small_widths)
    ]
    columns = lambda n: jnp.concatenate(
        [w[:, n * half : (n + 1) * half] for w in (weight_a, weight_b)], axis=1
    )
    weight_query, weight_key, weight_value = (columns(n) for n in range(3))

    queries = (
        (jnp.dot(states, weight_query, preferred_element_type=f32) + bias_query).astype(bf16)
        * jnp.asarray(score_scale, bf16)
    )
    keys = jnp.dot(reach, weight_key, preferred_element_type=f32).astype(bf16)
    values = (jnp.dot(reach, weight_value, preferred_element_type=f32) + bias_value).astype(bf16)
    attended, stats = attention_forward(lengths, first, queries, keys, values, side)
    if slotted:
        follow_parts = [
            [b, swap(after(b, attended), o[-1], count)] for b, o in zip(follow, follow_orders)
        ]

    vectors = jnp.stack(
        [bias_output, bias_downward, gain_one, shift_one, gain_two, shift_two]
        + [jnp.zeros((width,), f32)] * 2
    )
    me_of = me.astype(jnp.int32).reshape(1)
    outs = feed_forward(
        me_of,
        attended,
        states,
        cotangent,
        vectors,
        bias_upward[None],
        *follow_parts,
        follow_orders,
        (back_a, back_b),
    )
    result, grad_residual, grad_attended, small_sums = outs[:4]
    layer_output = jnp.take(result, slot_index, axis=0)
    if slotted:
        (mixed_keep, mixed_send, down_keep, down_send) = outs[4:]
        reductions = [
            halved(mixed_keep, mixed_send, back_a, count),
            halved(down_keep, down_send, back_b, count),
        ]
        sends = [next(r) for r in reductions]
        grad_attended = after(grad_attended, *sends)
        for _ in range(len(bits) - 1):
            sends = [r.send(s) for r, s in zip(reductions, sends)]
        out_mixed, out_downward = [r.send(s) for r, s in zip(reductions, sends)]
    else:
        out_mixed = reduced(outs[4].reshape(count, shard, -1), back_a, count, me)
        out_downward = reduced(outs[5].reshape((count,) + downward_weight.shape), back_b, count, me)

    grad_query, grad_key, grad_value = attention_backward(
        lengths, first, queries, keys, values, grad_attended, stats, side
    )
    grad_columns = [
        jnp.einsum("rd,rc->dc", rows_of, grad, preferred_element_type=f32).astype(bf16)
        for rows_of, grad in ((states, grad_query), (reach, grad_key), (reach, grad_value))
    ]
    grad_a, grad_b = (
        jnp.concatenate([g[:, o : o + half] for g in grad_columns], axis=1).reshape(
            count, shard, 3 * half
        )
        for o in (0, half)
    )
    grad_query_bias = jnp.sum(grad_query.astype(f32), axis=0)
    grad_value_bias = jnp.sum(grad_value.astype(f32), axis=0)
    grad_reach = jnp.einsum(
        "rc,dc->rd", grad_key, weight_key, preferred_element_type=f32
    ) + jnp.einsum("rc,dc->rd", grad_value, weight_value, preferred_element_type=f32)
    low_part, middle, high_part = (
        grad_reach[:side],
        grad_reach[side : side + rows],
        grad_reach[side + rows :],
    )
    grad_outer = jnp.where(is_first, low_part, high_part)
    grad_near = jnp.where(is_first, high_part[:rows], low_part[thin:])
    grad_edge = jnp.where(is_first, high_part[rows:], low_part[:thin])
    back = along(grad_outer.astype(bf16), -1, 1).astype(f32)
    back_edge = along(grad_edge.astype(bf16), 1, -1).astype(f32)
    back_own = jnp.where(is_first, back[:thin], back[rows:])
    back_partner = jnp.where(is_first, back[thin:], back[:rows])
    back_near = swap((grad_near + back_partner).astype(bf16), blocks_axis, count).astype(f32)
    pad_low = lambda v: jnp.pad(v, ((0, rows - thin), (0, 0)))
    pad_high = lambda v: jnp.pad(v, ((rows - thin, 0), (0, 0)))
    grad_input = (
        middle
        + jnp.einsum("rc,dc->rd", grad_query, weight_query, preferred_element_type=f32)
        + grad_residual
        + back_near
        + jnp.where(
            is_first, pad_high(back_own) + pad_low(back_edge), pad_low(back_own) + pad_high(back_edge)
        )
    )
    grad_hidden = jnp.take(grad_input, slot_index, axis=0)

    out_a = reduced(grad_a, back_a, count, me)
    out_b = reduced(grad_b, back_b, count, me)
    out_triple = jnp.concatenate(
        [o[:, n * half : (n + 1) * half] for n in range(3) for o in (out_a, out_b)], axis=1
    )
    by_device = lambda grad: grad.reshape((count, grad.shape[0] // count))
    packed_grads = jnp.concatenate(
        [by_device(g) for g in (grad_query_bias, grad_value_bias, *small_sums[:6])]
        + [by_device(small_sums[8 : 8 + upward_weight.shape[1] // width].reshape(-1))],
        axis=1,
    )
    packed_grads = jnp.pad(packed_grads, ((0, 0), (0, -packed_grads.shape[1] % 128)))
    summed = reduced(packed_grads, back_a, count, me)
    (
        out_query,
        out_value,
        out_output,
        out_down_bias,
        out_gain_one,
        out_shift_one,
        out_gain_two,
        out_shift_two,
        out_up_bias,
    ) = [summed[end - n : end] for end, n in zip(small_ends, small_widths)]
    return (
        layer_output,
        grad_hidden,
        out_triple,
        out_mixed[:, :width],
        out_mixed[:, width:],
        out_downward,
        out_query,
        out_value,
        out_output,
        out_up_bias,
        out_down_bias,
        out_gain_one,
        out_shift_one,
        out_gain_two,
        out_shift_two,
    )


def solution(mesh):
    matrix, vector = P(AXES, None), P(AXES)
    return jax.shard_map(
        local,
        mesh=mesh,
        in_specs=(matrix, vector, P(), *[matrix] * 4, *[vector] * 9, matrix),
        out_specs=(*[matrix] * 6, *[vector] * 9),
        check_vma=False,
    )
```

```python
import functools

import jax
import jax.numpy as jnp
import numpy as np
from jax import lax
from jax.experimental import pallas as pl
from jax.experimental.pallas import tpu as pltpu
from jax.sharding import PartitionSpec as P

DH = 64
SEG_TOK = 502
MEMR = 10
SEG_ROWS = SEG_TOK + 2 * MEMR
AXES = ("head", "blk")
TILE = 128
PAIR = 2 * DH
WINDOW = 544

norm_eps = 1e-12
masked_score = -1e30
score_scale = 0.125
root_half = 0.7071067811865476
inverse_root_two_pi = 0.3989422804014327
f32 = jnp.float32
bf16 = jnp.bfloat16


def swap(block, bit, count):
    return lax.ppermute(block, AXES, [(i, i ^ bit) for i in range(count)])


def tied(values, others):
    values = tuple(values)
    return list(lax.optimization_barrier((*values, *others))[: len(values)])


def after(value, *others):
    return tied([value], others)[0]


def relative(bits):
    return [sum(bit for at, bit in enumerate(bits) if j >> at & 1) for j in range(1 << len(bits))]


def gathered(shard, order, count, me):
    held, have = shard, []
    for bit in order:
        axis = sum(b > bit for b in have)
        have.append(bit)
        other = jnp.expand_dims(swap(held, bit, count), axis)
        own = jnp.expand_dims(held, axis)
        held = jnp.where(
            (me & bit) == 0,
            jnp.concatenate([own, other], axis=axis),
            jnp.concatenate([other, own], axis=axis),
        )
    return held.reshape((count * shard.shape[0],) + shard.shape[1:])


def reduced(blocks, order, count, me):
    have = sorted(order, reverse=True)
    held = blocks.reshape((2,) * len(have) + blocks.shape[1:])
    for step, bit in enumerate(order):
        axis = have.index(bit)
        have.remove(bit)
        mine = ((me & bit) != 0).astype(jnp.int32)
        keep = lax.dynamic_index_in_dim(held, mine, axis, keepdims=False)
        send = lax.dynamic_index_in_dim(held, 1 - mine, axis, keepdims=False)
        total = keep.astype(f32) + swap(send, bit, count).astype(f32)
        held = total if not have else total.astype(blocks.dtype)
    return held


class Spread:
    def __init__(self, held, rounds, count):
        self.held, self.rounds, self.count = held, list(rounds), count
        self.parts = None

    def start(self):
        self.recvs = [swap(self.held, c, self.count) for c in relative(self.rounds[0])[1:]]

    def finish(self, token=()):
        recvs = tied(self.recvs, token) if token else self.recvs
        self.held = jnp.concatenate([self.held, *recvs], axis=0)
        self.rounds.pop(0)
        return self.held

    def start_two(self):
        self.start()
        (self.last,) = self.rounds[1]
        self.own = swap(self.held, self.last, self.count)

    def finish_two(self, token=()):
        recvs = tied(self.recvs, token) if token else self.recvs
        self.parts = [self.held, *recvs, self.own, *[swap(r, self.last, self.count) for r in recvs]]
        return recvs


def piece_places(rounds):
    base = relative([b for r in rounds[:-2] for b in r])
    pieces = [[j + c for j in base] for c in relative(rounds[-2])]
    return [[j + c for j in piece] for c in relative(rounds[-1]) for piece in pieces]


class Gathering:
    def __init__(self, keep, send, rounds, count):
        self.terms, self.sends, self.rounds, self.count = [keep], [send], list(rounds), count
        self.total = None
        self.start()

    def start(self):
        combos = relative(self.rounds[0][::-1])[1:]
        self.recvs = [swap(s, c, self.count) for s, c in zip(self.sends, combos)]

    def arrive(self, token=()):
        self.recvs = tied(self.recvs, token) if token else self.recvs
        return self.recvs

    def advance(self, token=()):
        recvs = self.arrive(token)
        self.terms += recvs
        self.rounds.pop(0)
        add = lambda at: sum(t[at].astype(f32) for t in self.terms)
        if not self.rounds:
            self.total = add(0)
            return [self.total]
        parts = 1 << len(self.rounds[0])
        each = self.terms[0].shape[0] // parts
        self.sends = [add(slice(j * each, (j + 1) * each)).astype(bf16) for j in range(1, parts)]
        self.terms = [t[:each] for t in self.terms]
        self.start()
        return self.sends


def segment_at(lengths_ref, sequences, position):
    start = jnp.int32(0)
    low = jnp.int32(0)
    high = jnp.int32(0)
    for i in range(sequences):
        tokens = lengths_ref[i]
        end = start + tokens + 2 * MEMR * lax.div(tokens + (SEG_TOK - 1), jnp.int32(SEG_TOK))
        inside = (position >= start) & (position < end)
        first = start + lax.div(position - start, jnp.int32(SEG_ROWS)) * SEG_ROWS
        low = jnp.where(inside, first, low)
        high = jnp.where(inside, jnp.minimum(first + SEG_ROWS, end), high)
        start = end
    return low, high


def over_segments(lengths_ref, sequences, first_row, rows, side, body):
    def step(position):
        low, high = segment_at(lengths_ref, sequences, position)
        high = jnp.maximum(high, position + 1)
        low_at = low - first_row + side
        high_at = high - first_row + side
        window = jnp.minimum(lax.div(low_at, jnp.int32(16)) * 16, rows + 2 * side - WINDOW)
        window = pl.multiple_of(jnp.maximum(window, 0), 16)
        tile_from = lax.div(jnp.maximum(low - first_row, 0), jnp.int32(TILE))
        tile_to = lax.div(jnp.minimum(high - first_row, rows) + TILE - 1, jnp.int32(TILE))
        body(low_at, high_at, window, tile_from, tile_to)
        return high

    lax.while_loop(lambda position: position < first_row + rows, step, first_row)


def two_heads(block):
    lane = lax.broadcasted_iota(jnp.int32, block.shape, 1)
    zero = jnp.zeros_like(block)
    return jnp.concatenate(
        [jnp.where(lane < DH, block, zero), jnp.where(lane < DH, zero, block)], axis=0
    )


def own_blocks(product):
    return jnp.concatenate([product[:DH, :TILE], product[DH:, TILE:]], axis=0).T


def key_bias(low_at, high_at, window):
    row = lax.broadcasted_iota(jnp.int32, (WINDOW, 2 * TILE), 0) + window
    return jnp.where((row >= low_at) & (row < high_at), 0.0, masked_score)


def rows_inside(tile, low_at, high_at, side, shape, dim):
    at = lax.broadcasted_iota(jnp.int32, shape, dim)
    if dim == 1:
        at = at & (TILE - 1)
    at = at + (tile * TILE + side)
    return (at >= low_at) & (at < high_at)


NT = (((1,), (1,)), ((), ()))
NN = (((1,), (0,)), ((), ()))


def mul(left, right, dims=NN):
    return lax.dot_general(left, right, dims, preferred_element_type=f32)


def slots_to_rows(slots, shard, store):
    total, _, columns = slots.shape
    step = min(total, 8)
    for d in range(0, total, step):
        block = slots[d : d + step].astype(f32).reshape(step * shard, columns)
        store(slice(d * shard, (d + step) * shard), block.astype(bf16))


def forward_kernel(plan, lengths_ref, first_ref, me_ref, *refs):
    sequences, side, taken, dests, shard = plan
    outer_ref, states_ref, partner_ref, edge_ref = refs[:4]
    pieces, refs = (refs[4 : 4 + taken], refs[4 + taken : 4 + 2 * taken]), refs[4 + 2 * taken :]
    (q_ref, k_ref, v_ref, o_ref, stat_ref, weight_ref, reach_ref, vec_ref) = refs[:8]
    bias_ref, vt_ref, slots_a, slots_b, small_ref, in_sem = refs[8:]
    rows, width = states_ref.shape
    half, thin = width // 2, edge_ref.shape[0]
    pair = pl.program_id(0)
    me, head = me_ref[0], me_ref[1]

    @pl.when(pair == 0)
    def _():
        slots = len(dests[0][0])
        copies = [
            pltpu.make_async_copy(
                pieces[n][a].at[j], target.at[dests[n][a][j] ^ me], in_sem.at[n, a * slots + j]
            )
            for n, target in enumerate((slots_a, slots_b))
            for a in range(taken)
            for j in range(slots)
        ]
        for copy in copies:
            copy.start()

        @pl.when(head == 0)
        def _():
            reach_ref[:side, :] = outer_ref[...]
            reach_ref[side + rows : side + 2 * rows, :] = partner_ref[...]
            reach_ref[side + 2 * rows :, :] = edge_ref[...]

        @pl.when(head != 0)
        def _():
            reach_ref[:thin, :] = edge_ref[...]
            reach_ref[thin:side, :] = partner_ref[...]
            reach_ref[side + rows :, :] = outer_ref[...]

        reach_ref[side : side + rows, :] = states_ref[...]
        for copy in copies:
            copy.wait()

        def store(offset):
            def put(at, block):
                for n in range(3):
                    to = n * width + offset
                    weight_ref[at, to : to + half] = block[:, n * half : (n + 1) * half]
                if block.shape[1] > 3 * half:
                    small_ref[at, :] = block[:, 3 * half :]

            return put

        slots_to_rows(slots_a, shard, store(0))
        slots_to_rows(slots_b, shard, store(half))
        vec_ref[...] = small_ref[...].astype(f32).T[: vec_ref.shape[0]]

    stat_ref[...] = jnp.zeros_like(stat_ref)
    o_ref[...] = jnp.zeros_like(o_ref)
    lanes = [pl.ds(pl.multiple_of(pair * PAIR + n * width, PAIR), PAIR) for n in range(3)]
    queries = mul(states_ref[...], weight_ref[:, lanes[0]]) + vec_ref[0:1, lanes[0]]
    q_ref[...] = queries.astype(bf16) * jnp.asarray(score_scale, bf16)
    both_weight = jnp.concatenate([weight_ref[:, lanes[1]], weight_ref[:, lanes[2]]], axis=1)
    both = mul(reach_ref[...], both_weight)
    k_ref[...] = both[:, :PAIR].astype(bf16)
    v_ref[...] = (both[:, PAIR:] + vec_ref[1:2, lanes[0]]).astype(bf16)

    def segment(low_at, high_at, window, tile_from, tile_to):
        bias_ref[...] = key_bias(low_at, high_at, window)
        keys_at = pl.ds(window, WINDOW)
        vt_ref[...] = v_ref[keys_at, :].T

        def one(tile, carry):
            at = pl.ds(pl.multiple_of(tile * TILE, TILE), TILE)
            wide = pl.ds(pl.multiple_of(tile * 2 * TILE, 2 * TILE), 2 * TILE)
            queries = two_heads(q_ref[at, :])
            scores = mul(k_ref[keys_at, :], queries, NT) + bias_ref[...]
            top = jnp.max(scores, axis=0, keepdims=True)
            raised = jnp.exp(scores - top)
            inverse = 1.0 / jnp.sum(raised, axis=0, keepdims=True)
            weights = (raised * inverse).astype(bf16)
            mixed = own_blocks(mul(vt_ref[...], weights)).astype(bf16)
            inside = rows_inside(tile, low_at, high_at, side, (TILE, PAIR), 0)
            o_ref[at, :] = jnp.where(inside, mixed, o_ref[at, :])
            there = rows_inside(tile, low_at, high_at, side, (1, 2 * TILE), 1)
            stat_ref[0, 0:1, wide] = jnp.where(there, top, stat_ref[0, 0:1, wide])
            stat_ref[0, 1:2, wide] = jnp.where(there, inverse, stat_ref[0, 1:2, wide])
            return carry

        lax.fori_loop(tile_from, tile_to, one, 0)

    over_segments(lengths_ref, sequences, first_ref[0], rows, side, segment)


def backward_kernel(
    plan,
    lengths_ref,
    first_ref,
    me_ref,
    q_ref,
    k_ref,
    v_ref,
    g_ref,
    stat_ref,
    reach_ref,
    *refs,
):
    sequences, side, held, slot_of, shard = plan
    sums_in, dq_ref, dk_ref, dv_ref = refs[:4]
    outs = (refs[4 : 4 + held], refs[4 + held : 4 + 2 * held])
    (bias_ref, kt_ref, dq_acc, dk_acc, dv_acc, reach_t, slots_ref, small_ref, sem) = refs[4 + 2 * held :]
    rows = q_ref.shape[0]
    pair, pairs = pl.program_id(0), pl.num_programs(0)
    me = me_ref[0]
    total, width = slots_ref.shape[1], reach_ref.shape[1]
    half = width // 2

    @pl.when(pair == 0)
    def _():
        reach_t[...] = reach_ref[...].T
        small_ref[...] = jnp.zeros_like(small_ref)

    dq_acc[...] = jnp.zeros_like(dq_acc)
    dk_acc[...] = jnp.zeros_like(dk_acc)
    dv_acc[...] = jnp.zeros_like(dv_acc)

    def segment(low_at, high_at, window, tile_from, tile_to):
        bias_ref[...] = key_bias(low_at, high_at, window)
        keys_at = pl.ds(window, WINDOW)
        kt_ref[...] = k_ref[keys_at, :].T

        def one(tile, carry):
            at = pl.ds(pl.multiple_of(tile * TILE, TILE), TILE)
            wide = pl.ds(pl.multiple_of(tile * 2 * TILE, 2 * TILE), 2 * TILE)
            queries = two_heads(q_ref[at, :])
            grads = two_heads(g_ref[at, :])
            there = rows_inside(tile, low_at, high_at, side, (1, 2 * TILE), 1)
            top = jnp.where(there, stat_ref[0, 0:1, wide], -masked_score)
            inverse = jnp.where(there, stat_ref[0, 1:2, wide], 0.0)
            scores = mul(k_ref[keys_at, :], queries, NT) + bias_ref[...]
            probs = jnp.exp(scores - top) * inverse
            grad_probs = mul(v_ref[keys_at, :], grads, NT)
            shared = jnp.sum(probs * grad_probs, axis=0, keepdims=True)
            grad_scores = (probs * (grad_probs - shared)).astype(bf16)
            dv_acc[keys_at, :] += mul(probs.astype(bf16), grads)
            dk_acc[keys_at, :] += mul(grad_scores, queries)
            dq_acc[at, :] += own_blocks(mul(kt_ref[...], grad_scores))
            return carry

        lax.fori_loop(tile_from, tile_to, one, 0)

    over_segments(lengths_ref, sequences, first_ref[0], rows, side, segment)
    dq = (dq_acc[...] * score_scale).astype(bf16)
    dkv = jnp.concatenate([dk_acc[...].astype(bf16), dv_acc[...].astype(bf16)], axis=1)
    dq_ref[...] = dq
    dk_ref[...] = dkv[:, :PAIR]
    dv_ref[...] = dkv[:, PAIR:]
    here = pl.ds(pl.multiple_of(pair * PAIR, PAIR), PAIR)
    small_ref[0:1, here] = jnp.sum(dq.astype(f32), axis=0, keepdims=True)
    small_ref[1:2, here] = jnp.sum(dkv[:, PAIR:].astype(f32), axis=0, keepdims=True)
    which = lax.div(pair, lax.div(pairs, 2))
    inner = lax.rem(pair, lax.div(pairs, 2)) * PAIR
    lanes = [pl.ds(pl.multiple_of(inner + n * half, PAIR), PAIR) for n in range(3)]

    def put(to, value, columns):
        for i in range(total):
            slot = slot_of(to, i ^ me) if total > 1 else 0
            slots_ref[to, slot, :, columns] = value[i * shard : (i + 1) * shard].astype(bf16)

    own_t = reach_ref[side : side + rows, :]
    grad_q = mul(own_t, dq, (((0,), (0,)), ((), ())))
    grad_w = mul(reach_t[...], dkv)
    for to in range(2):

        @pl.when(which == to)
        def _():
            put(to, grad_q, lanes[0])
            put(to, grad_w[:, :PAIR], lanes[1])
            put(to, grad_w[:, PAIR:], lanes[2])

    each = total // held
    copies = lambda to: [
        pltpu.make_async_copy(
            slots_ref.at[to, pl.ds(a * each, each), :, pl.ds(0, 3 * half + to * TILE)],
            outs[to][a],
            sem.at[to, a],
        )
        for a in range(held)
    ]

    @pl.when(pair == lax.div(pairs, 2))
    def _():
        for copy in copies(0):
            copy.start()

    @pl.when(pair == pairs - 1)
    def _():
        count = sums_in.shape[0]
        small_ref[2 : 2 + count, :] = sums_in[...]
        put(1, small_ref[...].T, pl.ds(3 * half, TILE))
        for copy in copies(1):
            copy.start()
        for copy in (*copies(0), *copies(1)):
            copy.wait()


def pack_kernel(shard, weight_ref, output_ref, upward_ref, *refs):
    *vector_refs, lead_ref, mixed_ref, rows_ref = refs
    rows_ref[...] = jnp.zeros_like(rows_ref)
    row = 0
    for ref in vector_refs:
        values = ref[...].astype(f32).reshape(1, ref.shape[0])
        for at in range(0, ref.shape[0], shard):
            rows_ref[row : row + 1, :shard] = values[:, at : at + shard]
            row += 1
    width = output_ref.shape[1]
    half = width // 2
    for n in range(3):
        for to in range(2):
            at = (3 * to + n) * half
            lead_ref[:, at : at + half] = weight_ref[:, n * width + to * half :][:, :half]
    lead_ref[:, 3 * width :] = rows_ref[...].T[:shard].astype(bf16)
    mixed_ref[:, :width] = output_ref[...]
    mixed_ref[:, width:] = upward_ref[...]


def pack(weight, output, upward, vectors):
    shard = weight.shape[0]
    shape = jax.ShapeDtypeStruct
    return pl.pallas_call(
        functools.partial(pack_kernel, shard),
        name="pack",
        out_shape=(
            shape((shard, weight.shape[1] + 128), bf16),
            shape((shard, output.shape[1] + upward.shape[1]), bf16),
        ),
        in_specs=[pl.BlockSpec(memory_space=pltpu.VMEM)] * (3 + len(vectors)),
        out_specs=[pl.BlockSpec(memory_space=pltpu.VMEM)] * 2,
        scratch_shapes=[pltpu.VMEM((128, 128), f32)],
    )(weight, output, upward, *vectors)


def attention_forward(lengths, first, me_head, rows_of, pieces, side, dests):
    outer, states, partner, edge = rows_of
    rows, features = states.shape
    wide = rows + 2 * side
    taken, (slots, shard, columns) = len(pieces[0]), pieces[0][0].shape
    pairs = features // PAIR
    whole = lambda *shape: pl.BlockSpec(shape, lambda h, *_: (0,) * len(shape))
    column = lambda n: pl.BlockSpec((n, PAIR), lambda h, *_: (0, h))
    anywhere = pl.BlockSpec(memory_space=pl.ANY)
    shape = jax.ShapeDtypeStruct
    plan = (lengths.shape[0], side, taken, dests, shard)
    return pl.pallas_call(
        functools.partial(forward_kernel, plan),
        name="attention_forward",
        out_shape=(
            shape((rows, features), bf16),
            shape((wide, features), bf16),
            shape((wide, features), bf16),
            shape((rows, features), bf16),
            shape((pairs, 8, 2 * rows), f32),
            shape((features, 3 * features), bf16),
            shape((wide, features), bf16),
            shape((16, features), f32),
        ),
        grid_spec=pltpu.PrefetchScalarGridSpec(
            num_scalar_prefetch=3,
            grid=(pairs,),
            in_specs=[*[whole(*r.shape) for r in rows_of], *[anywhere] * (2 * taken)],
            out_specs=[
                column(rows),
                column(wide),
                column(wide),
                column(rows),
                pl.BlockSpec((1, 8, 2 * rows), lambda h, *_: (h, 0, 0)),
                whole(features, 3 * features),
                whole(wide, features),
                whole(16, features),
            ],
            scratch_shapes=[
                pltpu.VMEM((WINDOW, 2 * TILE), f32),
                pltpu.VMEM((PAIR, WINDOW), bf16),
                *[pltpu.VMEM((taken * slots,) + half[0].shape[1:], bf16) for half in pieces],
                pltpu.VMEM((features, columns - 3 * features // 2), bf16),
                pltpu.SemaphoreType.DMA((2, taken * slots)),
            ],
        ),
        compiler_params=pltpu.CompilerParams(vmem_limit_bytes=48 * 2**20),
    )(lengths, first, me_head, *rows_of, *pieces[0], *pieces[1])


def attention_backward(
    lengths, first, me, queries, keys, values, grads, stats, reach, side, shard, held, backs, sums
):
    rows, features = queries.shape
    wide = keys.shape[0]
    pairs = features // PAIR
    total = features // shard if held > 1 else 1
    per = shard if held > 1 else features
    columns = 3 * features // 2
    column = lambda n: pl.BlockSpec((n, PAIR), lambda h, *_: (0, h))
    whole = lambda *shape: pl.BlockSpec(shape, lambda h, *_: (0,) * len(shape))
    anywhere = pl.BlockSpec(memory_space=pl.ANY)
    shape = jax.ShapeDtypeStruct
    slot_of = [exchange_slot(back) for back in backs]
    place = lambda to, diff: slot_of[to](diff)
    return pl.pallas_call(
        functools.partial(backward_kernel, (lengths.shape[0], side, held, place, per)),
        name="attention_backward",
        out_shape=(
            shape((rows, features), bf16),
            shape((wide, features), bf16),
            shape((wide, features), bf16),
            *[shape((total // held, per, columns), bf16)] * held,
            *[shape((total // held, per, columns + TILE), bf16)] * held,
        ),
        grid_spec=pltpu.PrefetchScalarGridSpec(
            num_scalar_prefetch=3,
            grid=(pairs,),
            in_specs=[
                column(rows),
                column(wide),
                column(wide),
                column(rows),
                pl.BlockSpec((1, 8, 2 * rows), lambda h, *_: (h, 0, 0)),
                whole(wide, features),
                whole(*sums.shape),
            ],
            out_specs=[column(rows), column(wide), column(wide), *[anywhere] * (2 * held)],
            scratch_shapes=[
                pltpu.VMEM((WINDOW, 2 * TILE), f32),
                pltpu.VMEM((PAIR, WINDOW), bf16),
                pltpu.VMEM((rows, PAIR), f32),
                pltpu.VMEM((wide, PAIR), f32),
                pltpu.VMEM((wide, PAIR), f32),
                pltpu.VMEM((features, wide), bf16),
                pltpu.VMEM((2, total, per, columns + TILE), bf16),
                pltpu.VMEM((TILE, features), f32),
                pltpu.SemaphoreType.DMA((2, held)),
            ],
        ),
        compiler_params=pltpu.CompilerParams(vmem_limit_bytes=56 * 2**20),
    )(lengths, first, me, queries, keys, values, grads, stats, reach, sums)


TN = (((0,), (0,)), ((), ()))


def row_mean(value):
    return jnp.mean(value, axis=-1, keepdims=True)


def column_sum(value):
    return jnp.sum(value, axis=0, keepdims=True)


def normalize(summed):
    centered = summed - row_mean(summed)
    inverse_std = lax.rsqrt(row_mean(centered * centered) + norm_eps)
    return centered * inverse_std, inverse_std


def normalize_back(grad, normed, inverse_std):
    return inverse_std * (grad - row_mean(grad) - normed * row_mean(grad * normed))


def feed_kernel(plan, *refs):
    taken, held, in_dest, out_slot, shard, deep = plan
    me_ref, att_ref, states_ref, cot_ref, vec_ref, upb_ref = refs[:6]
    mixed_in, down_in = refs[6 : 6 + taken], refs[6 + taken : 6 + 2 * taken]
    at = 6 + 2 * taken
    result_ref, res_ref, gatt_ref, small_ref = refs[at : at + 4]
    mixed_out, down_out = refs[at + 4 : at + 4 + held], refs[at + 4 + held : at + 4 + 2 * held]
    at += 4 + 2 * held
    (wslot, wmix, wdown, act, slope, gmix, gdown, acc, in_sem, out_sem) = refs[at:]
    me = me_ref[0]
    width = states_ref.shape[1]
    hidden = wdown.shape[0]
    slots = len(in_dest[0][0])

    def copies_in():
        for a in range(taken):
            for j in range(slots):
                dest = in_dest[0][a][j] ^ me
                yield pltpu.make_async_copy(
                    mixed_in[a].at[j], wslot.at[dest], in_sem.at[0, a * slots + j]
                )

    def copies_down():
        for a in range(taken):
            for j in range(slots):
                dest = pl.multiple_of((in_dest[1][a][j] ^ me) * deep, 16)
                yield pltpu.make_async_copy(
                    down_in[a].at[j], wdown.at[pl.ds(dest, deep), :], in_sem.at[1, a * slots + j]
                )

    for copy in copies_in():
        copy.start()
    for copy in copies_down():
        copy.start()
    for copy in copies_in():
        copy.wait()
    total = taken * slots

    def store(at, block):
        wmix[at, :] = block

    slots_to_rows(wslot, shard, store)

    bias_out, bias_down, gain_one, shift_one, gain_two, shift_two = (
        vec_ref[i : i + 1, :] for i in range(2, 8)
    )
    branch = mul(att_ref[...], wmix[:, :width]) + bias_out
    normed_one, scale_one = normalize(states_ref[...].astype(f32) + branch)
    first_norm = normed_one * gain_one + shift_one
    inner = first_norm.astype(bf16)
    for copy in copies_down():
        copy.wait()
    chunks = range(0, hidden, width)
    for c in chunks:
        lifted = mul(inner, wmix[:, width + c : 2 * width + c]) + upb_ref[:, c : c + width]
        phi_sum = 0.5 * (1.0 + lax.erf(lifted * root_half))
        active = (lifted * phi_sum).astype(bf16)
        act[:, c : c + width] = active
        slope[:, c : c + width] = phi_sum + lifted * (
            inverse_root_two_pi * jnp.exp(-0.5 * lifted * lifted)
        )
        part = mul(active, wdown[c : c + width, :])
        acc[...] = part if c == 0 else acc[...] + part
    normed_two, scale_two = normalize(first_norm + (acc[...] + bias_down))
    result_ref[...] = (normed_two * gain_two + shift_two).astype(bf16)

    cot = cot_ref[...].astype(f32)
    small_ref[4:5, :] = column_sum(cot * normed_two)
    small_ref[5:6, :] = column_sum(cot)
    grad_mid = normalize_back(cot * gain_two, normed_two, scale_two)
    grad_down = grad_mid.astype(bf16)
    small_ref[1:2, :] = column_sum(grad_down.astype(f32))

    def put(target, order, value, first, per):
        for i in range(value.shape[0] // per):
            rows = value[i * per : (i + 1) * per]
            yield out_slot(order, (first + i) ^ me if total > 1 else 0), rows

    def copies_out(order, source, targets, sem):
        for a in range(held):
            yield pltpu.make_async_copy(
                source.at[pl.ds(a * (total // held), total // held)], targets[a], out_sem.at[sem, a]
            )

    inner_t = inner.T
    for c in chunks:
        active = act[:, c : c + width]
        grad_active = mul(grad_down, wdown[c : c + width, :], NT)
        grad_lift = (grad_active * slope[:, c : c + width]).astype(bf16)
        small_ref[8 + c // width : 9 + c // width, :] = column_sum(grad_lift.astype(f32))
        grad_w = mul(active, grad_down, TN).astype(bf16)
        for slot, rows in put(gdown, 1, grad_w, c // deep, min(deep, width)):
            if total > 1:
                gdown[slot] = rows
            else:
                gdown[slot, c : c + width, :] = rows
        grad_w = mul(inner_t, grad_lift)
        for slot, rows in put(gmix, 0, grad_w, 0, shard):
            gmix[slot, :, width + c : 2 * width + c] = rows.astype(bf16)
        part = mul(grad_lift, wmix[:, width + c : 2 * width + c], NT)
        acc[...] = part if c == 0 else acc[...] + part
    for copy in copies_out(1, gdown, down_out, 1):
        copy.start()
    grad_first = acc[...] + grad_mid
    small_ref[2:3, :] = column_sum(grad_first * normed_one)
    small_ref[3:4, :] = column_sum(grad_first)
    grad_residual = normalize_back(grad_first * gain_one, normed_one, scale_one)
    res_ref[...] = grad_residual
    grad_branch = grad_residual.astype(bf16)
    small_ref[0:1, :] = column_sum(grad_branch.astype(f32))
    grad_w = mul(att_ref[...], grad_branch, TN)
    for slot, rows in put(gmix, 0, grad_w, 0, shard):
        gmix[slot, :, :width] = rows.astype(bf16)
    for copy in copies_out(0, gmix, mixed_out, 0):
        copy.start()
    gatt_ref[...] = mul(grad_branch, wmix[:, :width], NT).astype(bf16)
    small_ref[6:8, :] = jnp.zeros((2, width), f32)
    small_ref[12:, :] = jnp.zeros((small_ref.shape[0] - 12, width), f32)
    for copy in (*copies_out(1, gdown, down_out, 1), *copies_out(0, gmix, mixed_out, 0)):
        copy.wait()


def exchange_slot(bits):
    def slot(diff):
        found = jnp.int32(0)
        for at, bit in enumerate(reversed(bits)):
            found = found + (((diff & bit) != 0).astype(jnp.int32) << at)
        return found

    return slot


def feed_forward(me, attended, states, cotangent, vectors, up_bias, mixed, down, dests, backs):
    rows, width = states.shape
    taken, (slots, shard, columns) = len(mixed), mixed[0].shape
    held = min(taken, 2)
    deep = down[0].shape[1]
    total = taken * slots
    hidden = total * deep
    slot_of = [exchange_slot(back) for back in backs]
    place = lambda order, diff: slot_of[order](diff) if held > 1 else 0
    plan = (taken, held, dests, place, shard, deep)
    whole = pl.BlockSpec(memory_space=pltpu.VMEM)
    anywhere = pl.BlockSpec(memory_space=pl.ANY)
    shape = jax.ShapeDtypeStruct
    return pl.pallas_call(
        functools.partial(feed_kernel, plan),
        name="feed_forward",
        out_shape=(
            shape((rows, width), bf16),
            shape((rows, width), f32),
            shape((rows, width), bf16),
            shape((16, width), f32),
            *[shape((total // held, shard, columns), bf16)] * held,
            *[shape((total // held, deep, width), bf16)] * held,
        ),
        in_specs=[pl.BlockSpec(memory_space=pltpu.SMEM), *[whole] * 5, *[anywhere] * (2 * taken)],
        out_specs=[*[whole] * 4, *[anywhere] * (2 * held)],
        scratch_shapes=[
            pltpu.VMEM((total, shard, columns), bf16),
            pltpu.VMEM((total * shard, columns), bf16),
            pltpu.VMEM((hidden, width), bf16),
            pltpu.VMEM((rows, hidden), bf16),
            pltpu.VMEM((rows, hidden), f32),
            pltpu.VMEM((total, shard, columns), bf16),
            pltpu.VMEM((total, deep, width), bf16),
            pltpu.VMEM((rows, width), f32),
            pltpu.SemaphoreType.DMA((2, total)),
            pltpu.SemaphoreType.DMA((2, held)),
        ],
        compiler_params=pltpu.CompilerParams(vmem_limit_bytes=60 * 2**20),
    )(me, attended, states, cotangent, vectors, up_bias, *mixed, *down)


def local(
    hidden_states,
    owner_rows,
    lengths,
    attention_weight,
    output_weight,
    upward_weight,
    downward_weight,
    query_bias,
    value_bias,
    output_bias,
    upward_bias,
    downward_bias,
    first_gain,
    first_shift,
    second_gain,
    second_shift,
    output_cotangent,
):
    rows, width = hidden_states.shape
    heads_axis, blocks_axis = lax.axis_size("head"), lax.axis_size("blk")
    count = heads_axis * blocks_axis
    me = lax.axis_index(AXES)
    head, blk = lax.axis_index("head"), lax.axis_index("blk")
    first = ((blk * heads_axis + head) * rows).astype(jnp.int32).reshape(1)
    bits = [1 << b for b in range((count - 1).bit_length())]
    far = tuple(b for b in bits if b not in (1, 2, blocks_axis))[::-1]
    near_y, near_x, core = (2,), (blocks_axis,), (1,)
    apart = [(b,) for b in far]
    lead_rounds = ([far, near_x, near_y, core], [far, near_y, near_x, core])
    follow_rounds = (
        [far, near_x, near_y, core],
        [near_y, *apart, near_x, core],
    )
    back_rounds = (
        [core, near_y, near_x, far[::-1]],
        [core, near_x, far[::-1], near_y],
        [core, near_x, near_y, far[::-1]],
        [core, near_y, near_x, far[::-1]],
    )
    back_bits = [[b for r in rounds for b in r] for rounds in back_rounds]
    order = bits[::-1]
    shard = attention_weight.shape[0]
    slotted = shard % 8 == 0
    half = width // 2
    def along(block, by_first, by_second):
        pairs = [
            (h * blocks_axis + b, h * blocks_axis + b + by)
            for h, by in ((0, by_first), (1, by_second))
            for b in range(blocks_axis)
            if 0 <= b + by < blocks_axis
        ]
        return lax.ppermute(block, AXES, pairs)

    slot_index = owner_rows % rows
    pick = (slot_index[None, :] == jnp.arange(rows, dtype=jnp.int32)[:, None]).astype(bf16)
    states = jnp.dot(pick, hidden_states, preferred_element_type=f32).astype(bf16)
    cotangent = jnp.dot(pick, output_cotangent, preferred_element_type=f32).astype(bf16)

    thin = -(-(SEG_ROWS - 1 - rows) // 16) * 16
    side = rows + thin
    partner = swap(states, blocks_axis, count)
    is_first = head == 0
    sent = jnp.where(
        is_first,
        jnp.concatenate([states[rows - thin :], partner], axis=0),
        jnp.concatenate([partner, states[:thin]], axis=0),
    )
    outer = along(sent, 1, -1)
    edge = along(jnp.where(is_first, states[:thin], states[rows - thin :]), -1, 1)
    rows_of = (outer, states, partner, edge)

    small = (
        query_bias,
        value_bias,
        output_bias,
        downward_bias,
        first_gain,
        first_shift,
        second_gain,
        second_shift,
        upward_bias,
    )
    extra = upward_bias.shape[0] // shard
    lead, mixed = pack(attention_weight, output_weight, upward_weight, small)
    cut = 6 * half
    me_of = me.astype(jnp.int32).reshape(1)
    me_head = jnp.stack([me, head]).astype(jnp.int32)
    if slotted:
        lead_all = Spread(lead[None], lead_rounds[0], count)
        lead_all.start()
        follow = [
            Spread(block[None], rounds, count)
            for block, rounds in zip((mixed, downward_weight), follow_rounds)
        ]
        follow[1].start()
        held = lead_all.finish()
        lead_a = Spread(
            jnp.concatenate([held[..., : cut // 2], held[..., cut:]], axis=-1),
            lead_rounds[0][1:],
            count,
        )
        lead_b = Spread(held[..., cut // 2 : cut], lead_rounds[1][1:], count)
        leads = (lead_a, lead_b)
        [chain.start() for chain in leads]
        follow[0].held = after(follow[0].held, held)
        follow[0].start()
        token = [follow[1].finish([held])]
        follow[1].start()
        token = [*[chain.finish(token) for chain in leads], sent]
        [chain.start_two() for chain in leads]
        token = [chain.finish(token) for chain in follow]
        [chain.start() for chain in follow]
        token = [x for chain in leads for x in chain.finish_two(token)]
        token = [chain.finish([*token, outer, edge]) for chain in follow]
        [chain.start_two() for chain in follow]
        pieces = [chain.parts for chain in leads]
        pieces[0][0] = after(pieces[0][0], *token)
        lead_places = [piece_places(rounds) for rounds in lead_rounds]
    else:
        full = gathered(lead, order, count, me)
        pieces = [
            [jnp.concatenate([full[:, : cut // 2], full[:, cut:]], axis=1)[None]],
            [full[None, :, cut // 2 : cut]],
        ]
        lead_places = [[[0]], [[0]]]
    queries, keys, values, attended, stats, weight_full, reach, vectors = attention_forward(
        lengths, first, me_head, rows_of, pieces, side, lead_places
    )
    if slotted:
        [chain.finish_two([attended]) for chain in follow]
        follow_parts = [chain.parts for chain in follow]
        follow_places = [piece_places(rounds) for rounds in follow_rounds]
    else:
        follow_parts = [
            [gathered(mixed, order, count, me)[None]],
            [gathered(downward_weight, order, count, me)[None]],
        ]
        follow_places = [[[0]], [[0]]]
    bias_upward = (
        vectors[8 : 8 + extra].reshape(extra, count, shard).transpose(1, 0, 2).reshape(1, -1)
    )

    outs = feed_forward(
        me_of,
        attended,
        states,
        cotangent,
        vectors,
        bias_upward,
        *follow_parts,
        follow_places,
        back_bits[:2],
    )
    result, grad_residual, grad_attended, small_sums = outs[:4]
    gradients = outs[4:]
    sums = jnp.concatenate(
        [
            small_sums[:6],
            small_sums[8 : 8 + extra].reshape(count, extra, shard).transpose(1, 0, 2).reshape(extra, width),
        ]
    )
    if slotted:
        group = [
            Gathering(*pair, rounds, count)
            for pair, rounds in zip((gradients[:2], gradients[2:]), back_rounds)
        ]
        token = [x for chain in group for x in chain.advance()]
        grad_attended = after(grad_attended, *token)

    grad_query, grad_key, grad_value, *slots = attention_backward(
        lengths,
        first,
        me_of,
        queries,
        keys,
        values,
        grad_attended,
        stats,
        reach,
        side,
        shard,
        2 if slotted else 1,
        back_bits[2:],
        sums,
    )

    step = lambda chains, token: [x for chain in chains for x in chain.advance(token)]
    if slotted:
        arrived = [x for chain in group for x in chain.arrive()]
        grad_query, grad_key, grad_value, *slots = tied(
            (grad_query, grad_key, grad_value, *slots), arrived
        )
        token = step(group, [grad_query])
        halves = [
            Gathering(*pair, rounds, count)
            for pair, rounds in zip((slots[:2], slots[2:]), back_rounds[2:])
        ]
        (grad_key,) = tied([grad_key], token)

    def input_rows(select):
        return sum(
            jnp.einsum(
                "rc,dc->rd",
                select(grad),
                weight_full[:, n * width : (n + 1) * width],
                preferred_element_type=f32,
            )
            for n, grad in ((1, grad_key), (2, grad_value))
        )

    grad_outer = input_rows(lambda g: jnp.where(is_first, g[:side], g[side + rows :]))
    grad_outer = grad_outer.astype(bf16)
    back = along(grad_outer, -1, 1)
    if slotted:
        token = step(halves, [grad_outer])
        (grad_key,) = tied([grad_key], token)
    grad_rest = input_rows(
        lambda g: jnp.where(
            is_first, g[side + rows :], jnp.concatenate([g[thin:side], g[:thin]], axis=0)
        )
    )
    back_edge = along(grad_rest[rows:].astype(bf16), 1, -1)
    if slotted:
        token = step(group, [grad_rest])
        (back,) = tied([back], token)
    back_own = jnp.where(is_first, back[:thin], back[rows:]).astype(f32)
    back_partner = jnp.where(is_first, back[thin:], back[:rows])
    grad_near = (grad_rest[:rows] + back_partner.astype(f32)).astype(bf16)
    back_near = swap(grad_near, blocks_axis, count)
    if slotted:
        (grad_key, grad_query, result) = tied([grad_key, grad_query, result], [grad_near])
    middle = (
        input_rows(lambda g: g[side : side + rows])
        + jnp.einsum("rc,dc->rd", grad_query, weight_full[:, :width], preferred_element_type=f32)
        + grad_residual
    )
    if slotted:
        token = step(halves, [middle])
        (result,) = tied([result], token)
    layer_output = jnp.take(result, slot_index, axis=0)
    if slotted:
        token = step(group, [layer_output])
        token = step(halves, token)
        (back_near,) = tied([back_near], token)
    pad_low = lambda v: jnp.pad(v, ((0, rows - thin), (0, 0)))
    pad_high = lambda v: jnp.pad(v, ((rows - thin, 0), (0, 0)))
    back_edge = back_edge.astype(f32)
    grad_input = (
        middle
        + back_near.astype(f32)
        + jnp.where(
            is_first, pad_high(back_own) + pad_low(back_edge), pad_low(back_own) + pad_high(back_edge)
        )
    )
    grad_hidden = jnp.take(grad_input, slot_index, axis=0)

    if slotted:
        step(halves, [grad_hidden])
        out_mixed, out_downward, out_a, out_b = (c.total for c in (*group, *halves))
    else:
        by_device = lambda grad: grad.reshape((count, grad.size // grad.shape[-1] // count, -1))
        out_mixed = reduced(by_device(gradients[0]), order, count, me)
        out_downward = reduced(by_device(gradients[1]), order, count, me)
        out_a = reduced(by_device(slots[0]), order, count, me)
        out_b = reduced(by_device(slots[1]), order, count, me)
    out_triple = jnp.concatenate(
        [o[:, n * half : (n + 1) * half] for n in range(3) for o in (out_a, out_b)], axis=1
    )
    summed = out_b[:, 3 * half :].T
    (
        out_query,
        out_value,
        out_output,
        out_down_bias,
        out_gain_one,
        out_shift_one,
        out_gain_two,
        out_shift_two,
    ) = [summed[i] for i in range(8)]
    out_up_bias = summed[8 : 8 + extra].reshape(-1)
    return (
        layer_output,
        grad_hidden,
        out_triple,
        out_mixed[:, :width],
        out_mixed[:, width:],
        out_downward,
        out_query,
        out_value,
        out_output,
        out_up_bias,
        out_down_bias,
        out_gain_one,
        out_shift_one,
        out_gain_two,
        out_shift_two,
    )


def solution(mesh):
    matrix, vector = P(AXES, None), P(AXES)
    return jax.shard_map(
        local,
        mesh=mesh,
        in_specs=(matrix, vector, P(), *[matrix] * 4, *[vector] * 9, matrix),
        out_specs=(*[matrix] * 6, *[vector] * 9),
        check_vma=False,
    )
```

```python
import functools

import jax
import jax.numpy as jnp
import numpy as np
from jax import lax
from jax.experimental import pallas as pl
from jax.experimental.pallas import tpu as pltpu
from jax.sharding import PartitionSpec as P

DH = 64
SEG_TOK = 502
MEMR = 10
SEG_ROWS = SEG_TOK + 2 * MEMR
AXES = ("head", "blk")
TILE = 128
PAIR = 2 * DH
AT_ONCE = 3
WIDE = AT_ONCE * PAIR
WINDOW = 544

norm_eps = 1e-12
masked_score = -1e30
score_scale = 0.125
root_half = 0.7071067811865476
inverse_root_two_pi = 0.3989422804014327
f32 = jnp.float32
bf16 = jnp.bfloat16


def swap(block, bit, count):
    return lax.ppermute(block, AXES, [(i, i ^ bit) for i in range(count)])


def tied(values, others):
    values = tuple(values)
    return list(lax.optimization_barrier((*values, *others))[: len(values)])


def after(value, *others):
    return tied([value], others)[0]


def relative(bits):
    return [sum(bit for at, bit in enumerate(bits) if j >> at & 1) for j in range(1 << len(bits))]


def gathered(shard, order, count, me):
    held, have = shard, []
    for bit in order:
        axis = sum(b > bit for b in have)
        have.append(bit)
        other = jnp.expand_dims(swap(held, bit, count), axis)
        own = jnp.expand_dims(held, axis)
        held = jnp.where(
            (me & bit) == 0,
            jnp.concatenate([own, other], axis=axis),
            jnp.concatenate([other, own], axis=axis),
        )
    return held.reshape((count * shard.shape[0],) + shard.shape[1:])


def reduced(blocks, order, count, me):
    have = sorted(order, reverse=True)
    held = blocks.reshape((2,) * len(have) + blocks.shape[1:])
    for step, bit in enumerate(order):
        axis = have.index(bit)
        have.remove(bit)
        mine = ((me & bit) != 0).astype(jnp.int32)
        keep = lax.dynamic_index_in_dim(held, mine, axis, keepdims=False)
        send = lax.dynamic_index_in_dim(held, 1 - mine, axis, keepdims=False)
        total = keep.astype(f32) + swap(send, bit, count).astype(f32)
        held = total if not have else total.astype(blocks.dtype)
    return held


class Spread:
    def __init__(self, held, rounds, count):
        self.held, self.rounds, self.count = held, list(rounds), count
        self.parts = None

    def start(self):
        self.recvs = [swap(self.held, c, self.count) for c in relative(self.rounds[0])[1:]]

    def finish(self, token=()):
        recvs = tied(self.recvs, token) if token else self.recvs
        self.held = jnp.concatenate([self.held, *recvs], axis=0)
        self.rounds.pop(0)
        return self.held

    def start_two(self):
        self.start()
        (self.last,) = self.rounds[1]
        self.own = swap(self.held, self.last, self.count)

    def finish_two(self, token=()):
        recvs = tied(self.recvs, token) if token else self.recvs
        self.parts = [self.held, *recvs, self.own, *[swap(r, self.last, self.count) for r in recvs]]
        return recvs


def piece_places(rounds, apart=2):
    pieces = [relative([b for r in rounds[: len(rounds) - apart] for b in r])]
    for bits in rounds[len(rounds) - apart :]:
        pieces = [[j + c for j in piece] for c in relative(bits) for piece in pieces]
    return pieces


class Gathering:
    def __init__(self, keep, send, cut, rounds, count):
        self.rounds, self.count, self.cut, self.at = rounds, count, cut, 0
        self.keep = keep
        self.recvs = [swap(send, self.rounds[0][0][0], count)]
        self.total = None

    def arrive(self, token=()):
        self.recvs = tied(self.recvs, token) if token else self.recvs
        return self.recvs

    def advance(self, token=()):
        recvs = self.arrive(token)
        add = lambda terms, at: sum(t[at].astype(f32) for t in terms)
        joined = lambda at: jnp.concatenate([add(terms, at) for terms in self.terms], axis=-1)
        self.at += 1
        if self.at == 1:
            terms = [self.keep, *recvs]
            self.terms = [[t[..., : self.cut] for t in terms], [t[..., self.cut :] for t in terms]]
        elif self.at in (2, 3):
            for terms, recv in zip(self.terms, recvs):
                terms.append(recv)
        else:
            self.total = joined(0) + sum(r[0].astype(f32) for r in recvs)
            return [self.total]
        if self.at < 3:
            half = self.terms[0][0].shape[0] // 2
            sends = [add(terms, slice(half, None)).astype(bf16) for terms in self.terms]
            bits = [rounds[self.at][0] for rounds in self.rounds]
            self.recvs = [swap(s, b, self.count) for s, b in zip(sends, bits)]
        else:
            combos = relative(self.rounds[0][3][::-1])
            half = 1
            sends = [joined(slice(j, j + 1)).astype(bf16) for j in range(1, len(combos))]
            self.recvs = [swap(s, c, self.count) for s, c in zip(sends, combos[1:])]
            half = 1
        self.terms = [[t[:half] for t in terms] for terms in self.terms]
        return sends


class Direct:
    def __init__(self, keep, send, rounds, count):
        self.rounds, self.count, self.terms, self.total = list(rounds[1:]), count, [keep], None
        self.recvs = [swap(send, rounds[0][0], count)]

    def advance(self, token=()):
        self.terms += tied(self.recvs, token) if token else self.recvs
        add = lambda at: sum(t[at].astype(f32) for t in self.terms)
        if not self.rounds:
            self.total = add(0)
            return [self.total]
        combos = relative(self.rounds.pop(0)[::-1])
        each = self.terms[0].shape[0] // len(combos)
        sends = [add(slice(j * each, (j + 1) * each)).astype(bf16) for j in range(1, len(combos))]
        self.terms = [t[:each] for t in self.terms]
        self.recvs = [swap(x, c, self.count) for x, c in zip(sends, combos[1:])]
        return sends


def segment_at(lengths_ref, sequences, position):
    start = jnp.int32(0)
    low = jnp.int32(0)
    high = jnp.int32(0)
    for i in range(sequences):
        tokens = lengths_ref[i]
        end = start + tokens + 2 * MEMR * lax.div(tokens + (SEG_TOK - 1), jnp.int32(SEG_TOK))
        inside = (position >= start) & (position < end)
        first = start + lax.div(position - start, jnp.int32(SEG_ROWS)) * SEG_ROWS
        low = jnp.where(inside, first, low)
        high = jnp.where(inside, jnp.minimum(first + SEG_ROWS, end), high)
        start = end
    return low, high


def over_segments(lengths_ref, sequences, first_row, rows, side, body):
    def step(position):
        low, high = segment_at(lengths_ref, sequences, position)
        high = jnp.maximum(high, position + 1)
        low_at = low - first_row + side
        high_at = high - first_row + side
        window = jnp.minimum(lax.div(low_at, jnp.int32(16)) * 16, rows + 2 * side - WINDOW)
        window = pl.multiple_of(jnp.maximum(window, 0), 16)
        tile_from = lax.div(jnp.maximum(low - first_row, 0), jnp.int32(TILE))
        tile_to = lax.div(jnp.minimum(high - first_row, rows) + TILE - 1, jnp.int32(TILE))
        body(low_at, high_at, window, tile_from, tile_to)
        return high

    lax.while_loop(lambda position: position < first_row + rows, step, first_row)


def two_heads(block):
    lane = lax.broadcasted_iota(jnp.int32, block.shape, 1)
    zero = jnp.zeros_like(block)
    return jnp.concatenate(
        [jnp.where(lane < DH, block, zero), jnp.where(lane < DH, zero, block)], axis=0
    )


def own_blocks(product):
    return jnp.concatenate([product[:DH, :TILE], product[DH:, TILE:]], axis=0).T


def key_bias(low_at, high_at, window):
    row = lax.broadcasted_iota(jnp.int32, (WINDOW, 2 * TILE), 0) + window
    return jnp.where((row >= low_at) & (row < high_at), 0.0, masked_score)


def rows_inside(tile, low_at, high_at, side, shape, dim):
    at = lax.broadcasted_iota(jnp.int32, shape, dim)
    if dim == 1:
        at = at & (TILE - 1)
    at = at + (tile * TILE + side)
    return (at >= low_at) & (at < high_at)


NT = (((1,), (1,)), ((), ()))
NN = (((1,), (0,)), ((), ()))


def mul(left, right, dims=NN):
    return lax.dot_general(left, right, dims, preferred_element_type=f32)


def slots_to_rows(slots, shard, store):
    total, _, columns = slots.shape
    step = min(total, 8)
    for d in range(0, total, step):
        block = slots[d : d + step].astype(f32).reshape(step * shard, columns)
        store(slice(d * shard, (d + step) * shard), block.astype(bf16))


def forward_kernel(plan, lengths_ref, first_ref, me_ref, *refs):
    sequences, side, taken, dests, shard = plan
    outer_ref, states_ref, partner_ref, edge_ref = refs[:4]
    pieces, refs = refs[4 : 4 + taken], refs[4 + taken :]
    (q_ref, k_ref, v_ref, o_ref, stat_ref, weight_ref, reach_ref, vec_ref) = refs[:8]
    bias_ref, vt_ref, slots_ref, small_ref, in_sem = refs[8:]
    rows, width = states_ref.shape
    thin = edge_ref.shape[0]
    pair = pl.program_id(0)
    me, head = me_ref[0], me_ref[1]

    @pl.when(pair == 0)
    def _():
        slots = len(dests[0])
        copies = [
            pltpu.make_async_copy(
                pieces[a].at[j], slots_ref.at[dests[a][j] ^ me], in_sem.at[a * slots + j]
            )
            for a in range(taken)
            for j in range(slots)
        ]
        for copy in copies:
            copy.start()

        @pl.when(head == 0)
        def _():
            reach_ref[:side, :] = outer_ref[...]
            reach_ref[side + rows : side + 2 * rows, :] = partner_ref[...]
            reach_ref[side + 2 * rows :, :] = edge_ref[...]

        @pl.when(head != 0)
        def _():
            reach_ref[:thin, :] = edge_ref[...]
            reach_ref[thin:side, :] = partner_ref[...]
            reach_ref[side + rows :, :] = outer_ref[...]

        reach_ref[side : side + rows, :] = states_ref[...]
        for copy in copies:
            copy.wait()

        def store(at, block):
            weight_ref[at, :] = block[:, : 3 * width]
            small_ref[at, :] = block[:, 3 * width :]

        slots_to_rows(slots_ref, shard, store)
        vec_ref[...] = small_ref[...].astype(f32).T[: vec_ref.shape[0]]

    stat_ref[...] = jnp.zeros_like(stat_ref)
    o_ref[...] = jnp.zeros_like(o_ref)
    lanes = [pl.ds(pl.multiple_of(pair * WIDE + n * width, PAIR), WIDE) for n in range(3)]
    queries = mul(states_ref[...], weight_ref[:, lanes[0]]) + vec_ref[0:1, lanes[0]]
    q_ref[...] = queries.astype(bf16) * jnp.asarray(score_scale, bf16)
    k_ref[...] = mul(reach_ref[...], weight_ref[:, lanes[1]]).astype(bf16)
    values = mul(reach_ref[...], weight_ref[:, lanes[2]]) + vec_ref[1:2, lanes[0]]
    v_ref[...] = values.astype(bf16)
    subs = [(n, slice(n * PAIR, (n + 1) * PAIR)) for n in range(AT_ONCE)]

    def segment(low_at, high_at, window, tile_from, tile_to):
        bias_ref[...] = key_bias(low_at, high_at, window)
        keys_at = pl.ds(window, WINDOW)
        for n, part in subs:
            vt_ref[n] = v_ref[keys_at, part].T

        def one(tile, carry):
            at = pl.ds(pl.multiple_of(tile * TILE, TILE), TILE)
            wide = pl.ds(pl.multiple_of(tile * 2 * TILE, 2 * TILE), 2 * TILE)
            inside = rows_inside(tile, low_at, high_at, side, (TILE, PAIR), 0)
            there = rows_inside(tile, low_at, high_at, side, (1, 2 * TILE), 1)
            scores = [
                mul(k_ref[keys_at, part], two_heads(q_ref[at, part]), NT) + bias_ref[...]
                for _, part in subs
            ]
            for (n, part), score in zip(subs, scores):
                top = jnp.max(score, axis=0, keepdims=True)
                raised = jnp.exp(score - top)
                total = jnp.sum(raised, axis=0, keepdims=True)
                mixed = mul(vt_ref[n], raised.astype(bf16)) * (1.0 / total)
                mixed = own_blocks(mixed).astype(bf16)
                o_ref[at, part] = jnp.where(inside, mixed, o_ref[at, part])
                level = top + jnp.log(total)
                stat_ref[n, 0:1, wide] = jnp.where(there, level, stat_ref[n, 0:1, wide])
            return carry

        lax.fori_loop(tile_from, tile_to, one, 0)

    over_segments(lengths_ref, sequences, first_ref[0], rows, side, segment)


def backward_kernel(
    plan,
    lengths_ref,
    first_ref,
    me_ref,
    q_ref,
    k_ref,
    v_ref,
    g_ref,
    stat_ref,
    reach_ref,
    *refs,
):
    sequences, side, held, slot_of, shard = plan
    sums_in, dq_ref, dk_ref, dv_ref = refs[:4]
    outs = refs[4 : 4 + held]
    (bias_ref, kt_ref, dq_acc, dk_acc, dv_acc, reach_t, slots_ref, small_ref, sem) = refs[4 + held :]
    rows = q_ref.shape[0]
    pair, pairs = pl.program_id(0), pl.num_programs(0)
    me = me_ref[0]
    total, width = slots_ref.shape[0], reach_ref.shape[1]

    @pl.when(pair == 0)
    def _():
        reach_t[...] = reach_ref[...].T
        small_ref[...] = jnp.zeros_like(small_ref)

    dq_acc[...] = jnp.zeros_like(dq_acc)
    dk_acc[...] = jnp.zeros_like(dk_acc)
    dv_acc[...] = jnp.zeros_like(dv_acc)

    subs = [(n, slice(n * PAIR, (n + 1) * PAIR)) for n in range(AT_ONCE)]

    def segment(low_at, high_at, window, tile_from, tile_to):
        bias_ref[...] = key_bias(low_at, high_at, window)
        keys_at = pl.ds(window, WINDOW)
        for n, part in subs:
            kt_ref[n] = k_ref[keys_at, part].T

        def one(tile, carry):
            at = pl.ds(pl.multiple_of(tile * TILE, TILE), TILE)
            wide = pl.ds(pl.multiple_of(tile * 2 * TILE, 2 * TILE), 2 * TILE)
            there = rows_inside(tile, low_at, high_at, side, (1, 2 * TILE), 1)
            queries = [two_heads(q_ref[at, part]) for _, part in subs]
            grads = [two_heads(g_ref[at, part]) for _, part in subs]
            scores = [
                mul(k_ref[keys_at, part], query, NT) + bias_ref[...]
                for (_, part), query in zip(subs, queries)
            ]
            grad_probs = [mul(v_ref[keys_at, part], g, NT) for (_, part), g in zip(subs, grads)]
            for n, part in subs:
                level = jnp.where(there, stat_ref[n, 0:1, wide], -masked_score)
                probs = jnp.exp(scores[n] - level)
                shared = jnp.sum(probs * grad_probs[n], axis=0, keepdims=True)
                grad_scores = (probs * (grad_probs[n] - shared)).astype(bf16)
                dv_acc[keys_at, part] += mul(probs.astype(bf16), grads[n])
                dk_acc[keys_at, part] += mul(grad_scores, queries[n])
                dq_acc[at, part] += own_blocks(mul(kt_ref[n], grad_scores))
            return carry

        lax.fori_loop(tile_from, tile_to, one, 0)

    over_segments(lengths_ref, sequences, first_ref[0], rows, side, segment)
    dq = (dq_acc[...] * score_scale).astype(bf16)
    dk, dv = dk_acc[...].astype(bf16), dv_acc[...].astype(bf16)
    dq_ref[...] = dq
    dk_ref[...] = dk
    dv_ref[...] = dv
    lanes = [pl.ds(pl.multiple_of(pair * WIDE + n * width, PAIR), WIDE) for n in range(3)]
    small_ref[0:1, lanes[0]] = jnp.sum(dq.astype(f32), axis=0, keepdims=True)
    small_ref[1:2, lanes[0]] = jnp.sum(dv.astype(f32), axis=0, keepdims=True)

    def put(value, columns):
        for i in range(total):
            slot = slot_of(i ^ me) if total > 1 else 0
            slots_ref[slot, :, columns] = value[i * shard : (i + 1) * shard].astype(bf16)

    own_t = reach_ref[side : side + rows, :]
    put(mul(own_t, dq, (((0,), (0,)), ((), ()))), lanes[0])
    put(mul(reach_t[...], dk), lanes[1])
    put(mul(reach_t[...], dv), lanes[2])
    each = total // held
    copies = [
        pltpu.make_async_copy(slots_ref.at[pl.ds(a * each, each)], outs[a], sem.at[a])
        for a in range(held)
    ]

    @pl.when(pair == pairs - 1)
    def _():
        count = sums_in.shape[0]
        small_ref[2 : 2 + count, :] = sums_in[...]
        put(small_ref[...].T, pl.ds(3 * width, TILE))
        for copy in copies:
            copy.start()
        for copy in copies:
            copy.wait()


def pack_kernel(shard, weight_ref, *refs):
    *rest_refs, lead_ref, rest_ref, rows_ref = refs
    (output_ref, upward_ref, downward_ref), vector_refs = rest_refs[:3], rest_refs[3:]
    rows_ref[...] = jnp.zeros_like(rows_ref)
    row = 0
    for ref in vector_refs:
        values = ref[...].astype(f32).reshape(1, ref.shape[0])
        for at in range(0, ref.shape[0], shard):
            rows_ref[row : row + 1, :shard] = values[:, at : at + shard]
            row += 1
    width = output_ref.shape[1]
    lead_ref[:, : 3 * width] = weight_ref[...]
    lead_ref[:, 3 * width :] = rows_ref[...].T[:shard].astype(bf16)
    hidden = upward_ref.shape[1]
    rest_ref[:, :width] = output_ref[...]
    rest_ref[:, width : width + hidden] = upward_ref[...]
    down = downward_ref[...].astype(f32)
    for k in range(down.shape[0] // shard):
        at = width + hidden + k * width
        rest_ref[:, at : at + width] = down[k * shard : (k + 1) * shard].astype(bf16)


def pack(weight, output, upward, downward, vectors):
    shard = weight.shape[0]
    shape = jax.ShapeDtypeStruct
    return pl.pallas_call(
        functools.partial(pack_kernel, shard),
        name="pack",
        out_shape=(
            shape((shard, weight.shape[1] + 128), bf16),
            shape((shard, output.shape[1] + 2 * upward.shape[1]), bf16),
        ),
        in_specs=[pl.BlockSpec(memory_space=pltpu.VMEM)] * (4 + len(vectors)),
        out_specs=[pl.BlockSpec(memory_space=pltpu.VMEM)] * 2,
        scratch_shapes=[pltpu.VMEM((128, 128), f32)],
    )(weight, output, upward, downward, *vectors)


def attention_forward(lengths, first, me_head, rows_of, pieces, side, dests):
    outer, states, partner, edge = rows_of
    rows, features = states.shape
    wide = rows + 2 * side
    taken, (slots, shard, columns) = len(pieces), pieces[0].shape
    pairs = features // PAIR
    whole = lambda *shape: pl.BlockSpec(shape, lambda h, *_: (0,) * len(shape))
    column = lambda n: pl.BlockSpec((n, WIDE), lambda h, *_: (0, h))
    anywhere = pl.BlockSpec(memory_space=pl.ANY)
    shape = jax.ShapeDtypeStruct
    plan = (lengths.shape[0], side, taken, dests, shard)
    return pl.pallas_call(
        functools.partial(forward_kernel, plan),
        name="attention_forward",
        out_shape=(
            shape((rows, features), bf16),
            shape((wide, features), bf16),
            shape((wide, features), bf16),
            shape((rows, features), bf16),
            shape((pairs, 8, 2 * rows), f32),
            shape((features, 3 * features), bf16),
            shape((wide, features), bf16),
            shape((16, features), f32),
        ),
        grid_spec=pltpu.PrefetchScalarGridSpec(
            num_scalar_prefetch=3,
            grid=(pairs // AT_ONCE,),
            in_specs=[*[whole(*r.shape) for r in rows_of], *[anywhere] * taken],
            out_specs=[
                column(rows),
                column(wide),
                column(wide),
                column(rows),
                pl.BlockSpec((AT_ONCE, 8, 2 * rows), lambda h, *_: (h, 0, 0)),
                whole(features, 3 * features),
                whole(wide, features),
                whole(16, features),
            ],
            scratch_shapes=[
                pltpu.VMEM((WINDOW, 2 * TILE), f32),
                pltpu.VMEM((AT_ONCE, PAIR, WINDOW), bf16),
                pltpu.VMEM((taken * slots, shard, columns), bf16),
                pltpu.VMEM((features, columns - 3 * features), bf16),
                pltpu.SemaphoreType.DMA((taken * slots,)),
            ],
        ),
        compiler_params=pltpu.CompilerParams(vmem_limit_bytes=48 * 2**20),
    )(lengths, first, me_head, *rows_of, *pieces)


def attention_backward(
    lengths, first, me, queries, keys, values, grads, stats, reach, side, shard, held, bits, sums
):
    rows, features = queries.shape
    wide = keys.shape[0]
    pairs = features // PAIR
    total = features // shard if held > 1 else 1
    per = shard if held > 1 else features
    columns = 3 * features + TILE
    column = lambda n: pl.BlockSpec((n, WIDE), lambda h, *_: (0, h))
    whole = lambda *shape: pl.BlockSpec(shape, lambda h, *_: (0,) * len(shape))
    anywhere = pl.BlockSpec(memory_space=pl.ANY)
    shape = jax.ShapeDtypeStruct
    place = exchange_slot(bits)
    return pl.pallas_call(
        functools.partial(backward_kernel, (lengths.shape[0], side, held, place, per)),
        name="attention_backward",
        out_shape=(
            shape((rows, features), bf16),
            shape((wide, features), bf16),
            shape((wide, features), bf16),
            *[shape((total // held, per, columns), bf16)] * held,
        ),
        grid_spec=pltpu.PrefetchScalarGridSpec(
            num_scalar_prefetch=3,
            grid=(pairs // AT_ONCE,),
            in_specs=[
                column(rows),
                column(wide),
                column(wide),
                column(rows),
                pl.BlockSpec((AT_ONCE, 8, 2 * rows), lambda h, *_: (h, 0, 0)),
                whole(wide, features),
                whole(*sums.shape),
            ],
            out_specs=[column(rows), column(wide), column(wide), *[anywhere] * held],
            scratch_shapes=[
                pltpu.VMEM((WINDOW, 2 * TILE), f32),
                pltpu.VMEM((AT_ONCE, PAIR, WINDOW), bf16),
                pltpu.VMEM((rows, WIDE), f32),
                pltpu.VMEM((wide, WIDE), f32),
                pltpu.VMEM((wide, WIDE), f32),
                pltpu.VMEM((features, wide), bf16),
                pltpu.VMEM((total, per, columns), bf16),
                pltpu.VMEM((TILE, features), f32),
                pltpu.SemaphoreType.DMA((held,)),
            ],
        ),
        compiler_params=pltpu.CompilerParams(vmem_limit_bytes=56 * 2**20),
    )(lengths, first, me, queries, keys, values, grads, stats, reach, sums)


TN = (((0,), (0,)), ((), ()))


def row_mean(value):
    return jnp.mean(value, axis=-1, keepdims=True)


def column_sum(value):
    return jnp.sum(value, axis=0, keepdims=True)


def normalize(summed):
    centered = summed - row_mean(summed)
    inverse_std = lax.rsqrt(row_mean(centered * centered) + norm_eps)
    return centered * inverse_std, inverse_std


def normalize_back(grad, normed, inverse_std):
    return inverse_std * (grad - row_mean(grad) - normed * row_mean(grad * normed))


def feed_kernel(plan, *refs):
    taken, held, in_dest, out_slot, shard = plan
    me_ref, att_ref, states_ref, cot_ref, vec_ref, upb_ref = refs[:6]
    mixed_in, down_in = refs[6 : 6 + taken], refs[6 + taken : 6 + 2 * taken]
    at = 6 + 2 * taken
    result_ref, res_ref, gatt_ref, small_ref = refs[at : at + 4]
    outs, refs = refs[at + 4 : at + 4 + held], refs[at + 4 + held :]
    (wslot, dslot, wmix, wdown, act, slope, gall, acc, in_sem, out_sem) = refs
    me = me_ref[0]
    width = states_ref.shape[1]
    hidden = wdown.shape[0]
    slots = len(in_dest[0][0])

    def copies_of(which, pieces, target):
        return [
            pltpu.make_async_copy(
                pieces[a].at[j],
                target.at[in_dest[which][a][j] ^ me],
                in_sem.at[which, a * slots + j],
            )
            for a in range(taken)
            for j in range(slots)
        ]

    copies_in = lambda: copies_of(0, mixed_in, wslot)
    copies_down = lambda: copies_of(1, down_in, dslot)
    for copy in copies_in():
        copy.start()
    for copy in copies_down():
        copy.start()
    for copy in copies_in():
        copy.wait()
    total = taken * slots

    def store(at, block):
        wmix[at, :] = block

    slots_to_rows(wslot, shard, store)

    bias_out, bias_down, gain_one, shift_one, gain_two, shift_two = (
        vec_ref[i : i + 1, :] for i in range(2, 8)
    )
    branch = mul(att_ref[...], wmix[:, :width]) + bias_out
    normed_one, scale_one = normalize(states_ref[...].astype(f32) + branch)
    first_norm = normed_one * gain_one + shift_one
    inner = first_norm.astype(bf16)
    for copy in copies_down():
        copy.wait()
    extra = hidden // width
    deep = extra * shard
    for d in range(total):
        block = dslot[d].astype(f32)
        block = [block[:, k * width : (k + 1) * width] for k in range(extra)]
        wdown[d * deep : (d + 1) * deep, :] = jnp.concatenate(block, axis=0).astype(bf16)
    chunks = range(0, hidden, width)
    for c in chunks:
        lifted = mul(inner, wmix[:, width + c : 2 * width + c]) + upb_ref[:, c : c + width]
        phi_sum = 0.5 * (1.0 + lax.erf(lifted * root_half))
        active = (lifted * phi_sum).astype(bf16)
        act[:, c : c + width] = active
        slope[:, c : c + width] = phi_sum + lifted * (
            inverse_root_two_pi * jnp.exp(-0.5 * lifted * lifted)
        )
        part = mul(active, wdown[c : c + width, :])
        acc[...] = part if c == 0 else acc[...] + part
    normed_two, scale_two = normalize(first_norm + (acc[...] + bias_down))
    result_ref[...] = (normed_two * gain_two + shift_two).astype(bf16)

    cot = cot_ref[...].astype(f32)
    small_ref[4:5, :] = column_sum(cot * normed_two)
    small_ref[5:6, :] = column_sum(cot)
    grad_mid = normalize_back(cot * gain_two, normed_two, scale_two)
    grad_down = grad_mid.astype(bf16)
    small_ref[1:2, :] = column_sum(grad_down.astype(f32))

    def put(order, value, first, per, columns):
        for i in range(value.shape[0] // per):
            slot = out_slot(order, (first + i) ^ me)
            for k in range(per // shard):
                at = i * per + k * shard
                lanes = slice(columns + k * width, columns + (k + 1) * width)
                gall[slot, :, lanes] = value[at : at + shard].astype(bf16)

    copies_out = [
        pltpu.make_async_copy(
            gall.at[pl.ds(a * (total // held), total // held)], outs[a], out_sem.at[a]
        )
        for a in range(held)
    ]
    inner_t = inner.T
    for c in chunks:
        active = act[:, c : c + width]
        grad_active = mul(grad_down, wdown[c : c + width, :], NT)
        grad_lift = (grad_active * slope[:, c : c + width]).astype(bf16)
        small_ref[8 + c // width : 9 + c // width, :] = column_sum(grad_lift.astype(f32))
        grad_w = mul(active, grad_down, TN)
        if total > 1:
            put(1, grad_w, c // deep, deep, width + hidden)
        else:
            gall[0, :, width + hidden + c : 2 * width + hidden + c] = grad_w.astype(bf16)
        put(0, mul(inner_t, grad_lift), 0, shard, width + c)
        part = mul(grad_lift, wmix[:, width + c : 2 * width + c], NT)
        acc[...] = part if c == 0 else acc[...] + part
    grad_first = acc[...] + grad_mid
    small_ref[2:3, :] = column_sum(grad_first * normed_one)
    small_ref[3:4, :] = column_sum(grad_first)
    grad_residual = normalize_back(grad_first * gain_one, normed_one, scale_one)
    res_ref[...] = grad_residual
    grad_branch = grad_residual.astype(bf16)
    small_ref[0:1, :] = column_sum(grad_branch.astype(f32))
    put(0, mul(att_ref[...], grad_branch, TN), 0, shard, 0)
    for copy in copies_out:
        copy.start()
    gatt_ref[...] = mul(grad_branch, wmix[:, :width], NT).astype(bf16)
    small_ref[6:8, :] = jnp.zeros((2, width), f32)
    small_ref[12:, :] = jnp.zeros((small_ref.shape[0] - 12, width), f32)
    for copy in copies_out:
        copy.wait()


def exchange_slot(bits):
    def slot(diff):
        found = jnp.int32(0)
        for at, bit in enumerate(reversed(bits)):
            found = found + (((diff & bit) != 0).astype(jnp.int32) << at)
        return found

    return slot


def feed_forward(me, attended, states, cotangent, vectors, up_bias, mixed, down, dests, backs):
    rows, width = states.shape
    taken, (slots, shard, columns) = len(mixed), mixed[0].shape
    held = min(taken, 2)
    total = taken * slots
    hidden = down[0].shape[2]
    slot_of = [exchange_slot(back) for back in backs]
    place = lambda order, diff: slot_of[order](diff) if held > 1 else 0
    plan = (taken, held, dests, place, shard)
    whole = pl.BlockSpec(memory_space=pltpu.VMEM)
    anywhere = pl.BlockSpec(memory_space=pl.ANY)
    shape = jax.ShapeDtypeStruct
    return pl.pallas_call(
        functools.partial(feed_kernel, plan),
        name="feed_forward",
        out_shape=(
            shape((rows, width), bf16),
            shape((rows, width), f32),
            shape((rows, width), bf16),
            shape((16, width), f32),
            *[shape((total // held, shard, columns + hidden), bf16)] * held,
        ),
        in_specs=[pl.BlockSpec(memory_space=pltpu.SMEM), *[whole] * 5, *[anywhere] * (2 * taken)],
        out_specs=[*[whole] * 4, *[anywhere] * held],
        scratch_shapes=[
            pltpu.VMEM((total, shard, columns), bf16),
            pltpu.VMEM((total, shard, hidden), bf16),
            pltpu.VMEM((total * shard, columns), bf16),
            pltpu.VMEM((hidden, width), bf16),
            pltpu.VMEM((rows, hidden), bf16),
            pltpu.VMEM((rows, hidden), f32),
            pltpu.VMEM((total, shard, columns + hidden), bf16),
            pltpu.VMEM((rows, width), f32),
            pltpu.SemaphoreType.DMA((2, total)),
            pltpu.SemaphoreType.DMA((held,)),
        ],
        compiler_params=pltpu.CompilerParams(vmem_limit_bytes=60 * 2**20),
    )(me, attended, states, cotangent, vectors, up_bias, *mixed, *down)


def local(
    hidden_states,
    owner_rows,
    lengths,
    attention_weight,
    output_weight,
    upward_weight,
    downward_weight,
    query_bias,
    value_bias,
    output_bias,
    upward_bias,
    downward_bias,
    first_gain,
    first_shift,
    second_gain,
    second_shift,
    output_cotangent,
):
    rows, width = hidden_states.shape
    heads_axis, blocks_axis = lax.axis_size("head"), lax.axis_size("blk")
    count = heads_axis * blocks_axis
    me = lax.axis_index(AXES)
    head, blk = lax.axis_index("head"), lax.axis_index("blk")
    first = ((blk * heads_axis + head) * rows).astype(jnp.int32).reshape(1)
    bits = [1 << b for b in range((count - 1).bit_length())]
    far = tuple(b for b in bits if b not in (1, 2, blocks_axis))[::-1]
    near_y, near_x, core = (2,), (blocks_axis,), (1,)
    follow_rounds = ([far, near_y, near_x, core], [far, near_x, near_y, core])
    back_rounds = (
        [core, near_y, near_x, far[::-1]],
        [core, near_x, near_y, far[::-1]],
        [core, (*near_x, *near_y), far[::-1]],
    )
    back_bits = [[b for r in rounds for b in r] for rounds in back_rounds]
    order = bits[::-1]
    shard = attention_weight.shape[0]
    slotted = shard % 8 == 0
    half = width // 2
    def along(block, by_first, by_second):
        pairs = [
            (h * blocks_axis + b, h * blocks_axis + b + by)
            for h, by in ((0, by_first), (1, by_second))
            for b in range(blocks_axis)
            if 0 <= b + by < blocks_axis
        ]
        return lax.ppermute(block, AXES, pairs)

    slot_index = owner_rows % rows
    pick = (slot_index[None, :] == jnp.arange(rows, dtype=jnp.int32)[:, None]).astype(bf16)
    states = jnp.dot(pick, hidden_states, preferred_element_type=f32).astype(bf16)
    cotangent = jnp.dot(pick, output_cotangent, preferred_element_type=f32).astype(bf16)

    thin = -(-(SEG_ROWS - 1 - rows) // 16) * 16
    side = rows + thin
    partner = swap(states, blocks_axis, count)
    is_first = head == 0
    sent = jnp.where(
        is_first,
        jnp.concatenate([states[rows - thin :], partner], axis=0),
        jnp.concatenate([partner, states[:thin]], axis=0),
    )
    outer = along(sent, 1, -1)
    edge = along(jnp.where(is_first, states[:thin], states[rows - thin :]), -1, 1)
    rows_of = (outer, states, partner, edge)

    small = (
        query_bias,
        value_bias,
        output_bias,
        downward_bias,
        first_gain,
        first_shift,
        second_gain,
        second_shift,
        upward_bias,
    )
    extra = upward_bias.shape[0] // shard
    lead, rest = pack(attention_weight, output_weight, upward_weight, downward_weight, small)
    first_rest = width + upward_weight.shape[1]

    def stacked(block, had, has):
        natural = block.reshape(*had, width).transpose(0, 2, 1, 3)
        if len(has) == 2:
            return natural.reshape(*has, width).transpose(1, 0, 2).reshape(has[1], -1)
        return natural.reshape(*has, width).transpose(0, 2, 1, 3).reshape(width, -1)

    me_of = me.astype(jnp.int32).reshape(1)
    me_head = jnp.stack([me, head]).astype(jnp.int32)
    if slotted:
        lead_all = Spread(lead[None], [far, core], count)
        lead_all.start()
        follow_all = Spread(rest[None], follow_rounds[0], count)
        held = lead_all.finish()
        lead_two = Spread(held, [(*near_x, *near_y), core], count)
        lead_two.start()
        follow_all.held = after(follow_all.held, held)
        follow_all.start()
        held = lead_two.finish([sent])
        lead_own = swap(held, core[0], count)
        pieces = [held, lead_own]
        lead_places = piece_places([far, (*near_x, *near_y), core], 1)
        held = follow_all.finish([held])
        follow = [
            Spread(block, rounds[1:], count)
            for block, rounds in zip((held[..., :first_rest], held[..., first_rest:]), follow_rounds)
        ]
        [chain.start() for chain in follow]
        token = [chain.finish([outer, edge]) for chain in follow]
        [chain.start_two() for chain in follow]
        pieces[0] = after(pieces[0], *token)
    else:
        full = gathered(lead, order, count, me)
        pieces = [full[None]]
        lead_places = [[0]]
    queries, keys, values, attended, stats, weight_full, reach, vectors = attention_forward(
        lengths, first, me_head, rows_of, pieces, side, lead_places
    )
    if slotted:
        [chain.finish_two([attended]) for chain in follow]
        follow_parts = [chain.parts for chain in follow]
        follow_places = [piece_places(rounds) for rounds in follow_rounds]
    else:
        full = gathered(rest, order, count, me)
        follow_parts = [
            [full[None, :, :first_rest]],
            [stacked(full[:, first_rest:], (count, shard, extra), (extra, width))[None]],
        ]
        follow_places = [[[0]], [[0]]]
    bias_upward = (
        vectors[8 : 8 + extra].reshape(extra, count, shard).transpose(1, 0, 2).reshape(1, -1)
    )

    outs = feed_forward(
        me_of,
        attended,
        states,
        cotangent,
        vectors,
        bias_upward,
        *follow_parts,
        follow_places,
        back_bits[:2],
    )
    result, grad_residual, grad_attended, small_sums = outs[:4]
    gradients = outs[4:]
    sums = jnp.concatenate(
        [
            small_sums[:6],
            small_sums[8 : 8 + extra].reshape(count, extra, shard).transpose(1, 0, 2).reshape(extra, width),
        ]
    )
    if slotted:
        group = [Gathering(*gradients, first_rest, back_rounds[:2], count)]
        token = [x for chain in group for x in chain.advance()]
        grad_attended = after(grad_attended, *token)

    grad_query, grad_key, grad_value, *slots = attention_backward(
        lengths,
        first,
        me_of,
        queries,
        keys,
        values,
        grad_attended,
        stats,
        reach,
        side,
        shard,
        2 if slotted else 1,
        back_bits[2],
        sums,
    )

    step = lambda chains, token: [x for chain in chains for x in chain.advance(token)]
    if slotted:
        arrived = [x for chain in group for x in chain.arrive()]
        grad_query, grad_key, grad_value, *slots = tied(
            (grad_query, grad_key, grad_value, *slots), arrived
        )
        halves = [Direct(*slots, back_rounds[2], count)]
        token = step(group, [grad_query])
        (grad_key,) = tied([grad_key], token)

    def input_rows(select):
        return sum(
            jnp.einsum(
                "rc,dc->rd",
                select(grad),
                weight_full[:, n * width : (n + 1) * width],
                preferred_element_type=f32,
            )
            for n, grad in ((1, grad_key), (2, grad_value))
        )

    grad_outer = input_rows(lambda g: jnp.where(is_first, g[:side], g[side + rows :]))
    grad_outer = grad_outer.astype(bf16)
    back = along(grad_outer, -1, 1)
    grad_rest = input_rows(
        lambda g: jnp.where(
            is_first, g[side + rows :], jnp.concatenate([g[thin:side], g[:thin]], axis=0)
        )
    )
    back_edge = along(grad_rest[rows:].astype(bf16), 1, -1)
    if slotted:
        token = step(group, [grad_outer, grad_rest])
        token = step(halves, token)
        (back,) = tied([back], token)
    back_own = jnp.where(is_first, back[:thin], back[rows:]).astype(f32)
    back_partner = jnp.where(is_first, back[thin:], back[:rows])
    grad_near = (grad_rest[:rows] + back_partner.astype(f32)).astype(bf16)
    back_near = swap(grad_near, blocks_axis, count)
    if slotted:
        (grad_key, grad_query) = tied([grad_key, grad_query], [grad_near])
    middle = (
        input_rows(lambda g: g[side : side + rows])
        + jnp.einsum("rc,dc->rd", grad_query, weight_full[:, :width], preferred_element_type=f32)
        + grad_residual
    )
    if slotted:
        (result,) = tied([result], [middle])
    layer_output = jnp.take(result, slot_index, axis=0)
    if slotted:
        token = step(group, [layer_output])
        token = step(halves, token)
        (back_near,) = tied([back_near], token)
    pad_low = lambda v: jnp.pad(v, ((0, rows - thin), (0, 0)))
    pad_high = lambda v: jnp.pad(v, ((rows - thin, 0), (0, 0)))
    back_edge = back_edge.astype(f32)
    grad_input = (
        middle
        + back_near.astype(f32)
        + jnp.where(
            is_first, pad_high(back_own) + pad_low(back_edge), pad_low(back_own) + pad_high(back_edge)
        )
    )
    grad_hidden = jnp.take(grad_input, slot_index, axis=0)

    if slotted:
        step(halves, [grad_hidden])
        out_rest, out_lead = group[0].total, halves[0].total
    else:
        by_device = lambda grad: grad.reshape((count, grad.size // grad.shape[-1] // count, -1))
        grad_down = stacked(gradients[0][0][:, first_rest:], (1, width, extra), (count, extra, shard))
        grad_rest_all = jnp.concatenate([gradients[0][0][:, :first_rest], grad_down], axis=1)
        out_rest = reduced(by_device(grad_rest_all), order, count, me)
        out_lead = reduced(by_device(slots[0]), order, count, me)
    out_triple = out_lead[:, : 3 * width]
    out_downward = out_rest[:, first_rest:].reshape(shard, extra, width)
    out_downward = out_downward.transpose(1, 0, 2).reshape(extra * shard, width)
    summed = out_lead[:, 3 * width :].T
    (
        out_query,
        out_value,
        out_output,
        out_down_bias,
        out_gain_one,
        out_shift_one,
        out_gain_two,
        out_shift_two,
    ) = [summed[i] for i in range(8)]
    out_up_bias = summed[8 : 8 + extra].reshape(-1)
    return (
        layer_output,
        grad_hidden,
        out_triple,
        out_rest[:, :width],
        out_rest[:, width:first_rest],
        out_downward,
        out_query,
        out_value,
        out_output,
        out_up_bias,
        out_down_bias,
        out_gain_one,
        out_shift_one,
        out_gain_two,
        out_shift_two,
    )


def solution(mesh):
    matrix, vector = P(AXES, None), P(AXES)
    return jax.shard_map(
        local,
        mesh=mesh,
        in_specs=(matrix, vector, P(), *[matrix] * 4, *[vector] * 9, matrix),
        out_specs=(*[matrix] * 6, *[vector] * 9),
        check_vma=False,
    )
```

```python
import functools

import jax
import jax.numpy as jnp
import numpy as np
from jax import lax
from jax.experimental import pallas as pl
from jax.experimental.pallas import tpu as pltpu
from jax.sharding import PartitionSpec as P

DH = 64
SEG_TOK = 502
MEMR = 10
SEG_ROWS = SEG_TOK + 2 * MEMR
AXES = ("head", "blk")
TILE = 128
PAIR = 2 * DH
AT_ONCE = 3
WIDE = AT_ONCE * PAIR
WINDOW = 544

norm_eps = 1e-12
masked_score = -1e30
score_scale = 0.125
root_half = 0.7071067811865476
inverse_root_two_pi = 0.3989422804014327
f32 = jnp.float32
bf16 = jnp.bfloat16


def swap(block, bit, count):
    return lax.ppermute(block, AXES, [(i, i ^ bit) for i in range(count)])


def tied(values, others):
    values = tuple(values)
    return list(lax.optimization_barrier((*values, *others))[: len(values)])


def after(value, *others):
    return tied([value], others)[0]


def relative(bits):
    return [sum(bit for at, bit in enumerate(bits) if j >> at & 1) for j in range(1 << len(bits))]


def gathered(shard, order, count, me):
    held, have = shard, []
    for bit in order:
        axis = sum(b > bit for b in have)
        have.append(bit)
        other = jnp.expand_dims(swap(held, bit, count), axis)
        own = jnp.expand_dims(held, axis)
        held = jnp.where(
            (me & bit) == 0,
            jnp.concatenate([own, other], axis=axis),
            jnp.concatenate([other, own], axis=axis),
        )
    return held.reshape((count * shard.shape[0],) + shard.shape[1:])


def reduced(blocks, order, count, me):
    have = sorted(order, reverse=True)
    held = blocks.reshape((2,) * len(have) + blocks.shape[1:])
    for step, bit in enumerate(order):
        axis = have.index(bit)
        have.remove(bit)
        mine = ((me & bit) != 0).astype(jnp.int32)
        keep = lax.dynamic_index_in_dim(held, mine, axis, keepdims=False)
        send = lax.dynamic_index_in_dim(held, 1 - mine, axis, keepdims=False)
        total = keep.astype(f32) + swap(send, bit, count).astype(f32)
        held = total if not have else total.astype(blocks.dtype)
    return held


class Spread:
    def __init__(self, held, rounds, count):
        self.held, self.rounds, self.count = held, list(rounds), count
        self.parts = None

    def start(self):
        self.recvs = [swap(self.held, c, self.count) for c in relative(self.rounds[0])[1:]]

    def finish(self, token=()):
        recvs = tied(self.recvs, token) if token else self.recvs
        self.held = jnp.concatenate([self.held, *recvs], axis=0)
        self.rounds.pop(0)
        return self.held

    def start_two(self):
        self.start()
        (self.last,) = self.rounds[1]
        self.own = swap(self.held, self.last, self.count)

    def finish_two(self, token=()):
        recvs = tied(self.recvs, token) if token else self.recvs
        self.parts = [self.held, *recvs, self.own, *[swap(r, self.last, self.count) for r in recvs]]
        return recvs


def piece_places(rounds, apart=2):
    pieces = [relative([b for r in rounds[: len(rounds) - apart] for b in r])]
    for bits in rounds[len(rounds) - apart :]:
        pieces = [[j + c for j in piece] for c in relative(bits) for piece in pieces]
    return pieces


class Gathering:
    def __init__(self, keep, send, cut, rounds, count):
        self.rounds, self.count, self.cut, self.at = rounds, count, cut, 0
        self.keep = keep
        self.recvs = [swap(send, self.rounds[0][0][0], count)]
        self.total = None

    def arrive(self, token=()):
        self.recvs = tied(self.recvs, token) if token else self.recvs
        return self.recvs

    def advance(self, token=()):
        recvs = self.arrive(token)
        add = lambda terms, at: sum(t[at].astype(f32) for t in terms)
        joined = lambda at: jnp.concatenate([add(terms, at) for terms in self.terms], axis=-1)
        self.at += 1
        if self.at == 1:
            terms = [self.keep, *recvs]
            self.terms = [[t[..., : self.cut] for t in terms], [t[..., self.cut :] for t in terms]]
        elif self.at in (2, 3):
            for terms, recv in zip(self.terms, recvs):
                terms.append(recv)
        else:
            self.total = joined(0) + sum(r[0].astype(f32) for r in recvs)
            return [self.total]
        if self.at < 3:
            half = self.terms[0][0].shape[0] // 2
            sends = [add(terms, slice(half, None)).astype(bf16) for terms in self.terms]
            bits = [rounds[self.at][0] for rounds in self.rounds]
            self.recvs = [swap(s, b, self.count) for s, b in zip(sends, bits)]
        else:
            combos = relative(self.rounds[0][3][::-1])
            half = 1
            sends = [joined(slice(j, j + 1)).astype(bf16) for j in range(1, len(combos))]
            self.recvs = [swap(s, c, self.count) for s, c in zip(sends, combos[1:])]
            half = 1
        self.terms = [[t[:half] for t in terms] for terms in self.terms]
        return sends


class Direct:
    def __init__(self, keep, send, rounds, count):
        self.rounds, self.count, self.terms, self.total = list(rounds[1:]), count, [keep], None
        self.recvs = [swap(send, rounds[0][0], count)]

    def advance(self, token=()):
        self.terms += tied(self.recvs, token) if token else self.recvs
        add = lambda at: sum(t[at].astype(f32) for t in self.terms)
        if not self.rounds:
            self.total = add(0)
            return [self.total]
        combos = relative(self.rounds.pop(0)[::-1])
        each = self.terms[0].shape[0] // len(combos)
        sends = [add(slice(j * each, (j + 1) * each)).astype(bf16) for j in range(1, len(combos))]
        self.terms = [t[:each] for t in self.terms]
        self.recvs = [swap(x, c, self.count) for x, c in zip(sends, combos[1:])]
        return sends


def segment_at(lengths_ref, sequences, position):
    start = jnp.int32(0)
    low = jnp.int32(0)
    high = jnp.int32(0)
    for i in range(sequences):
        tokens = lengths_ref[i]
        end = start + tokens + 2 * MEMR * lax.div(tokens + (SEG_TOK - 1), jnp.int32(SEG_TOK))
        inside = (position >= start) & (position < end)
        first = start + lax.div(position - start, jnp.int32(SEG_ROWS)) * SEG_ROWS
        low = jnp.where(inside, first, low)
        high = jnp.where(inside, jnp.minimum(first + SEG_ROWS, end), high)
        start = end
    return low, high


def over_segments(lengths_ref, sequences, first_row, rows, side, body):
    def step(position):
        low, high = segment_at(lengths_ref, sequences, position)
        high = jnp.maximum(high, position + 1)
        low_at = low - first_row + side
        high_at = high - first_row + side
        window = jnp.minimum(lax.div(low_at, jnp.int32(16)) * 16, rows + 2 * side - WINDOW)
        window = pl.multiple_of(jnp.maximum(window, 0), 16)
        tile_from = lax.div(jnp.maximum(low - first_row, 0), jnp.int32(TILE))
        tile_to = lax.div(jnp.minimum(high - first_row, rows) + TILE - 1, jnp.int32(TILE))
        body(low_at, high_at, window, tile_from, tile_to)
        return high

    lax.while_loop(lambda position: position < first_row + rows, step, first_row)


def two_heads(block):
    lane = lax.broadcasted_iota(jnp.int32, block.shape, 1)
    zero = jnp.zeros_like(block)
    return jnp.concatenate(
        [jnp.where(lane < DH, block, zero), jnp.where(lane < DH, zero, block)], axis=0
    )


def own_blocks(product):
    return jnp.concatenate([product[:DH, :TILE], product[DH:, TILE:]], axis=0).T


def key_bias(low_at, high_at, window):
    row = lax.broadcasted_iota(jnp.int32, (WINDOW, 2 * TILE), 0) + window
    return jnp.where((row >= low_at) & (row < high_at), 0.0, masked_score)


def rows_inside(tile, low_at, high_at, side, shape, dim):
    at = lax.broadcasted_iota(jnp.int32, shape, dim)
    if dim == 1:
        at = at & (TILE - 1)
    at = at + (tile * TILE + side)
    return (at >= low_at) & (at < high_at)


NT = (((1,), (1,)), ((), ()))
NN = (((1,), (0,)), ((), ()))


def mul(left, right, dims=NN):
    return lax.dot_general(left, right, dims, preferred_element_type=f32)


def slots_to_rows(slots, shard, store):
    total, _, columns = slots.shape
    step = min(total, 8)
    for d in range(0, total, step):
        block = slots[d : d + step].astype(f32).reshape(step * shard, columns)
        store(slice(d * shard, (d + step) * shard), block.astype(bf16))


def forward_kernel(plan, lengths_ref, first_ref, me_ref, *refs):
    sequences, side, taken, dests, shard = plan
    outer_ref, states_ref, partner_ref, edge_ref = refs[:4]
    pieces, refs = refs[4 : 4 + taken], refs[4 + taken :]
    (q_ref, k_ref, v_ref, o_ref, stat_ref, weight_ref, reach_ref, vec_ref) = refs[:8]
    bias_ref, vt_ref, slots_ref, small_ref, in_sem = refs[8:]
    rows, width = states_ref.shape
    thin = edge_ref.shape[0]
    pair = pl.program_id(0)
    me, head = me_ref[0], me_ref[1]

    @pl.when(pair == 0)
    def _():
        slots = len(dests[0])
        copies = [
            pltpu.make_async_copy(
                pieces[a].at[j], slots_ref.at[dests[a][j] ^ me], in_sem.at[a * slots + j]
            )
            for a in range(taken)
            for j in range(slots)
        ]
        for copy in copies:
            copy.start()

        @pl.when(head == 0)
        def _():
            reach_ref[:side, :] = outer_ref[...]
            reach_ref[side + rows : side + 2 * rows, :] = partner_ref[...]
            reach_ref[side + 2 * rows :, :] = edge_ref[...]

        @pl.when(head != 0)
        def _():
            reach_ref[:thin, :] = edge_ref[...]
            reach_ref[thin:side, :] = partner_ref[...]
            reach_ref[side + rows :, :] = outer_ref[...]

        reach_ref[side : side + rows, :] = states_ref[...]
        for copy in copies:
            copy.wait()

        def store(at, block):
            weight_ref[at, :] = block[:, : 3 * width]
            small_ref[at, :] = block[:, 3 * width :]

        slots_to_rows(slots_ref, shard, store)
        vec_ref[...] = small_ref[...].astype(f32).T[: vec_ref.shape[0]]

    stat_ref[...] = jnp.zeros_like(stat_ref)
    o_ref[...] = jnp.zeros_like(o_ref)
    lanes = [pl.ds(pl.multiple_of(pair * WIDE + n * width, PAIR), WIDE) for n in range(3)]
    queries = mul(states_ref[...], weight_ref[:, lanes[0]]) + vec_ref[0:1, lanes[0]]
    q_ref[...] = queries.astype(bf16) * jnp.asarray(score_scale, bf16)
    k_ref[...] = mul(reach_ref[...], weight_ref[:, lanes[1]]).astype(bf16)
    values = mul(reach_ref[...], weight_ref[:, lanes[2]]) + vec_ref[1:2, lanes[0]]
    v_ref[...] = values.astype(bf16)
    subs = [(n, slice(n * PAIR, (n + 1) * PAIR)) for n in range(AT_ONCE)]

    def segment(low_at, high_at, window, tile_from, tile_to):
        bias_ref[...] = key_bias(low_at, high_at, window)
        keys_at = pl.ds(window, WINDOW)
        for n, part in subs:
            vt_ref[n] = v_ref[keys_at, part].T

        def one(tile, carry):
            at = pl.ds(pl.multiple_of(tile * TILE, TILE), TILE)
            wide = pl.ds(pl.multiple_of(tile * 2 * TILE, 2 * TILE), 2 * TILE)
            inside = rows_inside(tile, low_at, high_at, side, (TILE, PAIR), 0)
            there = rows_inside(tile, low_at, high_at, side, (1, 2 * TILE), 1)
            scores = [
                mul(k_ref[keys_at, part], two_heads(q_ref[at, part]), NT) + bias_ref[...]
                for _, part in subs
            ]
            for (n, part), score in zip(subs, scores):
                top = jnp.max(score, axis=0, keepdims=True)
                raised = jnp.exp(score - top)
                total = jnp.sum(raised, axis=0, keepdims=True)
                mixed = mul(vt_ref[n], raised.astype(bf16)) * (1.0 / total)
                mixed = own_blocks(mixed).astype(bf16)
                o_ref[at, part] = jnp.where(inside, mixed, o_ref[at, part])
                level = top + jnp.log(total)
                stat_ref[n, 0:1, wide] = jnp.where(there, level, stat_ref[n, 0:1, wide])
            return carry

        lax.fori_loop(tile_from, tile_to, one, 0)

    over_segments(lengths_ref, sequences, first_ref[0], rows, side, segment)


def backward_kernel(
    plan,
    lengths_ref,
    first_ref,
    me_ref,
    q_ref,
    k_ref,
    v_ref,
    g_ref,
    stat_ref,
    reach_ref,
    *refs,
):
    sequences, side, held, slot_of, shard = plan
    sums_in, dq_ref, dk_ref, dv_ref = refs[:4]
    outs = refs[4 : 4 + held]
    (bias_ref, kt_ref, dq_acc, dk_acc, dv_acc, reach_t, slots_ref, small_ref, sem) = refs[4 + held :]
    rows = q_ref.shape[0]
    pair, pairs = pl.program_id(0), pl.num_programs(0)
    me = me_ref[0]
    total, width = slots_ref.shape[0], reach_ref.shape[1]

    @pl.when(pair == 0)
    def _():
        reach_t[...] = reach_ref[...].T
        small_ref[...] = jnp.zeros_like(small_ref)

    dq_acc[...] = jnp.zeros_like(dq_acc)
    dk_acc[...] = jnp.zeros_like(dk_acc)
    dv_acc[...] = jnp.zeros_like(dv_acc)

    subs = [(n, slice(n * PAIR, (n + 1) * PAIR)) for n in range(AT_ONCE)]

    def segment(low_at, high_at, window, tile_from, tile_to):
        bias_ref[...] = key_bias(low_at, high_at, window)
        keys_at = pl.ds(window, WINDOW)
        for n, part in subs:
            kt_ref[n] = k_ref[keys_at, part].T

        def one(tile, carry):
            at = pl.ds(pl.multiple_of(tile * TILE, TILE), TILE)
            wide = pl.ds(pl.multiple_of(tile * 2 * TILE, 2 * TILE), 2 * TILE)
            there = rows_inside(tile, low_at, high_at, side, (1, 2 * TILE), 1)
            queries = [two_heads(q_ref[at, part]) for _, part in subs]
            grads = [two_heads(g_ref[at, part]) for _, part in subs]
            scores = [
                mul(k_ref[keys_at, part], query, NT) + bias_ref[...]
                for (_, part), query in zip(subs, queries)
            ]
            grad_probs = [mul(v_ref[keys_at, part], g, NT) for (_, part), g in zip(subs, grads)]
            for n, part in subs:
                level = jnp.where(there, stat_ref[n, 0:1, wide], -masked_score)
                probs = jnp.exp(scores[n] - level)
                shared = jnp.sum(probs * grad_probs[n], axis=0, keepdims=True)
                grad_scores = (probs * (grad_probs[n] - shared)).astype(bf16)
                dv_acc[keys_at, part] += mul(probs.astype(bf16), grads[n])
                dk_acc[keys_at, part] += mul(grad_scores, queries[n])
                dq_acc[at, part] += own_blocks(mul(kt_ref[n], grad_scores))
            return carry

        lax.fori_loop(tile_from, tile_to, one, 0)

    over_segments(lengths_ref, sequences, first_ref[0], rows, side, segment)
    dq = (dq_acc[...] * score_scale).astype(bf16)
    dk, dv = dk_acc[...].astype(bf16), dv_acc[...].astype(bf16)
    dq_ref[...] = dq
    dk_ref[...] = dk
    dv_ref[...] = dv
    lanes = [pl.ds(pl.multiple_of(pair * WIDE + n * width, PAIR), WIDE) for n in range(3)]
    small_ref[0:1, lanes[0]] = jnp.sum(dq.astype(f32), axis=0, keepdims=True)
    small_ref[1:2, lanes[0]] = jnp.sum(dv.astype(f32), axis=0, keepdims=True)

    def put(value, columns):
        for i in range(total):
            slot = slot_of(i ^ me) if total > 1 else 0
            slots_ref[slot, :, columns] = value[i * shard : (i + 1) * shard].astype(bf16)

    own_t = reach_ref[side : side + rows, :]
    put(mul(own_t, dq, (((0,), (0,)), ((), ()))), lanes[0])
    put(mul(reach_t[...], dk), lanes[1])
    put(mul(reach_t[...], dv), lanes[2])
    each = total // held
    copies = [
        pltpu.make_async_copy(slots_ref.at[pl.ds(a * each, each)], outs[a], sem.at[a])
        for a in range(held)
    ]

    @pl.when(pair == pairs - 1)
    def _():
        count = sums_in.shape[0]
        small_ref[2 : 2 + count, :] = sums_in[...]
        put(small_ref[...].T, pl.ds(3 * width, TILE))
        for copy in copies:
            copy.start()
        for copy in copies:
            copy.wait()


def pack_kernel(shard, weight_ref, *refs):
    *rest_refs, lead_ref, rest_ref, rows_ref = refs
    (output_ref, upward_ref, downward_ref), vector_refs = rest_refs[:3], rest_refs[3:]
    rows_ref[...] = jnp.zeros_like(rows_ref)
    row = 0
    for ref in vector_refs:
        values = ref[...].astype(f32).reshape(1, ref.shape[0])
        for at in range(0, ref.shape[0], shard):
            rows_ref[row : row + 1, :shard] = values[:, at : at + shard]
            row += 1
    width = output_ref.shape[1]
    lead_ref[:, : 3 * width] = weight_ref[...]
    lead_ref[:, 3 * width :] = rows_ref[...].T[:shard].astype(bf16)
    hidden = upward_ref.shape[1]
    rest_ref[:, :width] = output_ref[...]
    rest_ref[:, width : width + hidden] = upward_ref[...]
    down = downward_ref[...].astype(f32)
    for k in range(down.shape[0] // shard):
        at = width + hidden + k * width
        rest_ref[:, at : at + width] = down[k * shard : (k + 1) * shard].astype(bf16)


def pack(weight, output, upward, downward, vectors):
    shard = weight.shape[0]
    shape = jax.ShapeDtypeStruct
    return pl.pallas_call(
        functools.partial(pack_kernel, shard),
        name="pack",
        out_shape=(
            shape((shard, weight.shape[1] + 128), bf16),
            shape((shard, output.shape[1] + 2 * upward.shape[1]), bf16),
        ),
        in_specs=[pl.BlockSpec(memory_space=pltpu.VMEM)] * (4 + len(vectors)),
        out_specs=[pl.BlockSpec(memory_space=pltpu.VMEM)] * 2,
        scratch_shapes=[pltpu.VMEM((128, 128), f32)],
    )(weight, output, upward, downward, *vectors)


def attention_forward(lengths, first, me_head, rows_of, pieces, side, dests):
    outer, states, partner, edge = rows_of
    rows, features = states.shape
    wide = rows + 2 * side
    taken, (slots, shard, columns) = len(pieces), pieces[0].shape
    pairs = features // PAIR
    whole = lambda *shape: pl.BlockSpec(shape, lambda h, *_: (0,) * len(shape))
    column = lambda n: pl.BlockSpec((n, WIDE), lambda h, *_: (0, h))
    anywhere = pl.BlockSpec(memory_space=pl.ANY)
    shape = jax.ShapeDtypeStruct
    plan = (lengths.shape[0], side, taken, dests, shard)
    return pl.pallas_call(
        functools.partial(forward_kernel, plan),
        name="attention_forward",
        out_shape=(
            shape((rows, features), bf16),
            shape((wide, features), bf16),
            shape((wide, features), bf16),
            shape((rows, features), bf16),
            shape((pairs, 8, 2 * rows), f32),
            shape((features, 3 * features), bf16),
            shape((wide, features), bf16),
            shape((16, features), f32),
        ),
        grid_spec=pltpu.PrefetchScalarGridSpec(
            num_scalar_prefetch=3,
            grid=(pairs // AT_ONCE,),
            in_specs=[*[whole(*r.shape) for r in rows_of], *[anywhere] * taken],
            out_specs=[
                column(rows),
                column(wide),
                column(wide),
                column(rows),
                pl.BlockSpec((AT_ONCE, 8, 2 * rows), lambda h, *_: (h, 0, 0)),
                whole(features, 3 * features),
                whole(wide, features),
                whole(16, features),
            ],
            scratch_shapes=[
                pltpu.VMEM((WINDOW, 2 * TILE), f32),
                pltpu.VMEM((AT_ONCE, PAIR, WINDOW), bf16),
                pltpu.VMEM((taken * slots, shard, columns), bf16),
                pltpu.VMEM((features, columns - 3 * features), bf16),
                pltpu.SemaphoreType.DMA((taken * slots,)),
            ],
        ),
        compiler_params=pltpu.CompilerParams(vmem_limit_bytes=48 * 2**20),
    )(lengths, first, me_head, *rows_of, *pieces)


def attention_backward(
    lengths, first, me, queries, keys, values, grads, stats, reach, side, shard, held, bits, sums
):
    rows, features = queries.shape
    wide = keys.shape[0]
    pairs = features // PAIR
    total = features // shard if held > 1 else 1
    per = shard if held > 1 else features
    columns = 3 * features + TILE
    column = lambda n: pl.BlockSpec((n, WIDE), lambda h, *_: (0, h))
    whole = lambda *shape: pl.BlockSpec(shape, lambda h, *_: (0,) * len(shape))
    anywhere = pl.BlockSpec(memory_space=pl.ANY)
    shape = jax.ShapeDtypeStruct
    place = exchange_slot(bits)
    return pl.pallas_call(
        functools.partial(backward_kernel, (lengths.shape[0], side, held, place, per)),
        name="attention_backward",
        out_shape=(
            shape((rows, features), bf16),
            shape((wide, features), bf16),
            shape((wide, features), bf16),
            *[shape((total // held, per, columns), bf16)] * held,
        ),
        grid_spec=pltpu.PrefetchScalarGridSpec(
            num_scalar_prefetch=3,
            grid=(pairs // AT_ONCE,),
            in_specs=[
                column(rows),
                column(wide),
                column(wide),
                column(rows),
                pl.BlockSpec((AT_ONCE, 8, 2 * rows), lambda h, *_: (h, 0, 0)),
                whole(wide, features),
                whole(*sums.shape),
            ],
            out_specs=[column(rows), column(wide), column(wide), *[anywhere] * held],
            scratch_shapes=[
                pltpu.VMEM((WINDOW, 2 * TILE), f32),
                pltpu.VMEM((AT_ONCE, PAIR, WINDOW), bf16),
                pltpu.VMEM((rows, WIDE), f32),
                pltpu.VMEM((wide, WIDE), f32),
                pltpu.VMEM((wide, WIDE), f32),
                pltpu.VMEM((features, wide), bf16),
                pltpu.VMEM((total, per, columns), bf16),
                pltpu.VMEM((TILE, features), f32),
                pltpu.SemaphoreType.DMA((held,)),
            ],
        ),
        compiler_params=pltpu.CompilerParams(vmem_limit_bytes=56 * 2**20),
    )(lengths, first, me, queries, keys, values, grads, stats, reach, sums)


TN = (((0,), (0,)), ((), ()))


def row_mean(value):
    return jnp.mean(value, axis=-1, keepdims=True)


def column_sum(value):
    return jnp.sum(value, axis=0, keepdims=True)


def normalize(summed):
    centered = summed - row_mean(summed)
    inverse_std = lax.rsqrt(row_mean(centered * centered) + norm_eps)
    return centered * inverse_std, inverse_std


def normalize_back(grad, normed, inverse_std):
    return inverse_std * (grad - row_mean(grad) - normed * row_mean(grad * normed))


def feed_kernel(plan, *refs):
    taken, held, in_dest, out_slot, shard, border = plan
    me_ref, att_ref, states_ref, cot_ref, vec_ref, upb_ref = refs[:6]
    mixed_in, down_in = refs[6 : 6 + taken], refs[6 + taken : 6 + 2 * taken]
    at = 6 + 2 * taken
    result_ref, res_ref, gatt_ref, small_ref = refs[at : at + 4]
    outs, refs = refs[at + 4 : at + 4 + held], refs[at + 4 + held :]
    (wslot, wmix, wdown, act, slope, gall, acc, in_sem, out_sem) = refs
    me = me_ref[0]
    width = states_ref.shape[1]
    hidden = wdown.shape[0]
    slots = len(in_dest[0][0])

    def copies_of(which, pieces, lanes):
        return [
            pltpu.make_async_copy(
                pieces[a].at[j],
                wslot.at[in_dest[which][a][j] ^ me, :, lanes],
                in_sem.at[which, a * slots + j],
            )
            for a in range(taken)
            for j in range(slots)
        ]

    first_lanes = pl.ds(0, border)
    last_lanes = pl.ds(border, wslot.shape[2] - border)
    copies_in = lambda: copies_of(0, mixed_in, first_lanes)
    copies_down = lambda: copies_of(1, down_in, last_lanes)
    for copy in copies_in():
        copy.start()
    for copy in copies_down():
        copy.start()
    for copy in copies_in():
        copy.wait()
    for copy in copies_down():
        copy.wait()
    total = taken * slots
    mixed_width = wmix.shape[1]

    def store(at, block):
        wmix[at, :] = block

    slots_to_rows(wslot.at[:, :, pl.ds(0, mixed_width)], shard, store)

    bias_out, bias_down, gain_one, shift_one, gain_two, shift_two = (
        vec_ref[i : i + 1, :] for i in range(2, 8)
    )
    branch = mul(att_ref[...], wmix[:, :width]) + bias_out
    normed_one, scale_one = normalize(states_ref[...].astype(f32) + branch)
    first_norm = normed_one * gain_one + shift_one
    inner = first_norm.astype(bf16)
    extra = hidden // width
    deep = extra * shard
    for d in range(total):
        block = wslot[d, :, mixed_width:].astype(f32)
        block = [block[:, k * width : (k + 1) * width] for k in range(extra)]
        wdown[d * deep : (d + 1) * deep, :] = jnp.concatenate(block, axis=0).astype(bf16)
    chunks = range(0, hidden, width)
    for c in chunks:
        lifted = mul(inner, wmix[:, width + c : 2 * width + c]) + upb_ref[:, c : c + width]
        phi_sum = 0.5 * (1.0 + lax.erf(lifted * root_half))
        active = (lifted * phi_sum).astype(bf16)
        act[:, c : c + width] = active
        slope[:, c : c + width] = phi_sum + lifted * (
            inverse_root_two_pi * jnp.exp(-0.5 * lifted * lifted)
        )
        part = mul(active, wdown[c : c + width, :])
        acc[...] = part if c == 0 else acc[...] + part
    normed_two, scale_two = normalize(first_norm + (acc[...] + bias_down))
    result_ref[...] = (normed_two * gain_two + shift_two).astype(bf16)

    cot = cot_ref[...].astype(f32)
    small_ref[4:5, :] = column_sum(cot * normed_two)
    small_ref[5:6, :] = column_sum(cot)
    grad_mid = normalize_back(cot * gain_two, normed_two, scale_two)
    grad_down = grad_mid.astype(bf16)
    small_ref[1:2, :] = column_sum(grad_down.astype(f32))

    def put(value, first, per, columns):
        for i in range(value.shape[0] // per):
            places = [out_slot(order, (first + i) ^ me) for order in range(2)]
            for k in range(per // shard):
                rows = value[i * per + k * shard :][:shard].astype(bf16)
                start = columns + k * width
                stop = start + width
                middle = min(max(border, start), stop)
                if middle > start:
                    gall[places[0], :, start:middle] = rows[:, : middle - start]
                if stop > middle:
                    gall[places[1], :, middle:stop] = rows[:, middle - start :]

    copies_out = [
        pltpu.make_async_copy(
            gall.at[pl.ds(a * (total // held), total // held)], outs[a], out_sem.at[a]
        )
        for a in range(held)
    ]
    inner_t = inner.T
    for c in chunks:
        active = act[:, c : c + width]
        grad_active = mul(grad_down, wdown[c : c + width, :], NT)
        grad_lift = (grad_active * slope[:, c : c + width]).astype(bf16)
        small_ref[8 + c // width : 9 + c // width, :] = column_sum(grad_lift.astype(f32))
        grad_w = mul(active, grad_down, TN)
        if total > 1:
            put(grad_w, c // deep, deep, width + hidden)
        else:
            gall[0, :, width + hidden + c : 2 * width + hidden + c] = grad_w.astype(bf16)
        put(mul(inner_t, grad_lift), 0, shard, width + c)
        part = mul(grad_lift, wmix[:, width + c : 2 * width + c], NT)
        acc[...] = part if c == 0 else acc[...] + part
    grad_first = acc[...] + grad_mid
    small_ref[2:3, :] = column_sum(grad_first * normed_one)
    small_ref[3:4, :] = column_sum(grad_first)
    grad_residual = normalize_back(grad_first * gain_one, normed_one, scale_one)
    res_ref[...] = grad_residual
    grad_branch = grad_residual.astype(bf16)
    small_ref[0:1, :] = column_sum(grad_branch.astype(f32))
    put(mul(att_ref[...], grad_branch, TN), 0, shard, 0)
    for copy in copies_out:
        copy.start()
    gatt_ref[...] = mul(grad_branch, wmix[:, :width], NT).astype(bf16)
    small_ref[6:8, :] = jnp.zeros((2, width), f32)
    small_ref[12:, :] = jnp.zeros((small_ref.shape[0] - 12, width), f32)
    for copy in copies_out:
        copy.wait()


def exchange_slot(bits):
    def slot(diff):
        found = jnp.int32(0)
        for at, bit in enumerate(reversed(bits)):
            found = found + (((diff & bit) != 0).astype(jnp.int32) << at)
        return found

    return slot


def feed_forward(me, attended, states, cotangent, vectors, up_bias, mixed, down, dests, backs):
    rows, width = states.shape
    taken, (slots, shard, border) = len(mixed), mixed[0].shape
    columns = border + down[0].shape[2]
    held = min(taken, 2)
    total = taken * slots
    hidden = (columns - width) // 2
    slot_of = [exchange_slot(back) for back in backs]
    place = lambda order, diff: slot_of[order](diff) if held > 1 else 0
    plan = (taken, held, dests, place, shard, border)
    whole = pl.BlockSpec(memory_space=pltpu.VMEM)
    anywhere = pl.BlockSpec(memory_space=pl.ANY)
    shape = jax.ShapeDtypeStruct
    return pl.pallas_call(
        functools.partial(feed_kernel, plan),
        name="feed_forward",
        out_shape=(
            shape((rows, width), bf16),
            shape((rows, width), f32),
            shape((rows, width), bf16),
            shape((16, width), f32),
            *[shape((total // held, shard, columns), bf16)] * held,
        ),
        in_specs=[pl.BlockSpec(memory_space=pltpu.SMEM), *[whole] * 5, *[anywhere] * (2 * taken)],
        out_specs=[*[whole] * 4, *[anywhere] * held],
        scratch_shapes=[
            pltpu.VMEM((total, shard, columns), bf16),
            pltpu.VMEM((total * shard, columns - hidden), bf16),
            pltpu.VMEM((hidden, width), bf16),
            pltpu.VMEM((rows, hidden), bf16),
            pltpu.VMEM((rows, hidden), f32),
            pltpu.VMEM((total, shard, columns), bf16),
            pltpu.VMEM((rows, width), f32),
            pltpu.SemaphoreType.DMA((2, total)),
            pltpu.SemaphoreType.DMA((held,)),
        ],
        compiler_params=pltpu.CompilerParams(vmem_limit_bytes=60 * 2**20),
    )(me, attended, states, cotangent, vectors, up_bias, *mixed, *down)


def local(
    hidden_states,
    owner_rows,
    lengths,
    attention_weight,
    output_weight,
    upward_weight,
    downward_weight,
    query_bias,
    value_bias,
    output_bias,
    upward_bias,
    downward_bias,
    first_gain,
    first_shift,
    second_gain,
    second_shift,
    output_cotangent,
):
    rows, width = hidden_states.shape
    heads_axis, blocks_axis = lax.axis_size("head"), lax.axis_size("blk")
    count = heads_axis * blocks_axis
    me = lax.axis_index(AXES)
    head, blk = lax.axis_index("head"), lax.axis_index("blk")
    first = ((blk * heads_axis + head) * rows).astype(jnp.int32).reshape(1)
    bits = [1 << b for b in range((count - 1).bit_length())]
    far = tuple(b for b in bits if b not in (1, 2, blocks_axis))[::-1]
    near_y, near_x, core = (2,), (blocks_axis,), (1,)
    follow_rounds = ([far, near_y, near_x, core], [far, near_x, near_y, core])
    back_rounds = (
        [core, near_y, near_x, far[::-1]],
        [core, near_x, near_y, far[::-1]],
        [core, (*near_x, *near_y), far[::-1]],
    )
    back_bits = [[b for r in rounds for b in r] for rounds in back_rounds]
    order = bits[::-1]
    shard = attention_weight.shape[0]
    slotted = shard % 8 == 0
    half = width // 2
    def along(block, by_first, by_second):
        pairs = [
            (h * blocks_axis + b, h * blocks_axis + b + by)
            for h, by in ((0, by_first), (1, by_second))
            for b in range(blocks_axis)
            if 0 <= b + by < blocks_axis
        ]
        return lax.ppermute(block, AXES, pairs)

    slot_index = owner_rows % rows
    pick = (slot_index[None, :] == jnp.arange(rows, dtype=jnp.int32)[:, None]).astype(bf16)
    states = jnp.dot(pick, hidden_states, preferred_element_type=f32).astype(bf16)
    cotangent = jnp.dot(pick, output_cotangent, preferred_element_type=f32).astype(bf16)

    thin = -(-(SEG_ROWS - 1 - rows) // 16) * 16
    side = rows + thin
    partner = swap(states, blocks_axis, count)
    is_first = head == 0
    sent = jnp.where(
        is_first,
        jnp.concatenate([states[rows - thin :], partner], axis=0),
        jnp.concatenate([partner, states[:thin]], axis=0),
    )
    outer = along(sent, 1, -1)
    edge = along(jnp.where(is_first, states[:thin], states[rows - thin :]), -1, 1)
    rows_of = (outer, states, partner, edge)

    small = (
        query_bias,
        value_bias,
        output_bias,
        downward_bias,
        first_gain,
        first_shift,
        second_gain,
        second_shift,
        upward_bias,
    )
    extra = upward_bias.shape[0] // shard
    lead, rest = pack(attention_weight, output_weight, upward_weight, downward_weight, small)
    first_rest = width + upward_weight.shape[1]
    border = rest.shape[1] // 256 * 128 if slotted else first_rest

    def stacked(block, had, has):
        natural = block.reshape(*had, width).transpose(0, 2, 1, 3)
        if len(has) == 2:
            return natural.reshape(*has, width).transpose(1, 0, 2).reshape(has[1], -1)
        return natural.reshape(*has, width).transpose(0, 2, 1, 3).reshape(width, -1)

    me_of = me.astype(jnp.int32).reshape(1)
    me_head = jnp.stack([me, head]).astype(jnp.int32)
    if slotted:
        follow_all = Spread(rest[None], follow_rounds[0], count)
        follow_all.start()
        lead_all = Spread(lead[None], [far, core], count)
        lead_all.start()
        held = lead_all.finish()
        lead_two = Spread(held, [(*near_x, *near_y), core], count)
        lead_two.start()
        held = follow_all.finish([held, sent])
        follow = [
            Spread(block, rounds[1:], count)
            for block, rounds in zip((held[..., :border], held[..., border:]), follow_rounds)
        ]
        [chain.start() for chain in follow]
        held = lead_two.finish([chain.held for chain in follow])
        pieces = [held, swap(held, core[0], count)]
        lead_places = piece_places([far, (*near_x, *near_y), core], 1)
        token = [chain.finish([held, outer, edge]) for chain in follow]
        [chain.start_two() for chain in follow]
        pieces[0] = after(pieces[0], *token)
    else:
        full = gathered(lead, order, count, me)
        pieces = [full[None]]
        lead_places = [[0]]
    queries, keys, values, attended, stats, weight_full, reach, vectors = attention_forward(
        lengths, first, me_head, rows_of, pieces, side, lead_places
    )
    if slotted:
        [chain.finish_two([attended]) for chain in follow]
        follow_parts = [chain.parts for chain in follow]
        follow_places = [piece_places(rounds) for rounds in follow_rounds]
    else:
        full = gathered(rest, order, count, me)
        follow_parts = [
            [full[None, :, :first_rest]],
            [stacked(full[:, first_rest:], (count, shard, extra), (extra, width))[None]],
        ]
        follow_places = [[[0]], [[0]]]
    bias_upward = (
        vectors[8 : 8 + extra].reshape(extra, count, shard).transpose(1, 0, 2).reshape(1, -1)
    )

    outs = feed_forward(
        me_of,
        attended,
        states,
        cotangent,
        vectors,
        bias_upward,
        *follow_parts,
        follow_places,
        back_bits[:2],
    )
    result, grad_residual, grad_attended, small_sums = outs[:4]
    gradients = outs[4:]
    sums = jnp.concatenate(
        [
            small_sums[:6],
            small_sums[8 : 8 + extra].reshape(count, extra, shard).transpose(1, 0, 2).reshape(extra, width),
        ]
    )
    if slotted:
        group = [Gathering(*gradients, border, back_rounds[:2], count)]
        layer_output = jnp.take(result, slot_index, axis=0)
        token = [x for chain in group for x in chain.advance([layer_output])]
        grad_attended = after(grad_attended, *token)

    grad_query, grad_key, grad_value, *slots = attention_backward(
        lengths,
        first,
        me_of,
        queries,
        keys,
        values,
        grad_attended,
        stats,
        reach,
        side,
        shard,
        2 if slotted else 1,
        back_bits[2],
        sums,
    )

    step = lambda chains, token: [x for chain in chains for x in chain.advance(token)]
    if slotted:
        arrived = [x for chain in group for x in chain.arrive()]
        grad_query, grad_key, grad_value, *slots = tied(
            (grad_query, grad_key, grad_value, *slots), arrived
        )
        halves = [Direct(*slots, back_rounds[2], count)]
        token = step(group, [grad_query])
        (grad_key,) = tied([grad_key], token)

    def input_rows(select):
        return sum(
            jnp.einsum(
                "rc,dc->rd",
                select(grad),
                weight_full[:, n * width : (n + 1) * width],
                preferred_element_type=f32,
            )
            for n, grad in ((1, grad_key), (2, grad_value))
        )

    grad_outer = input_rows(lambda g: jnp.where(is_first, g[:side], g[side + rows :]))
    grad_outer = grad_outer.astype(bf16)
    back = along(grad_outer, -1, 1)
    grad_rest = input_rows(
        lambda g: jnp.where(
            is_first, g[side + rows :], jnp.concatenate([g[thin:side], g[:thin]], axis=0)
        )
    )
    back_edge = along(grad_rest[rows:].astype(bf16), 1, -1)
    if slotted:
        token = step(group, [grad_outer, grad_rest])
        token = step(halves, token)
        (back,) = tied([back], token)
    back_own = jnp.where(is_first, back[:thin], back[rows:]).astype(f32)
    back_partner = jnp.where(is_first, back[thin:], back[:rows])
    grad_near = (grad_rest[:rows] + back_partner.astype(f32)).astype(bf16)
    back_near = swap(grad_near, blocks_axis, count)
    if slotted:
        (grad_key, grad_query) = tied([grad_key, grad_query], [grad_near])
    middle = (
        input_rows(lambda g: g[side : side + rows])
        + jnp.einsum("rc,dc->rd", grad_query, weight_full[:, :width], preferred_element_type=f32)
        + grad_residual
    )
    if slotted:
        token = step(group, [middle])
        token = step(halves, token)
        (back_near,) = tied([back_near], token)
    pad_low = lambda v: jnp.pad(v, ((0, rows - thin), (0, 0)))
    pad_high = lambda v: jnp.pad(v, ((rows - thin, 0), (0, 0)))
    back_edge = back_edge.astype(f32)
    grad_input = (
        middle
        + back_near.astype(f32)
        + jnp.where(
            is_first, pad_high(back_own) + pad_low(back_edge), pad_low(back_own) + pad_high(back_edge)
        )
    )
    grad_hidden = jnp.take(grad_input, slot_index, axis=0)

    if slotted:
        step(halves, [grad_hidden])
        out_rest, out_lead = group[0].total, halves[0].total
    else:
        by_device = lambda grad: grad.reshape((count, grad.size // grad.shape[-1] // count, -1))
        grad_down = stacked(gradients[0][0][:, first_rest:], (1, width, extra), (count, extra, shard))
        grad_rest_all = jnp.concatenate([gradients[0][0][:, :first_rest], grad_down], axis=1)
        out_rest = reduced(by_device(grad_rest_all), order, count, me)
        layer_output = jnp.take(result, slot_index, axis=0)
        out_lead = reduced(by_device(slots[0]), order, count, me)
    out_triple = out_lead[:, : 3 * width]
    out_downward = out_rest[:, first_rest:].reshape(shard, extra, width)
    out_downward = out_downward.transpose(1, 0, 2).reshape(extra * shard, width)
    summed = out_lead[:, 3 * width :].T
    (
        out_query,
        out_value,
        out_output,
        out_down_bias,
        out_gain_one,
        out_shift_one,
        out_gain_two,
        out_shift_two,
    ) = [summed[i] for i in range(8)]
    out_up_bias = summed[8 : 8 + extra].reshape(-1)
    return (
        layer_output,
        grad_hidden,
        out_triple,
        out_rest[:, :width],
        out_rest[:, width:first_rest],
        out_downward,
        out_query,
        out_value,
        out_output,
        out_up_bias,
        out_down_bias,
        out_gain_one,
        out_shift_one,
        out_gain_two,
        out_shift_two,
    )


def solution(mesh):
    matrix, vector = P(AXES, None), P(AXES)
    return jax.shard_map(
        local,
        mesh=mesh,
        in_specs=(matrix, vector, P(), *[matrix] * 4, *[vector] * 9, matrix),
        out_specs=(*[matrix] * 6, *[vector] * 9),
        check_vma=False,
    )
```

```python
import functools

import jax
import jax.numpy as jnp
import numpy as np
from jax import lax
from jax.experimental import pallas as pl
from jax.experimental.pallas import tpu as pltpu
from jax.sharding import PartitionSpec as P

DH = 64
SEG_TOK = 502
MEMR = 10
SEG_ROWS = SEG_TOK + 2 * MEMR
AXES = ("head", "blk")
TILE = 128
PAIR = 2 * DH
AT_ONCE = 6
WIDE = AT_ONCE * PAIR
WINDOW = 544

norm_eps = 1e-12
masked_score = -1e30
score_scale = 0.125
root_half = 0.7071067811865476
inverse_root_two_pi = 0.3989422804014327
f32 = jnp.float32
bf16 = jnp.bfloat16


def swap(block, bit, count):
    return lax.ppermute(block, AXES, [(i, i ^ bit) for i in range(count)])


def tied(values, others):
    values = tuple(values)
    return list(lax.optimization_barrier((*values, *others))[: len(values)])


def after(value, *others):
    return tied([value], others)[0]


def relative(bits):
    return [sum(bit for at, bit in enumerate(bits) if j >> at & 1) for j in range(1 << len(bits))]


def gathered(shard, order, count, me):
    held, have = shard, []
    for bit in order:
        axis = sum(b > bit for b in have)
        have.append(bit)
        other = jnp.expand_dims(swap(held, bit, count), axis)
        own = jnp.expand_dims(held, axis)
        held = jnp.where(
            (me & bit) == 0,
            jnp.concatenate([own, other], axis=axis),
            jnp.concatenate([other, own], axis=axis),
        )
    return held.reshape((count * shard.shape[0],) + shard.shape[1:])


def reduced(blocks, order, count, me):
    have = sorted(order, reverse=True)
    held = blocks.reshape((2,) * len(have) + blocks.shape[1:])
    for step, bit in enumerate(order):
        axis = have.index(bit)
        have.remove(bit)
        mine = ((me & bit) != 0).astype(jnp.int32)
        keep = lax.dynamic_index_in_dim(held, mine, axis, keepdims=False)
        send = lax.dynamic_index_in_dim(held, 1 - mine, axis, keepdims=False)
        total = keep.astype(f32) + swap(send, bit, count).astype(f32)
        held = total if not have else total.astype(blocks.dtype)
    return held


class Spread:
    def __init__(self, held, rounds, count):
        self.held, self.rounds, self.count = held, list(rounds), count
        self.parts = None

    def start(self):
        self.recvs = [swap(self.held, c, self.count) for c in relative(self.rounds[0])[1:]]

    def finish(self, token=()):
        recvs = tied(self.recvs, token) if token else self.recvs
        self.held = jnp.concatenate([self.held, *recvs], axis=0)
        self.rounds.pop(0)
        return self.held

    def start_two(self):
        self.start()
        (self.last,) = self.rounds[1]
        self.own = swap(self.held, self.last, self.count)

    def finish_two(self, token=()):
        recvs = tied(self.recvs, token) if token else self.recvs
        self.parts = [self.held, *recvs, self.own, *[swap(r, self.last, self.count) for r in recvs]]
        return recvs


def piece_places(rounds, apart=2):
    pieces = [relative([b for r in rounds[: len(rounds) - apart] for b in r])]
    for bits in rounds[len(rounds) - apart :]:
        pieces = [[j + c for j in piece] for c in relative(bits) for piece in pieces]
    return pieces


class Gathering:
    def __init__(self, keep, send, cut, rounds, count):
        self.rounds, self.count, self.cut, self.at = rounds, count, cut, 0
        self.keep = keep
        self.recvs = [swap(send, self.rounds[0][0][0], count)]
        self.total = None

    def arrive(self, token=()):
        self.recvs = tied(self.recvs, token) if token else self.recvs
        return self.recvs

    def advance(self, token=()):
        recvs = self.arrive(token)
        add = lambda terms, at: sum(t[at].astype(f32) for t in terms)
        joined = lambda at: jnp.concatenate([add(terms, at) for terms in self.terms], axis=-1)
        self.at += 1
        if self.at == 1:
            terms = [self.keep, *recvs]
            self.terms = [[t[..., : self.cut] for t in terms], [t[..., self.cut :] for t in terms]]
        elif self.at in (2, 3):
            for terms, recv in zip(self.terms, recvs):
                terms.append(recv)
        else:
            self.total = joined(0) + sum(r[0].astype(f32) for r in recvs)
            return [self.total]
        if self.at < 3:
            half = self.terms[0][0].shape[0] // 2
            sends = [add(terms, slice(half, None)).astype(bf16) for terms in self.terms]
            bits = [rounds[self.at][0] for rounds in self.rounds]
            self.recvs = [swap(s, b, self.count) for s, b in zip(sends, bits)]
        else:
            combos = relative(self.rounds[0][3][::-1])
            half = 1
            sends = [joined(slice(j, j + 1)).astype(bf16) for j in range(1, len(combos))]
            self.recvs = [swap(s, c, self.count) for s, c in zip(sends, combos[1:])]
            half = 1
        self.terms = [[t[:half] for t in terms] for terms in self.terms]
        return sends


class Direct:
    def __init__(self, keep, send, rounds, count):
        self.rounds, self.count, self.terms, self.total = list(rounds[1:]), count, [keep], None
        self.recvs = [swap(send, rounds[0][0], count)]

    def advance(self, token=()):
        self.terms += tied(self.recvs, token) if token else self.recvs
        add = lambda at: sum(t[at].astype(f32) for t in self.terms)
        if not self.rounds:
            self.total = add(0)
            return [self.total]
        combos = relative(self.rounds.pop(0)[::-1])
        each = self.terms[0].shape[0] // len(combos)
        sends = [add(slice(j * each, (j + 1) * each)).astype(bf16) for j in range(1, len(combos))]
        self.terms = [t[:each] for t in self.terms]
        self.recvs = [swap(x, c, self.count) for x, c in zip(sends, combos[1:])]
        return sends


def segment_at(lengths_ref, sequences, position):
    start = jnp.int32(0)
    low = jnp.int32(0)
    high = jnp.int32(0)
    for i in range(sequences):
        tokens = lengths_ref[i]
        end = start + tokens + 2 * MEMR * lax.div(tokens + (SEG_TOK - 1), jnp.int32(SEG_TOK))
        inside = (position >= start) & (position < end)
        first = start + lax.div(position - start, jnp.int32(SEG_ROWS)) * SEG_ROWS
        low = jnp.where(inside, first, low)
        high = jnp.where(inside, jnp.minimum(first + SEG_ROWS, end), high)
        start = end
    return low, high


def over_segments(lengths_ref, sequences, first_row, rows, side, body):
    def step(position):
        low, high = segment_at(lengths_ref, sequences, position)
        high = jnp.maximum(high, position + 1)
        low_at = low - first_row + side
        high_at = high - first_row + side
        window = jnp.minimum(lax.div(low_at, jnp.int32(16)) * 16, rows + 2 * side - WINDOW)
        window = pl.multiple_of(jnp.maximum(window, 0), 16)
        tile_from = lax.div(jnp.maximum(low - first_row, 0), jnp.int32(TILE))
        tile_to = lax.div(jnp.minimum(high - first_row, rows) + TILE - 1, jnp.int32(TILE))
        body(low_at, high_at, window, tile_from, tile_to)
        return high

    lax.while_loop(lambda position: position < first_row + rows, step, first_row)


def two_heads(block):
    lane = lax.broadcasted_iota(jnp.int32, block.shape, 1)
    zero = jnp.zeros_like(block)
    return jnp.concatenate(
        [jnp.where(lane < DH, block, zero), jnp.where(lane < DH, zero, block)], axis=0
    )


def own_blocks(product):
    return jnp.concatenate([product[:DH, :TILE], product[DH:, TILE:]], axis=0).T


def key_bias(low_at, high_at, window):
    row = lax.broadcasted_iota(jnp.int32, (WINDOW, 2 * TILE), 0) + window
    return jnp.where((row >= low_at) & (row < high_at), 0.0, masked_score)


def rows_inside(tile, low_at, high_at, side, shape, dim):
    at = lax.broadcasted_iota(jnp.int32, shape, dim)
    if dim == 1:
        at = at & (TILE - 1)
    at = at + (tile * TILE + side)
    return (at >= low_at) & (at < high_at)


NT = (((1,), (1,)), ((), ()))
NN = (((1,), (0,)), ((), ()))


def mul(left, right, dims=NN):
    return lax.dot_general(left, right, dims, preferred_element_type=f32)


def slots_to_rows(slots, shard, store):
    total, _, columns = slots.shape
    step = min(total, 8)
    for d in range(0, total, step):
        block = slots[d : d + step].astype(f32).reshape(step * shard, columns)
        store(slice(d * shard, (d + step) * shard), block.astype(bf16))


def forward_kernel(plan, lengths_ref, first_ref, me_ref, *refs):
    sequences, side, taken, dests, shard = plan
    outer_ref, states_ref, partner_ref, edge_ref = refs[:4]
    pieces, refs = refs[4 : 4 + taken], refs[4 + taken :]
    (q_ref, k_ref, v_ref, o_ref, stat_ref, weight_ref, reach_ref, vec_ref) = refs[:8]
    bias_ref, vt_ref, slots_ref, small_ref, in_sem = refs[8:]
    rows, width = states_ref.shape
    thin = edge_ref.shape[0]
    pair = pl.program_id(0)
    me, head = me_ref[0], me_ref[1]

    @pl.when(pair == 0)
    def _():
        slots = len(dests[0])
        copies = [
            pltpu.make_async_copy(
                pieces[a].at[j], slots_ref.at[dests[a][j] ^ me], in_sem.at[a * slots + j]
            )
            for a in range(taken)
            for j in range(slots)
        ]
        for copy in copies:
            copy.start()

        @pl.when(head == 0)
        def _():
            reach_ref[:side, :] = outer_ref[...]
            reach_ref[side + rows : side + 2 * rows, :] = partner_ref[...]
            reach_ref[side + 2 * rows :, :] = edge_ref[...]

        @pl.when(head != 0)
        def _():
            reach_ref[:thin, :] = edge_ref[...]
            reach_ref[thin:side, :] = partner_ref[...]
            reach_ref[side + rows :, :] = outer_ref[...]

        reach_ref[side : side + rows, :] = states_ref[...]
        for copy in copies:
            copy.wait()

        def store(at, block):
            weight_ref[at, :] = block[:, : 3 * width]
            small_ref[at, :] = block[:, 3 * width :]

        slots_to_rows(slots_ref, shard, store)
        vec_ref[...] = small_ref[...].astype(f32).T[: vec_ref.shape[0]]

    stat_ref[...] = jnp.zeros_like(stat_ref)
    o_ref[...] = jnp.zeros_like(o_ref)
    lanes = [pl.ds(pl.multiple_of(pair * WIDE + n * width, PAIR), WIDE) for n in range(3)]
    queries = mul(states_ref[...], weight_ref[:, lanes[0]]) + vec_ref[0:1, lanes[0]]
    q_ref[...] = queries.astype(bf16) * jnp.asarray(score_scale, bf16)
    k_ref[...] = mul(reach_ref[...], weight_ref[:, lanes[1]]).astype(bf16)
    values = mul(reach_ref[...], weight_ref[:, lanes[2]]) + vec_ref[1:2, lanes[0]]
    v_ref[...] = values.astype(bf16)
    subs = [(n, slice(n * PAIR, (n + 1) * PAIR)) for n in range(AT_ONCE)]

    def segment(low_at, high_at, window, tile_from, tile_to):
        bias_ref[...] = key_bias(low_at, high_at, window)
        keys_at = pl.ds(window, WINDOW)
        for n, part in subs:
            vt_ref[n] = v_ref[keys_at, part].T

        def one(tile, carry):
            at = pl.ds(pl.multiple_of(tile * TILE, TILE), TILE)
            wide = pl.ds(pl.multiple_of(tile * 2 * TILE, 2 * TILE), 2 * TILE)
            inside = rows_inside(tile, low_at, high_at, side, (TILE, PAIR), 0)
            there = rows_inside(tile, low_at, high_at, side, (1, 2 * TILE), 1)
            scores = [
                mul(k_ref[keys_at, part], two_heads(q_ref[at, part]), NT) + bias_ref[...]
                for _, part in subs
            ]
            for (n, part), score in zip(subs, scores):
                top = jnp.max(score, axis=0, keepdims=True)
                raised = jnp.exp(score - top)
                total = jnp.sum(raised, axis=0, keepdims=True)
                mixed = mul(vt_ref[n], raised.astype(bf16)) * (1.0 / total)
                mixed = own_blocks(mixed).astype(bf16)
                o_ref[at, part] = jnp.where(inside, mixed, o_ref[at, part])
                level = top + jnp.log(total)
                stat_ref[n, 0:1, wide] = jnp.where(there, level, stat_ref[n, 0:1, wide])
            return carry

        lax.fori_loop(tile_from, tile_to, one, 0)

    over_segments(lengths_ref, sequences, first_ref[0], rows, side, segment)


def backward_kernel(
    plan,
    lengths_ref,
    first_ref,
    me_ref,
    q_ref,
    k_ref,
    v_ref,
    g_ref,
    stat_ref,
    reach_ref,
    *refs,
):
    sequences, side, held, slot_of, shard = plan
    sums_in, dq_ref, dk_ref, dv_ref = refs[:4]
    outs = refs[4 : 4 + held]
    (bias_ref, kt_ref, dq_acc, dk_acc, dv_acc, reach_t, slots_ref, small_ref, sem) = refs[4 + held :]
    rows = q_ref.shape[0]
    pair, pairs = pl.program_id(0), pl.num_programs(0)
    me = me_ref[0]
    total, width = slots_ref.shape[0], reach_ref.shape[1]

    @pl.when(pair == 0)
    def _():
        reach_t[...] = reach_ref[...].T
        small_ref[...] = jnp.zeros_like(small_ref)

    dq_acc[...] = jnp.zeros_like(dq_acc)
    dk_acc[...] = jnp.zeros_like(dk_acc)
    dv_acc[...] = jnp.zeros_like(dv_acc)

    subs = [(n, slice(n * PAIR, (n + 1) * PAIR)) for n in range(AT_ONCE)]

    def segment(low_at, high_at, window, tile_from, tile_to):
        bias_ref[...] = key_bias(low_at, high_at, window)
        keys_at = pl.ds(window, WINDOW)
        for n, part in subs:
            kt_ref[n] = k_ref[keys_at, part].T

        def one(tile, carry):
            at = pl.ds(pl.multiple_of(tile * TILE, TILE), TILE)
            wide = pl.ds(pl.multiple_of(tile * 2 * TILE, 2 * TILE), 2 * TILE)
            there = rows_inside(tile, low_at, high_at, side, (1, 2 * TILE), 1)
            queries = [two_heads(q_ref[at, part]) for _, part in subs]
            grads = [two_heads(g_ref[at, part]) for _, part in subs]
            scores = [
                mul(k_ref[keys_at, part], query, NT) + bias_ref[...]
                for (_, part), query in zip(subs, queries)
            ]
            grad_probs = [mul(v_ref[keys_at, part], g, NT) for (_, part), g in zip(subs, grads)]
            for n, part in subs:
                level = jnp.where(there, stat_ref[n, 0:1, wide], -masked_score)
                probs = jnp.exp(scores[n] - level)
                shared = jnp.sum(probs * grad_probs[n], axis=0, keepdims=True)
                grad_scores = (probs * (grad_probs[n] - shared)).astype(bf16)
                dv_acc[keys_at, part] += mul(probs.astype(bf16), grads[n])
                dk_acc[keys_at, part] += mul(grad_scores, queries[n])
                dq_acc[at, part] += own_blocks(mul(kt_ref[n], grad_scores))
            return carry

        lax.fori_loop(tile_from, tile_to, one, 0)

    over_segments(lengths_ref, sequences, first_ref[0], rows, side, segment)
    dq = (dq_acc[...] * score_scale).astype(bf16)
    dk, dv = dk_acc[...].astype(bf16), dv_acc[...].astype(bf16)
    dq_ref[...] = dq
    dk_ref[...] = dk
    dv_ref[...] = dv
    lanes = [pl.ds(pl.multiple_of(pair * WIDE + n * width, PAIR), WIDE) for n in range(3)]
    small_ref[0:1, lanes[0]] = jnp.sum(dq.astype(f32), axis=0, keepdims=True)
    small_ref[1:2, lanes[0]] = jnp.sum(dv.astype(f32), axis=0, keepdims=True)

    def put(value, columns):
        for i in range(total):
            slot = slot_of(i ^ me) if total > 1 else 0
            slots_ref[slot, :, columns] = value[i * shard : (i + 1) * shard].astype(bf16)

    own_t = reach_ref[side : side + rows, :]
    put(mul(own_t, dq, (((0,), (0,)), ((), ()))), lanes[0])
    put(mul(reach_t[...], dk), lanes[1])
    put(mul(reach_t[...], dv), lanes[2])
    each = total // held
    copies = [
        pltpu.make_async_copy(slots_ref.at[pl.ds(a * each, each)], outs[a], sem.at[a])
        for a in range(held)
    ]

    @pl.when(pair == pairs - 1)
    def _():
        count = sums_in.shape[0]
        small_ref[2 : 2 + count, :] = sums_in[...]
        put(small_ref[...].T, pl.ds(3 * width, TILE))
        for copy in copies:
            copy.start()
        for copy in copies:
            copy.wait()


def pack_kernel(shard, weight_ref, *refs):
    *rest_refs, lead_ref, rest_ref, rows_ref = refs
    (output_ref, upward_ref, downward_ref), vector_refs = rest_refs[:3], rest_refs[3:]
    rows_ref[...] = jnp.zeros_like(rows_ref)
    row = 0
    for ref in vector_refs:
        values = ref[...].astype(f32).reshape(1, ref.shape[0])
        for at in range(0, ref.shape[0], shard):
            rows_ref[row : row + 1, :shard] = values[:, at : at + shard]
            row += 1
    width = output_ref.shape[1]
    lead_ref[:, : 3 * width] = weight_ref[...]
    lead_ref[:, 3 * width :] = rows_ref[...].T[:shard].astype(bf16)
    hidden = upward_ref.shape[1]
    rest_ref[:, :width] = output_ref[...]
    rest_ref[:, width : width + hidden] = upward_ref[...]
    down = downward_ref[...].astype(f32)
    for k in range(down.shape[0] // shard):
        at = width + hidden + k * width
        rest_ref[:, at : at + width] = down[k * shard : (k + 1) * shard].astype(bf16)


def pack(weight, output, upward, downward, vectors):
    shard = weight.shape[0]
    shape = jax.ShapeDtypeStruct
    return pl.pallas_call(
        functools.partial(pack_kernel, shard),
        name="pack",
        out_shape=(
            shape((shard, weight.shape[1] + 128), bf16),
            shape((shard, output.shape[1] + 2 * upward.shape[1]), bf16),
        ),
        in_specs=[pl.BlockSpec(memory_space=pltpu.VMEM)] * (4 + len(vectors)),
        out_specs=[pl.BlockSpec(memory_space=pltpu.VMEM)] * 2,
        scratch_shapes=[pltpu.VMEM((128, 128), f32)],
    )(weight, output, upward, downward, *vectors)


def attention_forward(lengths, first, me_head, rows_of, pieces, side, dests):
    outer, states, partner, edge = rows_of
    rows, features = states.shape
    wide = rows + 2 * side
    taken, (slots, shard, columns) = len(pieces), pieces[0].shape
    pairs = features // PAIR
    whole = lambda *shape: pl.BlockSpec(shape, lambda h, *_: (0,) * len(shape))
    column = lambda n: pl.BlockSpec((n, WIDE), lambda h, *_: (0, h))
    anywhere = pl.BlockSpec(memory_space=pl.ANY)
    shape = jax.ShapeDtypeStruct
    plan = (lengths.shape[0], side, taken, dests, shard)
    return pl.pallas_call(
        functools.partial(forward_kernel, plan),
        name="attention_forward",
        out_shape=(
            shape((rows, features), bf16),
            shape((wide, features), bf16),
            shape((wide, features), bf16),
            shape((rows, features), bf16),
            shape((pairs, 8, 2 * rows), f32),
            shape((features, 3 * features), bf16),
            shape((wide, features), bf16),
            shape((16, features), f32),
        ),
        grid_spec=pltpu.PrefetchScalarGridSpec(
            num_scalar_prefetch=3,
            grid=(pairs // AT_ONCE,),
            in_specs=[*[whole(*r.shape) for r in rows_of], *[anywhere] * taken],
            out_specs=[
                column(rows),
                column(wide),
                column(wide),
                column(rows),
                pl.BlockSpec((AT_ONCE, 8, 2 * rows), lambda h, *_: (h, 0, 0)),
                whole(features, 3 * features),
                whole(wide, features),
                whole(16, features),
            ],
            scratch_shapes=[
                pltpu.VMEM((WINDOW, 2 * TILE), f32),
                pltpu.VMEM((AT_ONCE, PAIR, WINDOW), bf16),
                pltpu.VMEM((taken * slots, shard, columns), bf16),
                pltpu.VMEM((features, columns - 3 * features), bf16),
                pltpu.SemaphoreType.DMA((taken * slots,)),
            ],
        ),
        compiler_params=pltpu.CompilerParams(vmem_limit_bytes=48 * 2**20),
    )(lengths, first, me_head, *rows_of, *pieces)


def attention_backward(
    lengths, first, me, queries, keys, values, grads, stats, reach, side, shard, held, bits, sums
):
    rows, features = queries.shape
    wide = keys.shape[0]
    pairs = features // PAIR
    total = features // shard if held > 1 else 1
    per = shard if held > 1 else features
    columns = 3 * features + TILE
    column = lambda n: pl.BlockSpec((n, WIDE), lambda h, *_: (0, h))
    whole = lambda *shape: pl.BlockSpec(shape, lambda h, *_: (0,) * len(shape))
    anywhere = pl.BlockSpec(memory_space=pl.ANY)
    shape = jax.ShapeDtypeStruct
    place = exchange_slot(bits)
    return pl.pallas_call(
        functools.partial(backward_kernel, (lengths.shape[0], side, held, place, per)),
        name="attention_backward",
        out_shape=(
            shape((rows, features), bf16),
            shape((wide, features), bf16),
            shape((wide, features), bf16),
            *[shape((total // held, per, columns), bf16)] * held,
        ),
        grid_spec=pltpu.PrefetchScalarGridSpec(
            num_scalar_prefetch=3,
            grid=(pairs // AT_ONCE,),
            in_specs=[
                column(rows),
                column(wide),
                column(wide),
                column(rows),
                pl.BlockSpec((AT_ONCE, 8, 2 * rows), lambda h, *_: (h, 0, 0)),
                whole(wide, features),
                whole(*sums.shape),
            ],
            out_specs=[column(rows), column(wide), column(wide), *[anywhere] * held],
            scratch_shapes=[
                pltpu.VMEM((WINDOW, 2 * TILE), f32),
                pltpu.VMEM((AT_ONCE, PAIR, WINDOW), bf16),
                pltpu.VMEM((rows, WIDE), f32),
                pltpu.VMEM((wide, WIDE), f32),
                pltpu.VMEM((wide, WIDE), f32),
                pltpu.VMEM((features, wide), bf16),
                pltpu.VMEM((total, per, columns), bf16),
                pltpu.VMEM((TILE, features), f32),
                pltpu.SemaphoreType.DMA((held,)),
            ],
        ),
        compiler_params=pltpu.CompilerParams(vmem_limit_bytes=56 * 2**20),
    )(lengths, first, me, queries, keys, values, grads, stats, reach, sums)


TN = (((0,), (0,)), ((), ()))


def row_mean(value):
    return jnp.mean(value, axis=-1, keepdims=True)


def column_sum(value):
    return jnp.sum(value, axis=0, keepdims=True)


def normalize(summed):
    centered = summed - row_mean(summed)
    inverse_std = lax.rsqrt(row_mean(centered * centered) + norm_eps)
    return centered * inverse_std, inverse_std


def normalize_back(grad, normed, inverse_std):
    return inverse_std * (grad - row_mean(grad) - normed * row_mean(grad * normed))


def feed_kernel(plan, *refs):
    taken, held, in_dest, out_slot, shard, border = plan
    me_ref, att_ref, states_ref, cot_ref, vec_ref, upb_ref = refs[:6]
    mixed_in, down_in = refs[6 : 6 + taken], refs[6 + taken : 6 + 2 * taken]
    at = 6 + 2 * taken
    result_ref, res_ref, gatt_ref, small_ref = refs[at : at + 4]
    outs, refs = refs[at + 4 : at + 4 + held], refs[at + 4 + held :]
    (wslot, wmix, wdown, act, slope, gall, acc, in_sem, out_sem) = refs
    me = me_ref[0]
    width = states_ref.shape[1]
    hidden = wdown.shape[0]
    slots = len(in_dest[0][0])

    def copies_of(which, pieces, lanes):
        return [
            pltpu.make_async_copy(
                pieces[a].at[j],
                wslot.at[in_dest[which][a][j] ^ me, :, lanes],
                in_sem.at[which, a * slots + j],
            )
            for a in range(taken)
            for j in range(slots)
        ]

    first_lanes = pl.ds(0, border)
    last_lanes = pl.ds(border, wslot.shape[2] - border)
    copies_in = lambda: copies_of(0, mixed_in, first_lanes)
    copies_down = lambda: copies_of(1, down_in, last_lanes)
    for copy in copies_in():
        copy.start()
    for copy in copies_down():
        copy.start()
    for copy in copies_in():
        copy.wait()
    for copy in copies_down():
        copy.wait()
    total = taken * slots
    mixed_width = wmix.shape[1]

    def store(at, block):
        wmix[at, :] = block

    slots_to_rows(wslot.at[:, :, pl.ds(0, mixed_width)], shard, store)

    bias_out, bias_down, gain_one, shift_one, gain_two, shift_two = (
        vec_ref[i : i + 1, :] for i in range(2, 8)
    )
    branch = mul(att_ref[...], wmix[:, :width]) + bias_out
    normed_one, scale_one = normalize(states_ref[...].astype(f32) + branch)
    first_norm = normed_one * gain_one + shift_one
    inner = first_norm.astype(bf16)
    extra = hidden // width
    deep = extra * shard
    for d in range(total):
        block = wslot[d, :, mixed_width:].astype(f32)
        block = [block[:, k * width : (k + 1) * width] for k in range(extra)]
        wdown[d * deep : (d + 1) * deep, :] = jnp.concatenate(block, axis=0).astype(bf16)
    chunks = range(0, hidden, width)
    for c in chunks:
        lifted = mul(inner, wmix[:, width + c : 2 * width + c]) + upb_ref[:, c : c + width]
        phi_sum = 0.5 * (1.0 + lax.erf(lifted * root_half))
        active = (lifted * phi_sum).astype(bf16)
        act[:, c : c + width] = active
        slope[:, c : c + width] = phi_sum + lifted * (
            inverse_root_two_pi * jnp.exp(-0.5 * lifted * lifted)
        )
        part = mul(active, wdown[c : c + width, :])
        acc[...] = part if c == 0 else acc[...] + part
    normed_two, scale_two = normalize(first_norm + (acc[...] + bias_down))
    result_ref[...] = (normed_two * gain_two + shift_two).astype(bf16)

    cot = cot_ref[...].astype(f32)
    small_ref[4:5, :] = column_sum(cot * normed_two)
    small_ref[5:6, :] = column_sum(cot)
    grad_mid = normalize_back(cot * gain_two, normed_two, scale_two)
    grad_down = grad_mid.astype(bf16)
    small_ref[1:2, :] = column_sum(grad_down.astype(f32))

    def put(value, first, per, columns):
        for i in range(value.shape[0] // per):
            places = [out_slot(order, (first + i) ^ me) for order in range(2)]
            for k in range(per // shard):
                rows = value[i * per + k * shard :][:shard].astype(bf16)
                start = columns + k * width
                stop = start + width
                middle = min(max(border, start), stop)
                if middle > start:
                    gall[places[0], :, start:middle] = rows[:, : middle - start]
                if stop > middle:
                    gall[places[1], :, middle:stop] = rows[:, middle - start :]

    copies_out = [
        pltpu.make_async_copy(
            gall.at[pl.ds(a * (total // held), total // held)], outs[a], out_sem.at[a]
        )
        for a in range(held)
    ]
    inner_t = inner.T
    for c in chunks:
        active = act[:, c : c + width]
        grad_active = mul(grad_down, wdown[c : c + width, :], NT)
        grad_lift = (grad_active * slope[:, c : c + width]).astype(bf16)
        small_ref[8 + c // width : 9 + c // width, :] = column_sum(grad_lift.astype(f32))
        grad_w = mul(active, grad_down, TN)
        if total > 1:
            put(grad_w, c // deep, deep, width + hidden)
        else:
            gall[0, :, width + hidden + c : 2 * width + hidden + c] = grad_w.astype(bf16)
        put(mul(inner_t, grad_lift), 0, shard, width + c)
        part = mul(grad_lift, wmix[:, width + c : 2 * width + c], NT)
        acc[...] = part if c == 0 else acc[...] + part
    grad_first = acc[...] + grad_mid
    small_ref[2:3, :] = column_sum(grad_first * normed_one)
    small_ref[3:4, :] = column_sum(grad_first)
    grad_residual = normalize_back(grad_first * gain_one, normed_one, scale_one)
    res_ref[...] = grad_residual
    grad_branch = grad_residual.astype(bf16)
    small_ref[0:1, :] = column_sum(grad_branch.astype(f32))
    put(mul(att_ref[...], grad_branch, TN), 0, shard, 0)
    for copy in copies_out:
        copy.start()
    gatt_ref[...] = mul(grad_branch, wmix[:, :width], NT).astype(bf16)
    small_ref[6:8, :] = jnp.zeros((2, width), f32)
    small_ref[12:, :] = jnp.zeros((small_ref.shape[0] - 12, width), f32)
    for copy in copies_out:
        copy.wait()


def exchange_slot(bits):
    def slot(diff):
        found = jnp.int32(0)
        for at, bit in enumerate(reversed(bits)):
            found = found + (((diff & bit) != 0).astype(jnp.int32) << at)
        return found

    return slot


def feed_forward(me, attended, states, cotangent, vectors, up_bias, mixed, down, dests, backs):
    rows, width = states.shape
    taken, (slots, shard, border) = len(mixed), mixed[0].shape
    columns = border + down[0].shape[2]
    held = min(taken, 2)
    total = taken * slots
    hidden = (columns - width) // 2
    slot_of = [exchange_slot(back) for back in backs]
    place = lambda order, diff: slot_of[order](diff) if held > 1 else 0
    plan = (taken, held, dests, place, shard, border)
    whole = pl.BlockSpec(memory_space=pltpu.VMEM)
    anywhere = pl.BlockSpec(memory_space=pl.ANY)
    shape = jax.ShapeDtypeStruct
    return pl.pallas_call(
        functools.partial(feed_kernel, plan),
        name="feed_forward",
        out_shape=(
            shape((rows, width), bf16),
            shape((rows, width), f32),
            shape((rows, width), bf16),
            shape((16, width), f32),
            *[shape((total // held, shard, columns), bf16)] * held,
        ),
        in_specs=[pl.BlockSpec(memory_space=pltpu.SMEM), *[whole] * 5, *[anywhere] * (2 * taken)],
        out_specs=[*[whole] * 4, *[anywhere] * held],
        scratch_shapes=[
            pltpu.VMEM((total, shard, columns), bf16),
            pltpu.VMEM((total * shard, columns - hidden), bf16),
            pltpu.VMEM((hidden, width), bf16),
            pltpu.VMEM((rows, hidden), bf16),
            pltpu.VMEM((rows, hidden), f32),
            pltpu.VMEM((total, shard, columns), bf16),
            pltpu.VMEM((rows, width), f32),
            pltpu.SemaphoreType.DMA((2, total)),
            pltpu.SemaphoreType.DMA((held,)),
        ],
        compiler_params=pltpu.CompilerParams(vmem_limit_bytes=60 * 2**20),
    )(me, attended, states, cotangent, vectors, up_bias, *mixed, *down)


def local(
    hidden_states,
    owner_rows,
    lengths,
    attention_weight,
    output_weight,
    upward_weight,
    downward_weight,
    query_bias,
    value_bias,
    output_bias,
    upward_bias,
    downward_bias,
    first_gain,
    first_shift,
    second_gain,
    second_shift,
    output_cotangent,
):
    rows, width = hidden_states.shape
    heads_axis, blocks_axis = lax.axis_size("head"), lax.axis_size("blk")
    count = heads_axis * blocks_axis
    me = lax.axis_index(AXES)
    head, blk = lax.axis_index("head"), lax.axis_index("blk")
    first = ((blk * heads_axis + head) * rows).astype(jnp.int32).reshape(1)
    bits = [1 << b for b in range((count - 1).bit_length())]
    far = tuple(b for b in bits if b not in (1, 2, blocks_axis))[::-1]
    near_y, near_x, core = (2,), (blocks_axis,), (1,)
    follow_rounds = ([far, near_y, near_x, core], [far, near_x, near_y, core])
    back_rounds = (
        [core, near_y, near_x, far[::-1]],
        [core, near_x, near_y, far[::-1]],
        [core, (*near_x, *near_y), far[::-1]],
    )
    back_bits = [[b for r in rounds for b in r] for rounds in back_rounds]
    order = bits[::-1]
    shard = attention_weight.shape[0]
    slotted = shard % 8 == 0
    half = width // 2
    def along(block, by_first, by_second):
        pairs = [
            (h * blocks_axis + b, h * blocks_axis + b + by)
            for h, by in ((0, by_first), (1, by_second))
            for b in range(blocks_axis)
            if 0 <= b + by < blocks_axis
        ]
        return lax.ppermute(block, AXES, pairs)

    slot_index = owner_rows % rows
    pick = (slot_index[None, :] == jnp.arange(rows, dtype=jnp.int32)[:, None]).astype(bf16)
    states = jnp.dot(pick, hidden_states, preferred_element_type=f32).astype(bf16)
    cotangent = jnp.dot(pick, output_cotangent, preferred_element_type=f32).astype(bf16)

    thin = -(-(SEG_ROWS - 1 - rows) // 16) * 16
    side = rows + thin
    partner = swap(states, blocks_axis, count)
    is_first = head == 0
    sent = jnp.where(
        is_first,
        jnp.concatenate([states[rows - thin :], partner], axis=0),
        jnp.concatenate([partner, states[:thin]], axis=0),
    )
    outer = along(sent, 1, -1)
    edge = along(jnp.where(is_first, states[:thin], states[rows - thin :]), -1, 1)
    rows_of = (outer, states, partner, edge)

    small = (
        query_bias,
        value_bias,
        output_bias,
        downward_bias,
        first_gain,
        first_shift,
        second_gain,
        second_shift,
        upward_bias,
    )
    extra = upward_bias.shape[0] // shard
    lead, rest = pack(attention_weight, output_weight, upward_weight, downward_weight, small)
    first_rest = width + upward_weight.shape[1]
    border = rest.shape[1] // 256 * 128 if slotted else first_rest

    def stacked(block, had, has):
        natural = block.reshape(*had, width).transpose(0, 2, 1, 3)
        if len(has) == 2:
            return natural.reshape(*has, width).transpose(1, 0, 2).reshape(has[1], -1)
        return natural.reshape(*has, width).transpose(0, 2, 1, 3).reshape(width, -1)

    me_of = me.astype(jnp.int32).reshape(1)
    me_head = jnp.stack([me, head]).astype(jnp.int32)
    if slotted:
        follow_all = Spread(rest[None], follow_rounds[0], count)
        follow_all.start()
        lead_all = Spread(lead[None], [far, core], count)
        lead_all.start()
        held = lead_all.finish()
        lead_two = Spread(held, [(*near_x, *near_y), core], count)
        lead_two.start()
        held = follow_all.finish([held, sent])
        follow = [
            Spread(block, rounds[1:], count)
            for block, rounds in zip((held[..., :border], held[..., border:]), follow_rounds)
        ]
        [chain.start() for chain in follow]
        held = lead_two.finish([chain.held for chain in follow])
        pieces = [held, swap(held, core[0], count)]
        lead_places = piece_places([far, (*near_x, *near_y), core], 1)
        token = [chain.finish([held, outer, edge]) for chain in follow]
        [chain.start_two() for chain in follow]
        pieces[0] = after(pieces[0], *token)
    else:
        full = gathered(lead, order, count, me)
        pieces = [full[None]]
        lead_places = [[0]]
    queries, keys, values, attended, stats, weight_full, reach, vectors = attention_forward(
        lengths, first, me_head, rows_of, pieces, side, lead_places
    )
    if slotted:
        [chain.finish_two([attended]) for chain in follow]
        follow_parts = [chain.parts for chain in follow]
        follow_places = [piece_places(rounds) for rounds in follow_rounds]
    else:
        full = gathered(rest, order, count, me)
        follow_parts = [
            [full[None, :, :first_rest]],
            [stacked(full[:, first_rest:], (count, shard, extra), (extra, width))[None]],
        ]
        follow_places = [[[0]], [[0]]]
    bias_upward = (
        vectors[8 : 8 + extra].reshape(extra, count, shard).transpose(1, 0, 2).reshape(1, -1)
    )

    outs = feed_forward(
        me_of,
        attended,
        states,
        cotangent,
        vectors,
        bias_upward,
        *follow_parts,
        follow_places,
        back_bits[:2],
    )
    result, grad_residual, grad_attended, small_sums = outs[:4]
    gradients = outs[4:]
    sums = jnp.concatenate(
        [
            small_sums[:6],
            small_sums[8 : 8 + extra].reshape(count, extra, shard).transpose(1, 0, 2).reshape(extra, width),
        ]
    )
    if slotted:
        group = [Gathering(*gradients, border, back_rounds[:2], count)]
        layer_output = jnp.take(result, slot_index, axis=0)
        token = [x for chain in group for x in chain.advance([layer_output])]
        grad_attended = after(grad_attended, *token)

    grad_query, grad_key, grad_value, *slots = attention_backward(
        lengths,
        first,
        me_of,
        queries,
        keys,
        values,
        grad_attended,
        stats,
        reach,
        side,
        shard,
        2 if slotted else 1,
        back_bits[2],
        sums,
    )

    step = lambda chains, token: [x for chain in chains for x in chain.advance(token)]
    if slotted:
        arrived = [x for chain in group for x in chain.arrive()]
        grad_query, grad_key, grad_value, *slots = tied(
            (grad_query, grad_key, grad_value, *slots), arrived
        )
        halves = [Direct(*slots, back_rounds[2], count)]
        token = step(group, [grad_query])
        (grad_key,) = tied([grad_key], token)

    def input_rows(select):
        return sum(
            jnp.einsum(
                "rc,dc->rd",
                select(grad),
                weight_full[:, n * width : (n + 1) * width],
                preferred_element_type=f32,
            )
            for n, grad in ((1, grad_key), (2, grad_value))
        )

    grad_outer = input_rows(lambda g: jnp.where(is_first, g[:side], g[side + rows :]))
    grad_outer = grad_outer.astype(bf16)
    back = along(grad_outer, -1, 1)
    grad_rest = input_rows(
        lambda g: jnp.where(
            is_first, g[side + rows :], jnp.concatenate([g[thin:side], g[:thin]], axis=0)
        )
    )
    back_edge = along(grad_rest[rows:].astype(bf16), 1, -1)
    if slotted:
        token = step(group, [grad_outer, grad_rest])
        token = step(halves, token)
        (back,) = tied([back], token)
    back_own = jnp.where(is_first, back[:thin], back[rows:]).astype(f32)
    back_partner = jnp.where(is_first, back[thin:], back[:rows])
    grad_near = (grad_rest[:rows] + back_partner.astype(f32)).astype(bf16)
    back_near = swap(grad_near, blocks_axis, count)
    if slotted:
        (grad_key, grad_query) = tied([grad_key, grad_query], [grad_near])
    middle = (
        input_rows(lambda g: g[side : side + rows])
        + jnp.einsum("rc,dc->rd", grad_query, weight_full[:, :width], preferred_element_type=f32)
        + grad_residual
    )
    if slotted:
        token = step(group, [middle])
        token = step(halves, token)
        (back_near,) = tied([back_near], token)
    pad_low = lambda v: jnp.pad(v, ((0, rows - thin), (0, 0)))
    pad_high = lambda v: jnp.pad(v, ((rows - thin, 0), (0, 0)))
    back_edge = back_edge.astype(f32)
    grad_input = (
        middle
        + back_near.astype(f32)
        + jnp.where(
            is_first, pad_high(back_own) + pad_low(back_edge), pad_low(back_own) + pad_high(back_edge)
        )
    )
    grad_hidden = jnp.take(grad_input, slot_index, axis=0)

    if slotted:
        step(halves, [grad_hidden])
        out_rest, out_lead = group[0].total, halves[0].total
    else:
        by_device = lambda grad: grad.reshape((count, grad.size // grad.shape[-1] // count, -1))
        grad_down = stacked(gradients[0][0][:, first_rest:], (1, width, extra), (count, extra, shard))
        grad_rest_all = jnp.concatenate([gradients[0][0][:, :first_rest], grad_down], axis=1)
        out_rest = reduced(by_device(grad_rest_all), order, count, me)
        layer_output = jnp.take(result, slot_index, axis=0)
        out_lead = reduced(by_device(slots[0]), order, count, me)
    out_triple = out_lead[:, : 3 * width]
    out_downward = out_rest[:, first_rest:].reshape(shard, extra, width)
    out_downward = out_downward.transpose(1, 0, 2).reshape(extra * shard, width)
    summed = out_lead[:, 3 * width :].T
    (
        out_query,
        out_value,
        out_output,
        out_down_bias,
        out_gain_one,
        out_shift_one,
        out_gain_two,
        out_shift_two,
    ) = [summed[i] for i in range(8)]
    out_up_bias = summed[8 : 8 + extra].reshape(-1)
    return (
        layer_output,
        grad_hidden,
        out_triple,
        out_rest[:, :width],
        out_rest[:, width:first_rest],
        out_downward,
        out_query,
        out_value,
        out_output,
        out_up_bias,
        out_down_bias,
        out_gain_one,
        out_shift_one,
        out_gain_two,
        out_shift_two,
    )


def solution(mesh):
    matrix, vector = P(AXES, None), P(AXES)
    return jax.shard_map(
        local,
        mesh=mesh,
        in_specs=(matrix, vector, P(), *[matrix] * 4, *[vector] * 9, matrix),
        out_specs=(*[matrix] * 6, *[vector] * 9),
        check_vma=False,
    )
```
